32 devices in a mesh: seq: 8 (over z, y), head: 4 (over x, core).
Axes of the slice: x: 2, y: 2, z: 4, core: 2. Of those that a mesh axis runs over, the one named last changes fastest.
Arguments:
- xs: bfloat16 [2048, 8192], P('seq', 'head'), may hold values from -6 to 6
- gate_z: bfloat16 [2048, 8192], P('seq', 'head'), may hold values from -400 to 400
- b_in: bfloat16 [2048, 1024], P('seq', 'head'), may hold values from -6 to 6
- c_in: bfloat16 [2048, 1024], P('seq', 'head'), may hold values from -6 to 6
- dt: float32 [2048, 128], P('seq', 'head'), may hold values from 0 to 0.07
- log_decay: float32 [2048, 128], P('seq', 'head'), may hold values from -0.7 to 0
- d_skip: float32 [128], P('head'), may hold values from 1 to 3
- conv_x: float32 [4, 8192], P(None, 'head'), may hold values from -3 to 3
- conv_b: float32 [4, 1024], P(None, 'head'), may hold values from -3 to 3
- conv_c: float32 [4, 1024], P(None, 'head'), may hold values from -3 to 3
- norm_gain: float32 [8192], P('head'), may hold values from 0.1 to 1.9
- doc_lengths: int32 [4], replicated, may hold values from 1 to 1024, 2048 in all
Outputs:
- mixed: bfloat16 [2048, 8192], P('seq', 'head')
The draws below stay inside these ranges and needn't reach their ends.
Inputs may be any that keep to these rules, and one draw needn't show every extreme that they name: `doc_lengths`: the longest document has exactly 1024 tokens; they add up to 2048.
All inputs are finite; a program needn't handle non-finite values.
Results may differ from the reference program's by a relative error of at most 0.0045.
Values may be sent and summed in bfloat16 or wider, within the bound.
A program may use at most 64 MiB of HBM per device.

```python
import math
import jax
import jax.numpy as jnp
import numpy as np
from jax import lax

MIXER_HEADS = 128
HEAD_DIM = 64
STATE = 128
GROUPS = 8
KW = 4
BLOCK = 128
SPAN = 4
TOKENS_PER_SHARD = 256
PACKED_TOKENS = 2048
DOCS = 4


def log_uniform(key, shape):
    return jnp.exp(jax.random.uniform(key, shape, jnp.float32, -math.log(2.0), math.log(2.0)))


def head_table(key):
    table_key = jax.random.fold_in(key, 101)
    key_pick, key_fast, key_slow = jax.random.split(table_key, 3)
    fast_share = 0.5
    fast_heads = jax.random.uniform(key_pick, (MIXER_HEADS,), jnp.float32) < fast_share
    rate_fast = jnp.exp(jax.random.uniform(key_fast, (MIXER_HEADS,), jnp.float32, math.log(1.0 / 50.0), math.log(1.0 / 30.0)))
    rate_slow = math.log(10.0) / PACKED_TOKENS * jnp.exp(jax.random.uniform(key_slow, (MIXER_HEADS,), jnp.float32, math.log(0.2), 0.0))
    rate_head = jnp.where(fast_heads, rate_fast, rate_slow)
    base_step = jnp.where(fast_heads, rate_fast, 1.0 / (2.0 * TOKENS_PER_SHARD))
    return (rate_head, base_step)


def draw_log_decay(key, part):
    rate_head, base_step = head_table(key)
    private_random_key = jax.random.fold_in(key, 202)
    noise_random_key, shard_random_key, spike_random_key, loss_random_key = jax.random.split(private_random_key, 4)
    jitter = log_uniform(noise_random_key, (PACKED_TOKENS, MIXER_HEADS))
    shard_scale = jnp.repeat(log_uniform(shard_random_key, (PACKED_TOKENS // TOKENS_PER_SHARD, MIXER_HEADS)), TOKENS_PER_SHARD, axis=0)
    decay_amount_scalar = -rate_head[None, :] * jitter * shard_scale
    spike_mask_rows = jax.random.uniform(spike_random_key, (PACKED_TOKENS, MIXER_HEADS), jnp.float32) < 1.0 / TOKENS_PER_SHARD
    spike_loss_term = jax.random.uniform(loss_random_key, (PACKED_TOKENS, MIXER_HEADS), jnp.float32, 0.22, 0.7)
    return jnp.where(spike_mask_rows, -spike_loss_term, decay_amount_scalar).astype(jnp.float32)


def draw_dt(key, part):
    rate_head, base_step = head_table(key)
    private_random_key = jax.random.fold_in(key, 303)
    jitter = log_uniform(private_random_key, (PACKED_TOKENS, MIXER_HEADS))
    return (base_step[None, :] * jitter).astype(jnp.float32)


def draw_gate_z(key, part):
    private_random_key = jax.random.fold_in(key, 404)
    key_value, key_rows = jax.random.split(private_random_key, 2)
    width = MIXER_HEADS * HEAD_DIM
    column = jnp.arange(width, dtype=jnp.float32) / (width - 1)
    row_scale = jnp.exp(jax.random.uniform(key_rows, (PACKED_TOKENS, 1), jnp.float32, 0.0, math.log(10.0)))
    values = jnp.clip(jax.random.normal(key_value, (PACKED_TOKENS, width), jnp.float32), -4.0, 4.0)
    column_scale = jnp.power(10.0, column)
    return (values * column_scale[None, :] * row_scale).astype(jnp.bfloat16)


def level_of(key, dims, cuts, low, high):
    factor_of, own = 1.0, jax.random.fold_in(key, 6)
    for axis_at, parts in cuts:
        steps = jnp.exp(jax.random.uniform(jax.random.fold_in(own, axis_at), (parts,), jnp.float32, low / len(cuts), high / len(cuts)))
        factor_of = factor_of * jnp.repeat(steps, dims[axis_at] // parts).reshape([-1 if axis == axis_at else 1 for axis in range(len(dims))])
    return factor_of


def length_profile(count, total, most, skew):
    portions = [(1 << 20) // math.isqrt(standing ** skew) + 1 for standing in range(2, count + 1)]
    rest, given = total - most - (count - 1), [1] * (count - 1)
    while rest > 0:
        movable = [i for i in range(count - 1) if given[i] < most]
        whole, budget = sum([portions[i] for i in movable]), rest
        for i in movable:
            more = min(most - given[i], max(1, budget * portions[i] // whole), rest)
            given[i] = given[i] + more
            rest = rest - more
    return np.array([most] + given)


def uneven_parts(stream_key, number_of, total, limit, skew):
    if number_of == 2:
        one = jax.random.randint(stream_key, (), max(1, total - limit), min(limit, total - 1) + 1)
        return jnp.stack([one, total - one])
    tallies = jnp.asarray(length_profile(number_of, total, limit, skew), jnp.int32)
    pairs = (number_of - 1) // 2
    giver, receiver = tallies[1:1 + 2 * pairs:2], tallies[2:2 + 2 * pairs:2]
    room = jnp.minimum(giver - 1, limit - receiver)
    passed = jax.random.randint(jax.random.fold_in(stream_key, 1), (pairs,), 0, 1 << 20) % (room + 1)
    tallies = tallies.at[1:1 + 2 * pairs:2].set(giver - passed).at[2:2 + 2 * pairs:2].set(receiver + passed)
    return tallies[jax.random.permutation(jax.random.fold_in(stream_key, 2), number_of)]


def gaussian(own_key, shape, scale, bound, pieces=(), kind=jnp.bfloat16):
    values = jax.random.normal(own_key, shape, jnp.float32) * scale
    if len(pieces) > 0:
        values = level_of(own_key, shape, pieces, -0.22, 0.18) * values
    return jnp.clip(values, min=-bound, max=bound).astype(kind)


def setup_inputs(seed: int = 0) -> dict:
    seeds = jax.random.split(jax.random.key(seed), 13)
    return {
        "xs": gaussian(seeds[0], (PACKED_TOKENS, MIXER_HEADS * HEAD_DIM), 1.0, 6.0, ((0, 8), (1, 4))),
        "gate_z": draw_gate_z(jax.random.fold_in(seeds[12], 71), 0),
        "b_in": gaussian(seeds[2], (PACKED_TOKENS, GROUPS * STATE), 1.0, 6.0, ((0, 8), (1, 4))),
        "c_in": gaussian(seeds[3], (PACKED_TOKENS, GROUPS * STATE), 1.0, 6.0, ((0, 8), (1, 4))),
        "dt": draw_dt(jax.random.fold_in(seeds[12], 71), 0),
        "log_decay": draw_log_decay(jax.random.fold_in(seeds[12], 71), 0),
        "d_skip": jnp.clip(1.0 + 2.0 * jax.random.uniform(seeds[6], (MIXER_HEADS,), jnp.float32) ** level_of(seeds[6], (MIXER_HEADS,), ((0, 4),), -0.2, 0.2), 1.0, 3.0),
        "conv_x": gaussian(seeds[7], (KW, MIXER_HEADS * HEAD_DIM), KW ** -0.5, 3.0, ((1, 4),), jnp.float32),
        "conv_b": gaussian(seeds[8], (KW, GROUPS * STATE), KW ** -0.5, 3.0, ((1, 4),), jnp.float32),
        "conv_c": gaussian(seeds[9], (KW, GROUPS * STATE), KW ** -0.5, 3.0, ((1, 4),), jnp.float32),
        "norm_gain": jnp.clip(1.0 + 0.18 * jax.random.normal(seeds[10], (MIXER_HEADS * HEAD_DIM,), jnp.float32), 0.1, 1.9),
        "doc_lengths": uneven_parts(seeds[11], DOCS, PACKED_TOKENS, SPAN * TOKENS_PER_SHARD, 2).astype(jnp.int32),
    }


norm_epsilon = 1e-05

def doc_index(position, starts):
    return lax.optimization_barrier(jnp.sum((starts[None, :] <= position[:, None]).astype(jnp.int32), axis=1)) - 1

def conv_silu(window, weight, docs_win):
    taps = weight.shape[0]
    row_count = window.shape[0] - taps + 1
    last_doc = docs_win[taps - 1:]
    summed = jnp.zeros((row_count, window.shape[1]), jnp.float32)
    for offset in range(taps):
        same_doc = (docs_win[offset:offset + row_count] == last_doc).astype(jnp.float32)
        summed = summed + weight[offset][None, :] * window[offset:offset + row_count].astype(jnp.float32) * same_doc[:, None]
    return jax.nn.silu(summed).astype(jnp.bfloat16)

def block_core(x_block, b_block, c_block, dt_block, decay_block, doc_ids, entry_doc, groups):
    length = dt_block.shape[0]
    per_group = dt_block.shape[1] // groups
    x_four = x_block.reshape(length, groups, per_group, -1).astype(jnp.float32)
    b_three = b_block.reshape(length, groups, -1).astype(jnp.float32)
    c_three = c_block.reshape(length, groups, -1).astype(jnp.float32)
    step_size = dt_block.reshape(length, groups, per_group)
    cumulate = jnp.cumsum(decay_block.reshape(length, groups, per_group), axis=0)
    scaled = (step_size[..., None] * x_four).astype(jnp.bfloat16)
    position = jnp.arange(length)
    allowed = (doc_ids[:, None] == doc_ids[None, :]) & (position[:, None] >= position[None, :])
    across = jnp.transpose(cumulate, (1, 2, 0))
    spread = across[:, :, :, None] - across[:, :, None, :]
    damping = jnp.where(allowed[None, None], jnp.exp(jnp.minimum(spread, 0.0)), 0.0)
    scores = jnp.einsum('tgn,sgn->gts', c_three, b_three)
    mixing = (scores[:, None] * damping).astype(jnp.bfloat16)
    local_part = jnp.einsum('gets,sgep->tgep', mixing.astype(jnp.float32), scaled.astype(jnp.float32))
    to_end = jnp.where((doc_ids == doc_ids[-1])[:, None, None], jnp.exp(cumulate[-1][None] - cumulate), 0.0)
    weighted = (to_end[..., None] * scaled.astype(jnp.float32)).astype(jnp.bfloat16)
    block_state = jnp.einsum('sgep,sgn->gepn', weighted.astype(jnp.float32), b_three)
    from_start = jnp.where((doc_ids == entry_doc)[:, None, None], jnp.exp(cumulate), 0.0)
    return (local_part, block_state, from_start)

def finish(local_part, from_start, c_block, state_now, x_block, z_block, d_skip, groups):
    length = x_block.shape[0]
    per_group = from_start.shape[2]
    c_three = c_block.reshape(length, groups, -1).astype(jnp.float32)
    x_four = x_block.reshape(length, groups, per_group, -1).astype(jnp.float32)
    carried = from_start[..., None] * jnp.einsum('tgn,gepn->tgep', c_three, state_now, precision=lax.Precision.HIGHEST)
    summed = local_part + carried + d_skip.reshape(groups, per_group)[None, :, :, None] * x_four
    return summed.reshape(length, -1) * jax.nn.silu(z_block.astype(jnp.float32))

def reference(xs, gate_z, b_in, c_in, dt, log_decay, d_skip, conv_x, conv_b, conv_c, norm_gain, doc_lengths):
    halo_rows = KW - 1
    starts = (jnp.cumsum(doc_lengths) - doc_lengths).astype(jnp.int32)

    def padded(values):
        return jnp.concatenate([jnp.zeros((halo_rows, values.shape[1]), values.dtype), values], 0)
    x_padded = padded(xs)
    b_padded = padded(b_in)
    c_padded = padded(c_in)

    def advance(state_now, block_index):
        first_row = (block_index * BLOCK).astype(jnp.int32)
        position = first_row - halo_rows + jnp.arange(BLOCK + halo_rows, dtype=jnp.int32)
        docs_win = doc_index(position, starts)
        x_conv = conv_silu(lax.dynamic_slice_in_dim(x_padded, first_row, BLOCK + halo_rows, 0), conv_x, docs_win)
        b_conv = conv_silu(lax.dynamic_slice_in_dim(b_padded, first_row, BLOCK + halo_rows, 0), conv_b, docs_win)
        c_conv = conv_silu(lax.dynamic_slice_in_dim(c_padded, first_row, BLOCK + halo_rows, 0), conv_c, docs_win)
        dt_block = lax.dynamic_slice_in_dim(dt, first_row, BLOCK, 0)
        decay_block = lax.dynamic_slice_in_dim(log_decay, first_row, BLOCK, 0)
        z_block = lax.dynamic_slice_in_dim(gate_z, first_row, BLOCK, 0)
        local_part, block_state, from_start = block_core(x_conv, b_conv, c_conv, dt_block, decay_block, docs_win[halo_rows:], docs_win[halo_rows - 1], GROUPS)
        gated = finish(local_part, from_start, c_conv, state_now, x_conv, z_block, d_skip, GROUPS)
        inverse_rms = lax.rsqrt(lax.optimization_barrier(jnp.sum(gated * gated, axis=1)) / (MIXER_HEADS * HEAD_DIM) + norm_epsilon)
        result = (gated * inverse_rms[:, None] * norm_gain[None, :]).astype(jnp.bfloat16)
        state_next = from_start[-1][..., None, None] * state_now + block_state
        return (state_next, result)
    state_zero = jnp.zeros((GROUPS, MIXER_HEADS // GROUPS, HEAD_DIM, STATE), jnp.float32)
    _, outputs = lax.scan(advance, state_zero, jnp.arange(PACKED_TOKENS // BLOCK, dtype=jnp.int32))
    return outputs.reshape(PACKED_TOKENS, MIXER_HEADS * HEAD_DIM)
```

```python
import functools

import jax
import jax.numpy as jnp
from jax import lax
from jax.experimental import pallas as pl
from jax.experimental.pallas import tpu as pltpu
from jax.sharding import PartitionSpec as P

HEAD_DIM = 64
STATE = 128
BLOCK = 128
LANES = 128
WIDE = 256
HALO = 16
SUBS = 4
norm_epsilon = 1e-05

MESH = pl.DeviceIdType.MESH
f32 = jnp.float32
bf16 = jnp.bfloat16


def silu(v):
    return v / (1.0 + jnp.exp(-v))


def split(v):
    high = v.astype(bf16)
    rest = v - high.astype(f32)
    middle = rest.astype(bf16)
    low = (rest - middle.astype(f32)).astype(bf16)
    parts = [high.astype(f32), middle.astype(f32), low.astype(f32)]
    width = LANES - 3 * v.shape[1]
    if width:
        parts.append(jnp.zeros((v.shape[0], width), f32))
    return jnp.concatenate(parts, axis=1).astype(bf16)


def dot(a, b):
    return jnp.dot(a, b, preferred_element_type=f32)


def kernel(
    seq_size,
    head_size,
    lengths_ref,
    xs_hbm,
    z_hbm,
    b_ref,
    c_ref,
    dt_ref,
    decay_ref,
    skip_ref,
    conv_x_ref,
    conv_b_ref,
    conv_c_ref,
    gain_ref,
    out_ref,
    xs_ref,
    z_ref,
    halo_x,
    halo_b,
    halo_c,
    own_s,
    first_s,
    enter,
    near_in,
    chain_out,
    chain_in,
    back_out,
    back_in,
    d_own,
    d_pair,
    masks,
    x_conv,
    scaled,
    c_conv,
    b_conv,
    b_turned,
    score,
    cum_turned,
    packed,
    hot,
    gated,
    square,
    square_own,
    square_in,
    halo_send,
    halo_recv,
    d_send,
    d_recv,
    near_send,
    near_recv,
    chain_send,
    chain_recv,
    back_send,
    back_recv,
    square_send,
    square_recv,
    load_sem,
):
    rows = xs_ref.shape[0]
    heads = dt_ref.shape[0]
    groups = b_ref.shape[1] // STATE
    chunks = xs_ref.shape[1] // WIDE
    per_chunk = WIDE // HEAD_DIM
    blocks = rows // BLOCK
    docs = lengths_ref.shape[0]
    n = chunks // 4
    events = 3 * n
    k = lax.axis_index("seq")
    me = lax.axis_index("head")
    r = lax.rem(k, 2)
    hop = k // 2
    partner = k + 1 - 2 * r
    keep = 2 * n + r * n
    give = 3 * n - r * n
    even = r == 0
    has_prev = k > 0
    has_next = k + 1 < seq_size
    has_chain_in = k > 1
    has_chain_out = k + 2 < seq_size

    def work_chunk(p):
        c = jnp.where(p < 3 * n, p - n, keep + p - 3 * n)
        c = jnp.where(p < 2 * n, p - n, c)
        return jnp.where(p < n, give + p, c)

    def event_chunk(e):
        c = jnp.where(e < 2 * n, keep + e - n, e - n)
        return jnp.where(e < n, e, c)

    def halo_copies():
        pairs = ((xs_hbm, halo_x), (b_ref, halo_b), (c_ref, halo_c))
        return [
            pltpu.make_async_remote_copy(
                src_ref=source.at[pl.ds(rows - HALO, HALO)],
                dst_ref=target,
                send_sem=halo_send.at[i],
                recv_sem=halo_recv.at[i],
                device_id={"seq": k + 1},
                device_id_type=MESH,
            )
            for i, (source, target) in enumerate(pairs)
        ]

    def d_copy():
        return pltpu.make_async_remote_copy(
            src_ref=d_own,
            dst_ref=d_pair,
            send_sem=d_send,
            recv_sem=d_recv,
            device_id={"seq": partner},
            device_id_type=MESH,
        )

    def lines_of(part):
        return pl.ds(part * (STATE // SUBS), STATE // SUBS)

    def near_copy(i, part):
        source = jnp.where(i < n, give + i, i)
        return pltpu.make_async_remote_copy(
            src_ref=own_s.at[source, lines_of(part)],
            dst_ref=near_in.at[i, lines_of(part)],
            send_sem=near_send.at[i, part],
            recv_sem=near_recv.at[i, part],
            device_id={"seq": partner},
            device_id_type=MESH,
        )

    def chain_copy(e, part):
        return pltpu.make_async_remote_copy(
            src_ref=chain_out.at[e, lines_of(part)],
            dst_ref=chain_in.at[e, lines_of(part)],
            send_sem=chain_send.at[e, part],
            recv_sem=chain_recv.at[e, part],
            device_id={"seq": k + 2},
            device_id_type=MESH,
        )

    def back_copy(e, part):
        return pltpu.make_async_remote_copy(
            src_ref=back_out.at[e, lines_of(part)],
            dst_ref=back_in.at[e, lines_of(part)],
            send_sem=back_send.at[e, part],
            recv_sem=back_recv.at[e, part],
            device_id={"seq": partner},
            device_id_type=MESH,
        )

    def square_copy(d):
        return pltpu.make_async_remote_copy(
            src_ref=square_own,
            dst_ref=square_in.at[d - 1],
            send_sem=square_send.at[d - 1],
            recv_sem=square_recv.at[d - 1],
            device_id={"head": lax.rem(me + d, head_size)},
            device_id_type=MESH,
        )

    load_x = pltpu.make_async_copy(xs_hbm, xs_ref, load_sem.at[0])
    load_z = pltpu.make_async_copy(z_hbm, z_ref, load_sem.at[1])
    load_x.start()

    barrier = pltpu.get_barrier_semaphore()
    for step, there in ((-1, has_prev), (1, has_next), (-2, has_chain_in), (2, has_chain_out)):

        @pl.when(there)
        def _():
            pl.semaphore_signal(
                barrier, inc=1, device_id={"seq": k + step}, device_id_type=MESH
            )

    for d in range(1, head_size):
        pl.semaphore_signal(
            barrier,
            inc=1,
            device_id={"head": lax.rem(me + d, head_size)},
            device_id_type=MESH,
        )
    expected = head_size - 1
    for there in (has_prev, has_next, has_chain_in, has_chain_out):
        expected = expected + there.astype(jnp.int32)

    @pl.when(k == 0)
    def _():
        halo_x[...] = jnp.zeros_like(halo_x)
        halo_b[...] = jnp.zeros_like(halo_b)
        halo_c[...] = jnp.zeros_like(halo_c)

    @pl.when(k < 2)
    def _():
        chain_in[...] = jnp.zeros_like(chain_in)

    near_in[2 * n] = jnp.zeros_like(near_in[2 * n])
    back_in[2 * n] = jnp.zeros_like(back_in[2 * n])
    for i in range(n):
        enter[give + i] = jnp.zeros_like(enter[give + i])

    starts = []
    running = jnp.int32(0)
    for j in range(docs):
        starts.append(running)
        running = running + lengths_ref[j]

    def start_at(position):
        found = jnp.full_like(position, -1)
        for start in starts:
            found = jnp.where(start <= position, start, found)
        return found

    base = k * rows
    column = base + lax.broadcasted_iota(jnp.int32, (rows, LANES), 0)
    own_start = start_at(column)
    for d in range(1, 4):
        masks[d - 1] = jnp.where(column - own_start >= d, 1.0, 0.0).astype(f32)
    lasts = [start_at(base + (b + 1) * BLOCK - 1) for b in range(blocks)]

    pl.semaphore_wait(barrier, expected)

    @pl.when(has_next)
    def _():
        for copy in halo_copies():
            copy.start()

    load_z.start()

    def turn(v):
        wide = jnp.concatenate([v, jnp.zeros((LANES - heads, rows), f32)], axis=0)
        return wide.T[:, :heads]

    dt_rows = turn(dt_ref[...])
    decay_rows = turn(decay_ref[...])
    t_index = lax.broadcasted_iota(jnp.int32, (BLOCK, BLOCK), 0)
    s_index = lax.broadcasted_iota(jnp.int32, (BLOCK, BLOCK), 1)
    lower = jnp.where(s_index <= t_index, 1.0, 0.0).astype(bf16)
    ends, enters, cums = [], [], []
    for b in range(blocks):
        here = slice(b * BLOCK, (b + 1) * BLOCK)
        parts = dot(lower, split(decay_rows[here, :]))
        cum = parts[:, :heads] + parts[:, heads : 2 * heads] + parts[:, 2 * heads : 3 * heads]
        begun = own_start[here, :heads]
        ends.append(jnp.where(begun == lasts[b], jnp.exp(cum[BLOCK - 1 :, :] - cum), 0.0))
        enters.append(jnp.where(begun < base + b * BLOCK, jnp.exp(cum), 0.0))
        cums.append(cum)
        wide = jnp.concatenate([cum, jnp.zeros((BLOCK, LANES - heads), f32)], axis=1)
        turned = wide.T
        for c in range(chunks):
            cum_turned[b, c, 0:per_chunk, :] = turned[c * per_chunk : (c + 1) * per_chunk, :]
    carry0 = enters[0][BLOCK - 1 :, :]
    carry1 = enters[1][BLOCK - 1 :, :]
    d_own[...] = split(jnp.broadcast_to(carry0 * carry1, (16, heads)))
    d_copy().start()
    packed[0] = split(dt_rows)
    packed[1] = split(jnp.concatenate(ends, axis=0))
    packed[2] = split(jnp.concatenate([enters[0], enters[1] * carry0], axis=0))
    packed[3] = split(jnp.concatenate([enters[0], enters[1]], axis=0))
    packed[4] = split(jnp.concatenate(cums, axis=0))
    few = split(
        jnp.concatenate(
            [jnp.broadcast_to(carry1, (8, heads)), jnp.broadcast_to(skip_ref[...], (8, heads))], 0
        )
    )
    packed[5, 0:16, :] = few

    def spread(c, width):
        row = lax.broadcasted_iota(jnp.int32, (LANES, per_chunk * width), 0)
        lane = lax.broadcasted_iota(jnp.int32, (LANES, per_chunk * width), 1)
        wanted = c * per_chunk + lane // width
        hit = (row == wanted) | (row == wanted + heads) | (row == wanted + 2 * heads)
        return jnp.where(hit, 1.0, 0.0).astype(bf16)

    def convolve(x, weight):
        x = x.astype(f32)
        total = weight[3:4, :] * x
        for d in range(1, 4):
            total = total + weight[3 - d : 4 - d, :] * (pltpu.roll(x, d, 0) * masks[d - 1])
        return silu(total).astype(bf16)

    def convolve_top(x, halo, weight):
        window = jnp.concatenate([halo.astype(f32), x.astype(f32)], axis=0)
        total = weight[3:4, :] * window[HALO:]
        for d in range(1, 4):
            shifted = window[HALO - d : 2 * HALO - d] * masks[d - 1, 0:HALO, :]
            total = total + weight[3 - d : 4 - d, :] * shifted
        return silu(total).astype(bf16)

    for g in range(groups):
        lanes = slice(g * STATE, (g + 1) * STATE)
        b_conv[g] = convolve(b_ref[:, lanes], conv_b_ref[:, lanes])
        b_turned[g, 1] = b_conv[g, BLOCK:, :].astype(f32).T.astype(bf16)

    load_x.wait()

    def lanes_of(c, half):
        return pl.ds(pl.multiple_of(c * WIDE + half * LANES, LANES), LANES)

    def conv_step(p, _):
        c = work_chunk(p)
        for half in range(WIDE // LANES):
            lanes = lanes_of(c, half)
            x_conv[c, :, half * LANES : (half + 1) * LANES] = convolve(
                xs_ref[:, lanes], conv_x_ref[:, lanes]
            )
        return 0

    lax.fori_loop(0, chunks, conv_step, 0)

    @pl.when(has_prev)
    def _():
        for copy in halo_copies():
            copy.wait_recv()

    for g in range(groups):
        lanes = slice(g * STATE, (g + 1) * STATE)
        b_conv[g, 0:HALO, :] = convolve_top(b_ref[0:HALO, lanes], halo_b[:, lanes], conv_b_ref[:, lanes])
        b_turned[g, 0] = b_conv[g, :BLOCK, :].astype(f32).T.astype(bf16)

    def state_step(p, _):
        c = work_chunk(p)
        g = c // (chunks // groups)
        for half in range(WIDE // LANES):
            lanes = lanes_of(c, half)
            x_conv[c, 0:HALO, half * LANES : (half + 1) * LANES] = convolve_top(
                xs_ref[0:HALO, lanes], halo_x[:, lanes], conv_x_ref[:, lanes]
            )
        x = x_conv[c]
        one_hot = spread(c, HEAD_DIM)
        hot[c] = one_hot
        product = (dot(packed[0], one_hot) * x.astype(f32)).astype(bf16)
        scaled[c] = product
        weighted = (dot(packed[1], one_hot) * product.astype(f32)).astype(bf16)
        state0 = dot(b_turned[g, 0], weighted[:BLOCK])
        state1 = dot(b_turned[g, 1], weighted[BLOCK:])
        few = dot(packed[5, 0:16, :], one_hot)
        first_s[c] = state0.astype(bf16)
        state = (few[0:1, :] * state0 + state1).astype(bf16)
        own_s[c] = state

        @pl.when(p < n)
        def _():
            for part in range(SUBS):
                near_copy(p, part).start()

        @pl.when((p >= 2 * n) & (p < 3 * n))
        def _():
            for part in range(SUBS):
                near_copy(p - n, part).start()

        @pl.when(p == n)
        def _():
            d_copy().wait_recv()

        @pl.when((p >= n) & (p < 2 * n) & (hop == 0) & has_chain_out)
        def _():
            decay_pair = dot(d_pair[...], one_hot)[0:1, :]
            wide = state.astype(f32)
            chain_out[p - n] = jnp.where(even, decay_pair * wide, wide).astype(bf16)
            for part in range(SUBS):
                chain_copy(p - n, part).start()

        return 0

    lax.fori_loop(0, chunks, state_step, 0)

    for g in range(groups):
        lanes = slice(g * STATE, (g + 1) * STATE)
        c_conv[g] = convolve(c_ref[:, lanes], conv_c_ref[:, lanes])
        c_conv[g, 0:HALO, :] = convolve_top(c_ref[0:HALO, lanes], halo_c[:, lanes], conv_c_ref[:, lanes])

    for b in range(blocks):
        here = slice(b * BLOCK, (b + 1) * BLOCK)
        allowed = (base + b * BLOCK + s_index >= own_start[here, :]) & (s_index <= t_index)
        for g in range(groups):
            value = lax.dot_general(
                c_conv[g, here, :],
                b_conv[g, here, :],
                (((1,), (1,)), ((), ())),
                preferred_element_type=f32,
            )
            score[g, b] = jnp.where(allowed, value, 0.0)

    square[...] = jnp.zeros_like(square)
    load_z.wait()

    def local_step(c, _):
        g = c // (chunks // groups)
        one_hot = hot[c]
        one_hot_wide = spread(c, BLOCK)
        lane = lax.broadcasted_iota(jnp.int32, (BLOCK, LANES), 1)
        locals_ = []
        for b in range(blocks):
            here = slice(b * BLOCK, (b + 1) * BLOCK)
            across = dot(packed[4, here, :], one_hot_wide)
            damped = score[g, b]
            pieces = []
            for j in range(per_chunk // 2):
                mixes = []
                for i in (2 * j, 2 * j + 1):
                    gap = across[:, i * BLOCK : (i + 1) * BLOCK] - cum_turned[b, c, i : i + 1, :]
                    mixes.append((damped * jnp.exp(jnp.minimum(gap, 0.0))).astype(bf16))
                values = scaled[c, here, j * LANES : (j + 1) * LANES]
                zero = jnp.zeros_like(values)
                left = jnp.where(lane < HEAD_DIM, values, zero)
                right = jnp.where(lane < HEAD_DIM, zero, values)
                pieces.append(
                    dot(jnp.concatenate(mixes, axis=1), jnp.concatenate([left, right], axis=0))
                )
            locals_.append(jnp.concatenate(pieces, axis=1))
        inner = dot(packed[3, BLOCK:, :], one_hot) * dot(c_conv[g, BLOCK:, :], first_s[c])
        few = dot(packed[5, 0:16, :], one_hot)
        total = jnp.concatenate([locals_[0], locals_[1] + inner], axis=0)
        gated[c] = total + few[8:9, :] * x_conv[c].astype(f32)
        return 0

    def chain_event(e):
        c = event_chunk(e)
        one_hot = hot[c]
        decay_own = dot(d_own[...], one_hot)[0:1, :]
        decay_pair = dot(d_pair[...], one_hot)[0:1, :]
        decay_first = jnp.where(even, decay_own, decay_pair)
        decay_second = jnp.where(even, decay_pair, decay_own)
        near = jnp.where(e < n, 2 * n, e - n)
        for part in range(SUBS):
            lines = lines_of(part)

            @pl.when(e >= n)
            def _():
                near_copy(e - n, part).wait_recv()

            @pl.when(has_chain_in)
            def _():
                chain_copy(e, part).wait_recv()

            own = own_s[c, lines].astype(f32)
            other = near_in[near, lines].astype(f32)
            before = chain_in[e, lines].astype(f32)
            middle = jnp.where(even, own, other) + decay_first * before
            after = jnp.where(even, other, own) + decay_second * middle

            @pl.when(has_chain_out & ((e >= n) | has_chain_in))
            def _():
                chain_out[e, lines] = after.astype(bf16)
                chain_copy(e, part).start()

            @pl.when(e < 2 * n)
            def _():
                back_out[e, lines] = jnp.where(even, middle, before).astype(bf16)

                @pl.when(has_chain_in)
                def _():
                    back_copy(e, part).start()

            enter[c, lines] = jnp.where(even, before, middle).astype(bf16)

        @pl.when((e == 2 * n - 1) & (hop == 0))
        def _():
            for other_e in range(2 * n):
                for part in range(SUBS):
                    back_copy(other_e, part).start()

    def last_step(f, _):
        t = f - 2 * n
        late = jnp.where(lax.rem(t, 2) == 0, n + t // 2, give + t // 2)
        c = jnp.where(f < n, keep + f, jnp.where(f < 2 * n, f - n, late))
        added = (f >= n) & ((f < 2 * n) | (lax.rem(f, 2) == 1))
        slot = jnp.where(f < 2 * n, f - n, n + t // 2)
        slot = jnp.where(added, slot, 2 * n)
        g = c // (chunks // groups)

        @pl.when(added)
        def _():
            for part in range(SUBS):
                back_copy(slot, part).wait_recv()

        entering = (enter[c].astype(f32) + back_in[slot].astype(f32)).astype(bf16)
        total = gated[c] + dot(packed[2], hot[c]) * dot(c_conv[g], entering)
        lanes = pl.ds(pl.multiple_of(c * WIDE, WIDE), WIDE)
        value = total * silu(z_ref[:, lanes].astype(f32))
        gated[c] = value
        power = value * value
        square[...] += power[:, :LANES] + power[:, LANES:]
        return 0

    def locals_before(e):
        count = jnp.where(hop == 0, 2 * e - 3 * n // 2, chunks)
        count = jnp.where(hop == 1, 2 * e + n, count)
        count = jnp.where(e >= events - 1, chunks, count)
        return jnp.clip(jnp.where(e < 0, 0, count), 0, chunks)

    def lasts_after(e):
        count = jnp.where(e < 2 * n - 1, 0, 2 * (e + 1) - 2 * n)
        count = jnp.where((hop == 0) | (locals_before(e) < chunks), 0, count)
        return jnp.where(e >= events - 1, chunks, count)

    def outer(e, _):
        lax.fori_loop(locals_before(e - 1), locals_before(e), local_step, 0)
        chain_event(e)
        lax.fori_loop(lasts_after(e - 1), lasts_after(e), last_step, 0)
        return 0

    lax.fori_loop(0, events, outer, 0)

    own_square = jnp.sum(square[...].T, axis=0, keepdims=True)
    square_own[...] = jnp.broadcast_to(own_square, square_own.shape)
    for d in range(1, head_size):
        square_copy(d).start()

    def drain_near(i, _):
        for part in range(SUBS):
            near_copy(i, part).wait_send()
            back_copy(i, part).wait_send()
        return 0

    def drain_chain(e, _):
        for part in range(SUBS):
            chain_copy(e, part).wait_send()
        return 0

    lax.fori_loop(0, 2 * n, drain_near, 0)

    @pl.when(has_chain_out)
    def _():
        lax.fori_loop(0, events, drain_chain, 0)

    d_copy().wait_send()

    @pl.when(has_next)
    def _():
        for copy in halo_copies():
            copy.wait_send()

    for d in range(1, head_size):
        square_copy(d).wait_recv()
    total_square = square_own[...]
    for d in range(1, head_size):
        total_square = total_square + square_in[d - 1]
    inverse = lax.rsqrt(total_square / (xs_ref.shape[1] * head_size) + norm_epsilon)
    inverse = jnp.broadcast_to(inverse[0:1, :], (LANES, rows)).T
    inverse = jnp.concatenate([inverse] * (WIDE // LANES), axis=1)
    for c in range(chunks):
        lanes = slice(c * WIDE, (c + 1) * WIDE)
        out_ref[:, lanes] = (gated[c] * inverse * gain_ref[:, lanes]).astype(bf16)
    for d in range(1, head_size):
        square_copy(d).wait_send()


def solution(mesh):
    seq_size = mesh.shape["seq"]
    head_size = mesh.shape["head"]

    def per_device(
        xs, gate_z, b_in, c_in, dt, log_decay, d_skip, conv_x, conv_b, conv_c, gain, doc_lengths
    ):
        rows, width = xs.shape
        heads = dt.shape[1]
        groups = b_in.shape[1] // STATE
        chunks = width // WIDE
        blocks = rows // BLOCK
        per_chunk = WIDE // HEAD_DIM
        vmem = pltpu.VMEM
        dma = pltpu.SemaphoreType.DMA
        n = chunks // 4

        def states(count):
            return vmem((count, STATE, WIDE), bf16)

        return pl.pallas_call(
            functools.partial(kernel, seq_size, head_size),
            out_shape=pltpu.VMEM((rows, width), bf16),
            in_specs=[pl.BlockSpec(memory_space=pltpu.SMEM)]
            + [pl.BlockSpec(memory_space=pltpu.HBM)] * 2
            + [pl.BlockSpec(memory_space=pltpu.VMEM)] * 9,
            out_specs=pl.BlockSpec(memory_space=pltpu.VMEM),
            scratch_shapes=[
                vmem((rows, width), bf16),
                vmem((rows, width), bf16),
                vmem((HALO, width), bf16),
                vmem((HALO, groups * STATE), bf16),
                vmem((HALO, groups * STATE), bf16),
                states(chunks),
                states(chunks),
                states(chunks),
                states(2 * n + 1),
                states(3 * n),
                states(3 * n),
                states(2 * n),
                states(2 * n + 1),
                vmem((16, LANES), bf16),
                vmem((16, LANES), bf16),
                vmem((3, rows, LANES), f32),
                vmem((chunks, rows, WIDE), bf16),
                vmem((chunks, rows, WIDE), bf16),
                vmem((groups, rows, STATE), bf16),
                vmem((groups, rows, STATE), bf16),
                vmem((groups, blocks, STATE, BLOCK), bf16),
                vmem((groups, blocks, BLOCK, BLOCK), f32),
                vmem((blocks, chunks, 8, BLOCK), f32),
                vmem((6, rows, LANES), bf16),
                vmem((chunks, LANES, WIDE), bf16),
                vmem((chunks, rows, WIDE), f32),
                vmem((rows, LANES), f32),
                vmem((8, rows), f32),
                vmem((head_size - 1, 8, rows), f32),
                dma((3,)),
                dma((3,)),
                dma,
                dma,
                dma((2 * n, SUBS)),
                dma((2 * n, SUBS)),
                dma((3 * n, SUBS)),
                dma((3 * n, SUBS)),
                dma((2 * n, SUBS)),
                dma((2 * n, SUBS)),
                dma((head_size - 1,)),
                dma((head_size - 1,)),
                dma((2,)),
            ],
            compiler_params=pltpu.CompilerParams(
                collective_id=0, has_side_effects=True, vmem_limit_bytes=60_000_000
            ),
        )(
            doc_lengths,
            xs,
            gate_z,
            b_in,
            c_in,
            dt.T,
            log_decay.T,
            d_skip.reshape(1, -1),
            conv_x,
            conv_b,
            conv_c,
            gain.reshape(1, -1),
        )

    whole = P("seq", "head")
    across = P(None, "head")
    return jax.shard_map(
        per_device,
        mesh=mesh,
        in_specs=(
            whole,
            whole,
            whole,
            whole,
            whole,
            whole,
            P("head"),
            across,
            across,
            across,
            P("head"),
            P(),
        ),
        out_specs=whole,
        check_vma=False,
    )
```

```python
import functools

import jax
import jax.numpy as jnp
from jax import lax
from jax.experimental import pallas as pl
from jax.experimental.pallas import tpu as pltpu
from jax.sharding import PartitionSpec as P

HEAD_DIM = 64
STATE = 128
BLOCK = 128
LANES = 128
WIDE = 256
HALO = 16
SUBS = 4
norm_epsilon = 1e-05

MESH = pl.DeviceIdType.MESH
f32 = jnp.float32
bf16 = jnp.bfloat16


def silu(v):
    return v / (1.0 + jnp.exp(-v))


def split(v):
    high = v.astype(bf16)
    rest = v - high.astype(f32)
    middle = rest.astype(bf16)
    low = (rest - middle.astype(f32)).astype(bf16)
    parts = [high.astype(f32), middle.astype(f32), low.astype(f32)]
    width = LANES - 3 * v.shape[1]
    if width:
        parts.append(jnp.zeros((v.shape[0], width), f32))
    return jnp.concatenate(parts, axis=1).astype(bf16)


def dot(a, b):
    return jnp.dot(a, b, preferred_element_type=f32)


def kernel(
    seq_size,
    head_size,
    lengths_hbm,
    xs_hbm,
    z_hbm,
    b_hbm,
    c_hbm,
    dt_hbm,
    decay_hbm,
    skip_hbm,
    conv_x_hbm,
    conv_b_hbm,
    conv_c_hbm,
    gain_hbm,
    out_ref,
    lengths_ref,
    xs_ref,
    z_ref,
    b_ref,
    c_ref,
    dt_ref,
    decay_ref,
    skip_ref,
    conv_x_ref,
    conv_b_ref,
    conv_c_ref,
    gain_ref,
    tail_x,
    halo_out,
    halo_in,
    halo_x,
    halo_b,
    halo_c,
    own_s,
    first_s,
    enter,
    near_in,
    chain_out,
    chain_in,
    back_out,
    back_in,
    d_own,
    d_pair,
    masks,
    x_conv,
    scaled,
    c_conv,
    b_conv,
    b_turned,
    score,
    cum_turned,
    packed,
    hot,
    gated,
    square,
    square_own,
    square_in,
    halo_send,
    halo_recv,
    d_send,
    d_recv,
    near_send,
    near_recv,
    chain_send,
    chain_recv,
    back_send,
    back_recv,
    square_send,
    square_recv,
    load_sem,
):
    rows = xs_ref.shape[0]
    heads = dt_ref.shape[0]
    groups = b_ref.shape[1] // STATE
    chunks = xs_ref.shape[1] // WIDE
    per_chunk = WIDE // HEAD_DIM
    blocks = rows // BLOCK
    docs = lengths_ref.shape[0]
    n = chunks // 4
    events = 3 * n
    k = lax.axis_index("seq")
    me = lax.axis_index("head")
    r = lax.rem(k, 2)
    hop = k // 2
    partner = k + 1 - 2 * r
    keep = 2 * n + r * n
    give = 3 * n - r * n
    even = r == 0
    has_prev = k > 0
    has_next = k + 1 < seq_size
    has_chain_in = k > 1
    has_chain_out = k + 2 < seq_size

    def work_chunk(p):
        c = jnp.where(p < 3 * n, p - n, keep + p - 3 * n)
        c = jnp.where(p < 2 * n, p - n, c)
        return jnp.where(p < n, give + p, c)

    def event_chunk(e):
        c = jnp.where(e < 2 * n, keep + e - n, e - n)
        return jnp.where(e < n, e, c)

    def halo_copy():
        return pltpu.make_async_remote_copy(
            src_ref=halo_out,
            dst_ref=halo_in,
            send_sem=halo_send,
            recv_sem=halo_recv,
            device_id={"seq": k + 1},
            device_id_type=MESH,
        )

    def d_copy():
        return pltpu.make_async_remote_copy(
            src_ref=d_own,
            dst_ref=d_pair,
            send_sem=d_send,
            recv_sem=d_recv,
            device_id={"seq": partner},
            device_id_type=MESH,
        )

    def lines_of(part):
        return pl.ds(part * (STATE // SUBS), STATE // SUBS)

    def near_copy(i, part):
        source = jnp.where(i < n, give + i, i)
        return pltpu.make_async_remote_copy(
            src_ref=own_s.at[source, lines_of(part)],
            dst_ref=near_in.at[i, lines_of(part)],
            send_sem=near_send.at[i, part],
            recv_sem=near_recv.at[i, part],
            device_id={"seq": partner},
            device_id_type=MESH,
        )

    def chain_copy(e, part):
        return pltpu.make_async_remote_copy(
            src_ref=chain_out.at[e, lines_of(part)],
            dst_ref=chain_in.at[e, lines_of(part)],
            send_sem=chain_send.at[e, part],
            recv_sem=chain_recv.at[e, part],
            device_id={"seq": k + 2},
            device_id_type=MESH,
        )

    def back_copy(e, part):
        return pltpu.make_async_remote_copy(
            src_ref=back_out.at[e, lines_of(part)],
            dst_ref=back_in.at[e, lines_of(part)],
            send_sem=back_send.at[e, part],
            recv_sem=back_recv.at[e, part],
            device_id={"seq": partner},
            device_id_type=MESH,
        )

    def square_copy(d):
        return pltpu.make_async_remote_copy(
            src_ref=square_own,
            dst_ref=square_in.at[d - 1],
            send_sem=square_send.at[d - 1],
            recv_sem=square_recv.at[d - 1],
            device_id={"head": lax.rem(me + d, head_size)},
            device_id_type=MESH,
        )

    barrier = pltpu.get_barrier_semaphore()
    for step, there in ((-1, has_prev), (1, has_next), (-2, has_chain_in), (2, has_chain_out)):

        @pl.when(there)
        def _():
            pl.semaphore_signal(
                barrier, inc=1, device_id={"seq": k + step}, device_id_type=MESH
            )

    for d in range(1, head_size):
        pl.semaphore_signal(
            barrier,
            inc=1,
            device_id={"head": lax.rem(me + d, head_size)},
            device_id_type=MESH,
        )
    expected = head_size - 1
    for there in (has_prev, has_next, has_chain_in, has_chain_out):
        expected = expected + there.astype(jnp.int32)

    moves = (
        (xs_hbm.at[pl.ds(rows - HALO, HALO)], tail_x),
        (lengths_hbm, lengths_ref),
        (b_hbm, b_ref),
        (c_hbm, c_ref),
        (decay_hbm, decay_ref),
        (dt_hbm, dt_ref),
        (xs_hbm, xs_ref),
        (conv_b_hbm, conv_b_ref),
        (conv_x_hbm, conv_x_ref),
        (conv_c_hbm, conv_c_ref),
        (skip_hbm, skip_ref),
        (gain_hbm, gain_ref),
        (z_hbm, z_ref),
    )
    loads = [
        pltpu.make_async_copy(source, target, load_sem.at[i])
        for i, (source, target) in enumerate(moves)
    ]
    for load in loads:
        load.start()
    (
        load_tail, load_lengths, load_b, load_c, load_decay, load_dt, load_x,
        load_conv_b, load_conv_x, load_conv_c, load_skip, load_gain, load_z,
    ) = loads

    quarter = xs_ref.shape[1] // 4
    b_width = b_ref.shape[1]
    halo_row = lax.broadcasted_iota(jnp.int32, (HALO, quarter), 0) // 3

    load_tail.wait()
    parcel = jnp.zeros((HALO, quarter), f32)
    for q in range(4):
        piece = tail_x[:, q * quarter : (q + 1) * quarter].astype(f32)
        parcel = jnp.where(halo_row == q, pltpu.roll(piece, 3 * q + 3, 0), parcel)
    load_b.wait()
    load_c.wait()
    pieces = [b_ref[rows - HALO :, :].astype(f32), c_ref[rows - HALO :, :].astype(f32)]
    if quarter > 2 * b_width:
        pieces.append(jnp.zeros((HALO, quarter - 2 * b_width), f32))
    piece = pltpu.roll(jnp.concatenate(pieces, axis=1), 15, 0)
    halo_out[...] = jnp.where(halo_row == 4, piece, parcel).astype(bf16)

    load_lengths.wait()
    starts = []
    running = jnp.int32(0)
    for j in range(docs):
        starts.append(running)
        running = running + lengths_ref[j]

    def start_at(position):
        found = jnp.full_like(position, -1)
        for start in starts:
            found = jnp.where(start <= position, start, found)
        return found

    base = k * rows
    column = base + lax.broadcasted_iota(jnp.int32, (rows, LANES), 0)
    own_start = start_at(column)
    for d in range(1, 4):
        masks[d - 1] = jnp.where(column - own_start >= d, 1.0, 0.0).astype(f32)
    lasts = [start_at(base + (b + 1) * BLOCK - 1) for b in range(blocks)]
    load_decay.wait()
    load_dt.wait()
    load_skip.wait()

    pl.semaphore_wait(barrier, expected)

    @pl.when(has_next)
    def _():
        halo_copy().start()

    def turn(v):
        wide = jnp.concatenate([v, jnp.zeros((LANES - heads, rows), f32)], axis=0)
        return wide.T[:, :heads]

    dt_rows = turn(dt_ref[...])
    decay_rows = turn(decay_ref[...])
    t_index = lax.broadcasted_iota(jnp.int32, (BLOCK, BLOCK), 0)
    s_index = lax.broadcasted_iota(jnp.int32, (BLOCK, BLOCK), 1)
    lower = jnp.where(s_index <= t_index, 1.0, 0.0).astype(bf16)
    ends, enters, cums = [], [], []
    for b in range(blocks):
        here = slice(b * BLOCK, (b + 1) * BLOCK)
        parts = dot(lower, split(decay_rows[here, :]))
        cum = parts[:, :heads] + parts[:, heads : 2 * heads] + parts[:, 2 * heads : 3 * heads]
        begun = own_start[here, :heads]
        ends.append(jnp.where(begun == lasts[b], jnp.exp(cum[BLOCK - 1 :, :] - cum), 0.0))
        enters.append(jnp.where(begun < base + b * BLOCK, jnp.exp(cum), 0.0))
        cums.append(cum)
        wide = jnp.concatenate([cum, jnp.zeros((BLOCK, LANES - heads), f32)], axis=1)
        turned = wide.T
        for c in range(chunks):
            cum_turned[b, c, 0:per_chunk, :] = turned[c * per_chunk : (c + 1) * per_chunk, :]
    carry0 = enters[0][BLOCK - 1 :, :]
    carry1 = enters[1][BLOCK - 1 :, :]
    d_own[...] = split(jnp.broadcast_to(carry0 * carry1, (16, heads)))
    d_copy().start()
    packed[0] = split(dt_rows)
    packed[1] = split(jnp.concatenate(ends, axis=0))
    packed[2] = split(jnp.concatenate([enters[0], enters[1] * carry0], axis=0))
    packed[3] = split(jnp.concatenate([enters[0], enters[1]], axis=0))
    packed[4] = split(jnp.concatenate(cums, axis=0))
    few = split(
        jnp.concatenate(
            [jnp.broadcast_to(carry1, (8, heads)), jnp.broadcast_to(skip_ref[...], (8, heads))], 0
        )
    )
    packed[5, 0:16, :] = few

    def spread(c, width):
        row = lax.broadcasted_iota(jnp.int32, (LANES, per_chunk * width), 0)
        lane = lax.broadcasted_iota(jnp.int32, (LANES, per_chunk * width), 1)
        wanted = c * per_chunk + lane // width
        hit = (row == wanted) | (row == wanted + heads) | (row == wanted + 2 * heads)
        return jnp.where(hit, 1.0, 0.0).astype(bf16)

    def convolve(x, weight):
        x = x.astype(f32)
        total = weight[3:4, :] * x
        for d in range(1, 4):
            total = total + weight[3 - d : 4 - d, :] * (pltpu.roll(x, d, 0) * masks[d - 1])
        return silu(total).astype(bf16)

    def convolve_top(x, halo, weight):
        window = jnp.concatenate([halo.astype(f32), x.astype(f32)], axis=0)
        total = weight[3:4, :] * window[HALO:]
        for d in range(1, 4):
            shifted = window[HALO - d : 2 * HALO - d] * masks[d - 1, 0:HALO, :]
            total = total + weight[3 - d : 4 - d, :] * shifted
        return silu(total).astype(bf16)

    load_conv_b.wait()
    for g in range(groups):
        lanes = slice(g * STATE, (g + 1) * STATE)
        b_conv[g] = convolve(b_ref[:, lanes], conv_b_ref[:, lanes])
        b_turned[g, 1] = b_conv[g, BLOCK:, :].astype(f32).T.astype(bf16)

    load_x.wait()
    load_conv_x.wait()

    def lanes_of(c, half):
        return pl.ds(pl.multiple_of(c * WIDE + half * LANES, LANES), LANES)

    def conv_step(p, _):
        c = work_chunk(p)
        for half in range(WIDE // LANES):
            lanes = lanes_of(c, half)
            x_conv[c, :, half * LANES : (half + 1) * LANES] = convolve(
                xs_ref[:, lanes], conv_x_ref[:, lanes]
            )
        return 0

    lax.fori_loop(0, 3 * n, conv_step, 0)

    @pl.when(k < 2)
    def _():
        chain_in[...] = jnp.zeros_like(chain_in)

    near_in[2 * n] = jnp.zeros_like(near_in[2 * n])
    back_in[2 * n] = jnp.zeros_like(back_in[2 * n])
    for i in range(n):
        enter[give + i] = jnp.zeros_like(enter[give + i])

    @pl.when(k == 0)
    def _():
        halo_in[...] = jnp.zeros_like(halo_in)

    @pl.when(has_prev)
    def _():
        halo_copy().wait_recv()

    arrived = halo_in[...].astype(f32)
    for q in range(4):
        halo_x[:, q * quarter : (q + 1) * quarter] = pltpu.roll(
            arrived, HALO - 3 - 3 * q, 0
        ).astype(bf16)
    piece = pltpu.roll(arrived, 1, 0)
    halo_b[...] = piece[:, :b_width].astype(bf16)
    halo_c[...] = piece[:, b_width : 2 * b_width].astype(bf16)

    for g in range(groups):
        lanes = slice(g * STATE, (g + 1) * STATE)
        b_conv[g, 0:HALO, :] = convolve_top(b_ref[0:HALO, lanes], halo_b[:, lanes], conv_b_ref[:, lanes])
        b_turned[g, 0] = b_conv[g, :BLOCK, :].astype(f32).T.astype(bf16)

    def state_step(p, _):
        c = work_chunk(p)
        g = c // (chunks // groups)
        for half in range(WIDE // LANES):
            lanes = lanes_of(c, half)
            x_conv[c, 0:HALO, half * LANES : (half + 1) * LANES] = convolve_top(
                xs_ref[0:HALO, lanes], halo_x[:, lanes], conv_x_ref[:, lanes]
            )
        x = x_conv[c]
        one_hot = spread(c, HEAD_DIM)
        hot[c] = one_hot
        product = (dot(packed[0], one_hot) * x.astype(f32)).astype(bf16)
        scaled[c] = product
        weighted = (dot(packed[1], one_hot) * product.astype(f32)).astype(bf16)
        state0 = dot(b_turned[g, 0], weighted[:BLOCK])
        state1 = dot(b_turned[g, 1], weighted[BLOCK:])
        few = dot(packed[5, 0:16, :], one_hot)
        first_s[c] = state0.astype(bf16)
        state = (few[0:1, :] * state0 + state1).astype(bf16)
        own_s[c] = state

        @pl.when(p < n)
        def _():
            for part in range(SUBS):
                near_copy(p, part).start()

        @pl.when((p >= 2 * n) & (p < 3 * n))
        def _():
            for part in range(SUBS):
                near_copy(p - n, part).start()

        @pl.when(p == n)
        def _():
            d_copy().wait_recv()

        @pl.when((p >= n) & (p < 2 * n) & (hop == 0) & has_chain_out)
        def _():
            decay_pair = dot(d_pair[...], one_hot)[0:1, :]
            wide = state.astype(f32)
            chain_out[p - n] = jnp.where(even, decay_pair * wide, wide).astype(bf16)
            for part in range(SUBS):
                chain_copy(p - n, part).start()

        return 0

    lax.fori_loop(0, 3 * n, state_step, 0)
    lax.fori_loop(3 * n, chunks, conv_step, 0)
    lax.fori_loop(3 * n, chunks, state_step, 0)
    load_conv_c.wait()

    for g in range(groups):
        lanes = slice(g * STATE, (g + 1) * STATE)
        c_conv[g] = convolve(c_ref[:, lanes], conv_c_ref[:, lanes])
        c_conv[g, 0:HALO, :] = convolve_top(c_ref[0:HALO, lanes], halo_c[:, lanes], conv_c_ref[:, lanes])

    for b in range(blocks):
        here = slice(b * BLOCK, (b + 1) * BLOCK)
        allowed = (base + b * BLOCK + s_index >= own_start[here, :]) & (s_index <= t_index)
        for g in range(groups):
            value = lax.dot_general(
                c_conv[g, here, :],
                b_conv[g, here, :],
                (((1,), (1,)), ((), ())),
                preferred_element_type=f32,
            )
            score[g, b] = jnp.where(allowed, value, 0.0)

    square[...] = jnp.zeros_like(square)
    load_z.wait()
    load_gain.wait()

    def local_step(c, _):
        g = c // (chunks // groups)
        one_hot = hot[c]
        one_hot_wide = spread(c, BLOCK)
        lane = lax.broadcasted_iota(jnp.int32, (BLOCK, LANES), 1)
        locals_ = []
        for b in range(blocks):
            here = slice(b * BLOCK, (b + 1) * BLOCK)
            across = dot(packed[4, here, :], one_hot_wide)
            damped = score[g, b]
            pieces = []
            for j in range(per_chunk // 2):
                mixes = []
                for i in (2 * j, 2 * j + 1):
                    gap = across[:, i * BLOCK : (i + 1) * BLOCK] - cum_turned[b, c, i : i + 1, :]
                    mixes.append((damped * jnp.exp(jnp.minimum(gap, 0.0))).astype(bf16))
                values = scaled[c, here, j * LANES : (j + 1) * LANES]
                zero = jnp.zeros_like(values)
                left = jnp.where(lane < HEAD_DIM, values, zero)
                right = jnp.where(lane < HEAD_DIM, zero, values)
                pieces.append(
                    dot(jnp.concatenate(mixes, axis=1), jnp.concatenate([left, right], axis=0))
                )
            locals_.append(jnp.concatenate(pieces, axis=1))
        inner = dot(packed[3, BLOCK:, :], one_hot) * dot(c_conv[g, BLOCK:, :], first_s[c])
        few = dot(packed[5, 0:16, :], one_hot)
        total = jnp.concatenate([locals_[0], locals_[1] + inner], axis=0)
        gated[c] = total + few[8:9, :] * x_conv[c].astype(f32)
        return 0

    def chain_event(e):
        c = event_chunk(e)
        one_hot = hot[c]
        decay_own = dot(d_own[...], one_hot)[0:1, :]
        decay_pair = dot(d_pair[...], one_hot)[0:1, :]
        decay_first = jnp.where(even, decay_own, decay_pair)
        decay_second = jnp.where(even, decay_pair, decay_own)
        near = jnp.where(e < n, 2 * n, e - n)
        for part in range(SUBS):
            lines = lines_of(part)

            @pl.when(e >= n)
            def _():
                near_copy(e - n, part).wait_recv()

            @pl.when(has_chain_in)
            def _():
                chain_copy(e, part).wait_recv()

            own = own_s[c, lines].astype(f32)
            other = near_in[near, lines].astype(f32)
            before = chain_in[e, lines].astype(f32)
            middle = jnp.where(even, own, other) + decay_first * before
            after = jnp.where(even, other, own) + decay_second * middle

            @pl.when(has_chain_out & ((e >= n) | has_chain_in))
            def _():
                chain_out[e, lines] = after.astype(bf16)
                chain_copy(e, part).start()

            @pl.when(e < 2 * n)
            def _():
                back_out[e, lines] = jnp.where(even, middle, before).astype(bf16)

                @pl.when(has_chain_in)
                def _():
                    back_copy(e, part).start()

            enter[c, lines] = jnp.where(even, before, middle).astype(bf16)

        @pl.when((e == 2 * n - 1) & (hop == 0))
        def _():
            for other_e in range(2 * n):
                for part in range(SUBS):
                    back_copy(other_e, part).start()

    def last_step(f, _):
        t = f - 2 * n
        late = jnp.where(lax.rem(t, 2) == 0, n + t // 2, give + t // 2)
        c = jnp.where(f < n, keep + f, jnp.where(f < 2 * n, f - n, late))
        added = (f >= n) & ((f < 2 * n) | (lax.rem(f, 2) == 1))
        slot = jnp.where(f < 2 * n, f - n, n + t // 2)
        slot = jnp.where(added, slot, 2 * n)
        g = c // (chunks // groups)

        @pl.when(added)
        def _():
            for part in range(SUBS):
                back_copy(slot, part).wait_recv()

        entering = (enter[c].astype(f32) + back_in[slot].astype(f32)).astype(bf16)
        total = gated[c] + dot(packed[2], hot[c]) * dot(c_conv[g], entering)
        lanes = pl.ds(pl.multiple_of(c * WIDE, WIDE), WIDE)
        value = total * silu(z_ref[:, lanes].astype(f32))
        gated[c] = value
        power = value * value
        square[...] += power[:, :LANES] + power[:, LANES:]
        return 0

    def locals_before(e):
        count = jnp.where(hop == 0, 2 * e - 3 * n // 2, chunks)
        count = jnp.where(hop == 1, 2 * e + n, count)
        count = jnp.where(e >= events - 1, chunks, count)
        return jnp.clip(jnp.where(e < 0, 0, count), 0, chunks)

    def lasts_after(e):
        count = jnp.where(e < 2 * n - 1, 0, 2 * (e + 1) - 2 * n)
        count = jnp.where((hop == 0) | (locals_before(e) < chunks), 0, count)
        return jnp.where(e >= events - 1, chunks, count)

    def outer(e, _):
        lax.fori_loop(locals_before(e - 1), locals_before(e), local_step, 0)
        chain_event(e)
        lax.fori_loop(lasts_after(e - 1), lasts_after(e), last_step, 0)
        return 0

    lax.fori_loop(0, events, outer, 0)

    own_square = jnp.sum(square[...].T, axis=0, keepdims=True)
    square_own[...] = jnp.broadcast_to(own_square, square_own.shape)
    for d in range(1, head_size):
        square_copy(d).start()

    def drain_near(i, _):
        for part in range(SUBS):
            near_copy(i, part).wait_send()
            back_copy(i, part).wait_send()
        return 0

    def drain_chain(e, _):
        for part in range(SUBS):
            chain_copy(e, part).wait_send()
        return 0

    lax.fori_loop(0, 2 * n, drain_near, 0)

    @pl.when(has_chain_out)
    def _():
        lax.fori_loop(0, events, drain_chain, 0)

    d_copy().wait_send()

    @pl.when(has_next)
    def _():
        halo_copy().wait_send()

    for d in range(1, head_size):
        square_copy(d).wait_recv()
    total_square = square_own[...]
    for d in range(1, head_size):
        total_square = total_square + square_in[d - 1]
    inverse = lax.rsqrt(total_square / (xs_ref.shape[1] * head_size) + norm_epsilon)
    inverse = jnp.broadcast_to(inverse[0:1, :], (LANES, rows)).T
    inverse = jnp.concatenate([inverse] * (WIDE // LANES), axis=1)
    for c in range(chunks):
        lanes = slice(c * WIDE, (c + 1) * WIDE)
        out_ref[:, lanes] = (gated[c] * inverse * gain_ref[:, lanes]).astype(bf16)
    for d in range(1, head_size):
        square_copy(d).wait_send()


def solution(mesh):
    seq_size = mesh.shape["seq"]
    head_size = mesh.shape["head"]

    def per_device(
        xs, gate_z, b_in, c_in, dt, log_decay, d_skip, conv_x, conv_b, conv_c, gain, doc_lengths
    ):
        rows, width = xs.shape
        heads = dt.shape[1]
        groups = b_in.shape[1] // STATE
        chunks = width // WIDE
        blocks = rows // BLOCK
        per_chunk = WIDE // HEAD_DIM
        vmem = pltpu.VMEM
        dma = pltpu.SemaphoreType.DMA
        n = chunks // 4

        def states(count):
            return vmem((count, STATE, WIDE), bf16)

        return pl.pallas_call(
            functools.partial(kernel, seq_size, head_size),
            out_shape=pltpu.VMEM((rows, width), bf16),
            in_specs=[pl.BlockSpec(memory_space=pltpu.HBM)] * 12,
            out_specs=pl.BlockSpec(memory_space=pltpu.VMEM),
            scratch_shapes=[
                pltpu.SMEM(doc_lengths.shape, jnp.int32),
                vmem((rows, width), bf16),
                vmem((rows, width), bf16),
                vmem((rows, groups * STATE), bf16),
                vmem((rows, groups * STATE), bf16),
                vmem((heads, rows), f32),
                vmem((heads, rows), f32),
                vmem((1, heads), f32),
                vmem((4, width), f32),
                vmem((4, groups * STATE), f32),
                vmem((4, groups * STATE), f32),
                vmem((1, width), f32),
                vmem((HALO, width), bf16),
                vmem((HALO, width // 4), bf16),
                vmem((HALO, width // 4), bf16),
                vmem((HALO, width), bf16),
                vmem((HALO, groups * STATE), bf16),
                vmem((HALO, groups * STATE), bf16),
                states(chunks),
                states(chunks),
                states(chunks),
                states(2 * n + 1),
                states(3 * n),
                states(3 * n),
                states(2 * n),
                states(2 * n + 1),
                vmem((16, LANES), bf16),
                vmem((16, LANES), bf16),
                vmem((3, rows, LANES), f32),
                vmem((chunks, rows, WIDE), bf16),
                vmem((chunks, rows, WIDE), bf16),
                vmem((groups, rows, STATE), bf16),
                vmem((groups, rows, STATE), bf16),
                vmem((groups, blocks, STATE, BLOCK), bf16),
                vmem((groups, blocks, BLOCK, BLOCK), f32),
                vmem((blocks, chunks, 8, BLOCK), f32),
                vmem((6, rows, LANES), bf16),
                vmem((chunks, LANES, WIDE), bf16),
                vmem((chunks, rows, WIDE), f32),
                vmem((rows, LANES), f32),
                vmem((8, rows), f32),
                vmem((head_size - 1, 8, rows), f32),
                dma,
                dma,
                dma,
                dma,
                dma((2 * n, SUBS)),
                dma((2 * n, SUBS)),
                dma((3 * n, SUBS)),
                dma((3 * n, SUBS)),
                dma((2 * n, SUBS)),
                dma((2 * n, SUBS)),
                dma((head_size - 1,)),
                dma((head_size - 1,)),
                dma((13,)),
            ],
            compiler_params=pltpu.CompilerParams(
                collective_id=0, has_side_effects=True, vmem_limit_bytes=60_000_000
            ),
        )(
            doc_lengths,
            xs,
            gate_z,
            b_in,
            c_in,
            dt.T,
            log_decay.T,
            d_skip.reshape(1, -1),
            conv_x,
            conv_b,
            conv_c,
            gain.reshape(1, -1),
        )

    whole = P("seq", "head")
    across = P(None, "head")
    return jax.shard_map(
        per_device,
        mesh=mesh,
        in_specs=(
            whole,
            whole,
            whole,
            whole,
            whole,
            whole,
            P("head"),
            across,
            across,
            across,
            P("head"),
            P(),
        ),
        out_specs=whole,
        check_vma=False,
    )
```

```python
import functools

import jax
import jax.numpy as jnp
from jax import lax
from jax.experimental import pallas as pl
from jax.experimental.pallas import tpu as pltpu
from jax.sharding import PartitionSpec as P

HEAD_DIM = 64
STATE = 128
BLOCK = 128
LANES = 128
WIDE = 256
HALO = 16
SUBS = 4
norm_epsilon = 1e-05

MESH = pl.DeviceIdType.MESH
f32 = jnp.float32
bf16 = jnp.bfloat16


def silu(v):
    return v / (1.0 + jnp.exp(-v))


def split(v):
    high = v.astype(bf16)
    rest = v - high.astype(f32)
    middle = rest.astype(bf16)
    low = (rest - middle.astype(f32)).astype(bf16)
    parts = [high.astype(f32), middle.astype(f32), low.astype(f32)]
    width = LANES - 3 * v.shape[1]
    if width:
        parts.append(jnp.zeros((v.shape[0], width), f32))
    return jnp.concatenate(parts, axis=1).astype(bf16)


def dot(a, b):
    return jnp.dot(a, b, preferred_element_type=f32)


def kernel(
    seq_size,
    head_size,
    lengths_hbm,
    xs_hbm,
    z_hbm,
    b_hbm,
    c_hbm,
    dt_hbm,
    decay_hbm,
    skip_hbm,
    conv_x_hbm,
    conv_b_hbm,
    conv_c_hbm,
    gain_hbm,
    out_ref,
    lengths_ref,
    xs_ref,
    z_ref,
    b_ref,
    c_ref,
    dt_ref,
    decay_ref,
    skip_ref,
    conv_x_ref,
    conv_b_ref,
    conv_c_ref,
    gain_ref,
    tail_x,
    halo_out,
    halo_in,
    halo_x,
    halo_b,
    halo_c,
    own_s,
    first_s,
    enter,
    near_in,
    chain_out,
    chain_in,
    back_out,
    back_in,
    d_own,
    d_pair,
    masks,
    x_conv,
    scaled,
    c_conv,
    b_conv,
    b_turned,
    score,
    cum_turned,
    packed,
    hot,
    hot_wide,
    gated,
    square,
    square_own,
    square_in,
    halo_send,
    halo_recv,
    d_send,
    d_recv,
    near_send,
    near_recv,
    chain_send,
    chain_recv,
    back_send,
    back_recv,
    square_send,
    square_recv,
    load_sem,
):
    rows = xs_ref.shape[0]
    heads = dt_ref.shape[0]
    groups = b_ref.shape[1] // STATE
    chunks = xs_ref.shape[1] // WIDE
    per_chunk = WIDE // HEAD_DIM
    blocks = rows // BLOCK
    docs = lengths_ref.shape[0]
    n = chunks // 4
    events = 3 * n
    k = lax.axis_index("seq")
    me = lax.axis_index("head")
    r = lax.rem(k, 2)
    hop = k // 2
    partner = k + 1 - 2 * r
    keep = 2 * n + r * n
    give = 3 * n - r * n
    even = r == 0
    has_prev = k > 0
    has_next = k + 1 < seq_size
    has_chain_in = k > 1
    has_chain_out = k + 2 < seq_size

    def work_chunk(p):
        c = jnp.where(p < 3 * n, p - n, keep + p - 3 * n)
        c = jnp.where(p < 2 * n, p - n, c)
        return jnp.where(p < n, give + p, c)

    def event_chunk(e):
        c = jnp.where(e < 2 * n, keep + e - n, e - n)
        return jnp.where(e < n, e, c)

    def halo_copy():
        return pltpu.make_async_remote_copy(
            src_ref=halo_out,
            dst_ref=halo_in,
            send_sem=halo_send,
            recv_sem=halo_recv,
            device_id={"seq": k + 1},
            device_id_type=MESH,
        )

    def d_copy():
        return pltpu.make_async_remote_copy(
            src_ref=d_own,
            dst_ref=d_pair,
            send_sem=d_send,
            recv_sem=d_recv,
            device_id={"seq": partner},
            device_id_type=MESH,
        )

    def lines_of(part):
        return pl.ds(part * (STATE // SUBS), STATE // SUBS)

    def near_copy(i, part):
        source = jnp.where(i < n, give + i, i)
        return pltpu.make_async_remote_copy(
            src_ref=own_s.at[source, lines_of(part)],
            dst_ref=near_in.at[i, lines_of(part)],
            send_sem=near_send.at[i, part],
            recv_sem=near_recv.at[i, part],
            device_id={"seq": partner},
            device_id_type=MESH,
        )

    def chain_copy(e, part):
        return pltpu.make_async_remote_copy(
            src_ref=chain_out.at[e, lines_of(part)],
            dst_ref=chain_in.at[e, lines_of(part)],
            send_sem=chain_send.at[e, part],
            recv_sem=chain_recv.at[e, part],
            device_id={"seq": k + 2},
            device_id_type=MESH,
        )

    def back_copy(e, part):
        return pltpu.make_async_remote_copy(
            src_ref=back_out.at[e, lines_of(part)],
            dst_ref=back_in.at[e, lines_of(part)],
            send_sem=back_send.at[e, part],
            recv_sem=back_recv.at[e, part],
            device_id={"seq": partner},
            device_id_type=MESH,
        )

    def square_copy(d):
        return pltpu.make_async_remote_copy(
            src_ref=square_own,
            dst_ref=square_in.at[d - 1],
            send_sem=square_send.at[d - 1],
            recv_sem=square_recv.at[d - 1],
            device_id={"head": lax.rem(me + d, head_size)},
            device_id_type=MESH,
        )

    barrier = pltpu.get_barrier_semaphore()
    for step, there in ((-1, has_prev), (1, has_next), (-2, has_chain_in), (2, has_chain_out)):

        @pl.when(there)
        def _():
            pl.semaphore_signal(
                barrier, inc=1, device_id={"seq": k + step}, device_id_type=MESH
            )

    for d in range(1, head_size):
        pl.semaphore_signal(
            barrier,
            inc=1,
            device_id={"head": lax.rem(me + d, head_size)},
            device_id_type=MESH,
        )
    expected = head_size - 1
    for there in (has_prev, has_next, has_chain_in, has_chain_out):
        expected = expected + there.astype(jnp.int32)

    moves = (
        (xs_hbm.at[pl.ds(rows - HALO, HALO)], tail_x),
        (lengths_hbm, lengths_ref),
        (b_hbm, b_ref),
        (c_hbm, c_ref),
        (decay_hbm, decay_ref),
        (dt_hbm, dt_ref),
        (xs_hbm, xs_ref),
        (conv_b_hbm, conv_b_ref),
        (conv_x_hbm, conv_x_ref),
        (conv_c_hbm, conv_c_ref),
        (skip_hbm, skip_ref),
        (gain_hbm, gain_ref),
        (z_hbm, z_ref),
    )
    loads = [
        pltpu.make_async_copy(source, target, load_sem.at[i])
        for i, (source, target) in enumerate(moves)
    ]
    for load in loads:
        load.start()
    (
        load_tail, load_lengths, load_b, load_c, load_decay, load_dt, load_x,
        load_conv_b, load_conv_x, load_conv_c, load_skip, load_gain, load_z,
    ) = loads

    quarter = xs_ref.shape[1] // 4
    b_width = b_ref.shape[1]
    halo_row = lax.broadcasted_iota(jnp.int32, (HALO, quarter), 0) // 3

    load_tail.wait()
    parcel = jnp.zeros((HALO, quarter), f32)
    for q in range(4):
        piece = tail_x[:, q * quarter : (q + 1) * quarter].astype(f32)
        parcel = jnp.where(halo_row == q, pltpu.roll(piece, 3 * q + 3, 0), parcel)
    load_b.wait()
    load_c.wait()
    pieces = [b_ref[rows - HALO :, :].astype(f32), c_ref[rows - HALO :, :].astype(f32)]
    if quarter > 2 * b_width:
        pieces.append(jnp.zeros((HALO, quarter - 2 * b_width), f32))
    piece = pltpu.roll(jnp.concatenate(pieces, axis=1), 15, 0)
    halo_out[...] = jnp.where(halo_row == 4, piece, parcel).astype(bf16)

    load_lengths.wait()
    starts = []
    running = jnp.int32(0)
    for j in range(docs):
        starts.append(running)
        running = running + lengths_ref[j]

    def start_at(position):
        found = jnp.full_like(position, -1)
        for start in starts:
            found = jnp.where(start <= position, start, found)
        return found

    base = k * rows
    column = base + lax.broadcasted_iota(jnp.int32, (rows, LANES), 0)
    own_start = start_at(column)
    for d in range(1, 4):
        masks[d - 1] = jnp.where(column - own_start >= d, 1.0, 0.0).astype(f32)
    lasts = [start_at(base + (b + 1) * BLOCK - 1) for b in range(blocks)]
    load_decay.wait()
    load_dt.wait()
    load_skip.wait()

    def turn(v):
        wide = jnp.concatenate([v, jnp.zeros((LANES - heads, rows), f32)], axis=0)
        return wide.T[:, :heads]

    dt_rows = turn(dt_ref[...])
    decay_rows = turn(decay_ref[...])
    t_index = lax.broadcasted_iota(jnp.int32, (BLOCK, BLOCK), 0)
    s_index = lax.broadcasted_iota(jnp.int32, (BLOCK, BLOCK), 1)
    lower = jnp.where(s_index <= t_index, 1.0, 0.0).astype(bf16)
    ends, enters, cums = [], [], []
    for b in range(blocks):
        here = slice(b * BLOCK, (b + 1) * BLOCK)
        parts = dot(lower, split(decay_rows[here, :]))
        cum = parts[:, :heads] + parts[:, heads : 2 * heads] + parts[:, 2 * heads : 3 * heads]
        begun = own_start[here, :heads]
        ends.append(jnp.where(begun == lasts[b], jnp.exp(cum[BLOCK - 1 :, :] - cum), 0.0))
        enters.append(jnp.where(begun < base + b * BLOCK, jnp.exp(cum), 0.0))
        cums.append(cum)
    carry0 = enters[0][BLOCK - 1 :, :]
    carry1 = enters[1][BLOCK - 1 :, :]
    d_own[...] = split(jnp.broadcast_to(carry0 * carry1, (16, heads)))
    packed[0] = split(dt_rows)
    packed[1] = split(jnp.concatenate(ends, axis=0))
    few = split(
        jnp.concatenate(
            [jnp.broadcast_to(carry1, (8, heads)), jnp.broadcast_to(skip_ref[...], (8, heads))], 0
        )
    )
    packed[5, 0:16, :] = few

    def spread(c, width):
        row = lax.broadcasted_iota(jnp.int32, (LANES, per_chunk * width), 0)
        lane = lax.broadcasted_iota(jnp.int32, (LANES, per_chunk * width), 1)
        wanted = c * per_chunk + lane // width
        hit = (row == wanted) | (row == wanted + heads) | (row == wanted + 2 * heads)
        return jnp.where(hit, 1.0, 0.0).astype(bf16)

    def convolve(x, weight):
        x = x.astype(f32)
        total = weight[3:4, :] * x
        for d in range(1, 4):
            total = total + weight[3 - d : 4 - d, :] * (pltpu.roll(x, d, 0) * masks[d - 1])
        return silu(total).astype(bf16)

    def convolve_top(x, halo, weight):
        window = jnp.concatenate([halo.astype(f32), x.astype(f32)], axis=0)
        total = weight[3:4, :] * window[HALO:]
        for d in range(1, 4):
            shifted = window[HALO - d : 2 * HALO - d] * masks[d - 1, 0:HALO, :]
            total = total + weight[3 - d : 4 - d, :] * shifted
        return silu(total).astype(bf16)

    load_conv_b.wait()
    for g in range(groups):
        lanes = slice(g * STATE, (g + 1) * STATE)
        b_conv[g] = convolve(b_ref[:, lanes], conv_b_ref[:, lanes])
        b_turned[g, 1] = b_conv[g, BLOCK:, :].astype(f32).T.astype(bf16)

    load_x.wait()
    load_conv_x.wait()
    pl.semaphore_wait(barrier, expected)

    @pl.when(has_next)
    def _():
        halo_copy().start()

    d_copy().start()

    def lanes_of(c, half):
        return pl.ds(pl.multiple_of(c * WIDE + half * LANES, LANES), LANES)

    def conv_step(p, _):
        c = work_chunk(p)
        for half in range(WIDE // LANES):
            lanes = lanes_of(c, half)
            x_conv[c, :, half * LANES : (half + 1) * LANES] = convolve(
                xs_ref[:, lanes], conv_x_ref[:, lanes]
            )
        return 0

    lax.fori_loop(0, 3 * n, conv_step, 0)

    def hot_step(c, _):
        hot[c] = spread(c, HEAD_DIM)
        hot_wide[c] = spread(c, BLOCK)
        return 0

    lax.fori_loop(0, chunks, hot_step, 0)

    @pl.when(k < 2)
    def _():
        chain_in[...] = jnp.zeros_like(chain_in)

    near_in[2 * n] = jnp.zeros_like(near_in[2 * n])
    back_in[2 * n] = jnp.zeros_like(back_in[2 * n])
    for i in range(n):
        enter[give + i] = jnp.zeros_like(enter[give + i])

    @pl.when(k == 0)
    def _():
        halo_in[...] = jnp.zeros_like(halo_in)

    @pl.when(has_prev)
    def _():
        halo_copy().wait_recv()

    arrived = halo_in[...].astype(f32)
    for q in range(4):
        halo_x[:, q * quarter : (q + 1) * quarter] = pltpu.roll(
            arrived, HALO - 3 - 3 * q, 0
        ).astype(bf16)
    piece = pltpu.roll(arrived, 1, 0)
    halo_b[...] = piece[:, :b_width].astype(bf16)
    halo_c[...] = piece[:, b_width : 2 * b_width].astype(bf16)

    for g in range(groups):
        lanes = slice(g * STATE, (g + 1) * STATE)
        b_conv[g, 0:HALO, :] = convolve_top(b_ref[0:HALO, lanes], halo_b[:, lanes], conv_b_ref[:, lanes])
        b_turned[g, 0] = b_conv[g, :BLOCK, :].astype(f32).T.astype(bf16)

    def state_step(p, _):
        c = work_chunk(p)
        g = c // (chunks // groups)
        for half in range(WIDE // LANES):
            lanes = lanes_of(c, half)
            x_conv[c, 0:HALO, half * LANES : (half + 1) * LANES] = convolve_top(
                xs_ref[0:HALO, lanes], halo_x[:, lanes], conv_x_ref[:, lanes]
            )
        x = x_conv[c]
        one_hot = hot[c]
        product = (dot(packed[0], one_hot) * x.astype(f32)).astype(bf16)
        scaled[c] = product
        weighted = (dot(packed[1], one_hot) * product.astype(f32)).astype(bf16)
        state0 = dot(b_turned[g, 0], weighted[:BLOCK])
        state1 = dot(b_turned[g, 1], weighted[BLOCK:])
        few = dot(packed[5, 0:16, :], one_hot)
        first_s[c] = state0.astype(bf16)
        state = (few[0:1, :] * state0 + state1).astype(bf16)
        own_s[c] = state

        @pl.when(p < n)
        def _():
            for part in range(SUBS):
                near_copy(p, part).start()

        @pl.when((p >= 2 * n) & (p < 3 * n))
        def _():
            for part in range(SUBS):
                near_copy(p - n, part).start()

        @pl.when(p == n)
        def _():
            d_copy().wait_recv()

        @pl.when((p >= n) & (p < 2 * n) & (hop == 0) & has_chain_out)
        def _():
            decay_pair = dot(d_pair[...], one_hot)[0:1, :]
            wide = state.astype(f32)
            chain_out[p - n] = jnp.where(even, decay_pair * wide, wide).astype(bf16)
            for part in range(SUBS):
                chain_copy(p - n, part).start()

        return 0

    lax.fori_loop(0, 3 * n, state_step, 0)
    lax.fori_loop(3 * n, chunks, conv_step, 0)
    lax.fori_loop(3 * n, chunks, state_step, 0)
    load_conv_c.wait()

    packed[2] = split(jnp.concatenate([enters[0], enters[1] * carry0], axis=0))
    packed[3] = split(jnp.concatenate([enters[0], enters[1]], axis=0))
    packed[4] = split(jnp.concatenate(cums, axis=0))
    for b in range(blocks):
        wide = jnp.concatenate([cums[b], jnp.zeros((BLOCK, LANES - heads), f32)], axis=1)
        turned = wide.T
        for c in range(chunks):
            cum_turned[b, c, 0:per_chunk, :] = turned[c * per_chunk : (c + 1) * per_chunk, :]

    for g in range(groups):
        lanes = slice(g * STATE, (g + 1) * STATE)
        c_conv[g] = convolve(c_ref[:, lanes], conv_c_ref[:, lanes])
        c_conv[g, 0:HALO, :] = convolve_top(c_ref[0:HALO, lanes], halo_c[:, lanes], conv_c_ref[:, lanes])

    for b in range(blocks):
        here = slice(b * BLOCK, (b + 1) * BLOCK)
        allowed = (base + b * BLOCK + s_index >= own_start[here, :]) & (s_index <= t_index)
        for g in range(groups):
            value = lax.dot_general(
                c_conv[g, here, :],
                b_conv[g, here, :],
                (((1,), (1,)), ((), ())),
                preferred_element_type=f32,
            )
            score[g, b] = jnp.where(allowed, value, 0.0)

    square[...] = jnp.zeros_like(square)
    load_z.wait()
    load_gain.wait()

    def local_step(c, _):
        g = c // (chunks // groups)
        one_hot = hot[c]
        one_hot_wide = hot_wide[c]
        lane = lax.broadcasted_iota(jnp.int32, (BLOCK, LANES), 1)
        locals_ = []
        for b in range(blocks):
            here = slice(b * BLOCK, (b + 1) * BLOCK)
            across = dot(packed[4, here, :], one_hot_wide)
            damped = score[g, b]
            pieces = []
            for j in range(per_chunk // 2):
                mixes = []
                for i in (2 * j, 2 * j + 1):
                    gap = across[:, i * BLOCK : (i + 1) * BLOCK] - cum_turned[b, c, i : i + 1, :]
                    mixes.append((damped * jnp.exp(jnp.minimum(gap, 0.0))).astype(bf16))
                values = scaled[c, here, j * LANES : (j + 1) * LANES]
                zero = jnp.zeros_like(values)
                left = jnp.where(lane < HEAD_DIM, values, zero)
                right = jnp.where(lane < HEAD_DIM, zero, values)
                pieces.append(
                    dot(jnp.concatenate(mixes, axis=1), jnp.concatenate([left, right], axis=0))
                )
            locals_.append(jnp.concatenate(pieces, axis=1))
        inner = dot(packed[3, BLOCK:, :], one_hot) * dot(c_conv[g, BLOCK:, :], first_s[c])
        few = dot(packed[5, 0:16, :], one_hot)
        total = jnp.concatenate([locals_[0], locals_[1] + inner], axis=0)
        gated[c] = total + few[8:9, :] * x_conv[c].astype(f32)
        return 0

    def chain_event(e):
        c = event_chunk(e)
        one_hot = hot[c]
        decay_own = dot(d_own[...], one_hot)[0:1, :]
        decay_pair = dot(d_pair[...], one_hot)[0:1, :]
        decay_first = jnp.where(even, decay_own, decay_pair)
        decay_second = jnp.where(even, decay_pair, decay_own)
        near = jnp.where(e < n, 2 * n, e - n)
        for part in range(SUBS):
            lines = lines_of(part)

            @pl.when(e >= n)
            def _():
                near_copy(e - n, part).wait_recv()

            @pl.when(has_chain_in)
            def _():
                chain_copy(e, part).wait_recv()

            own = own_s[c, lines].astype(f32)
            other = near_in[near, lines].astype(f32)
            before = chain_in[e, lines].astype(f32)
            middle = jnp.where(even, own, other) + decay_first * before
            after = jnp.where(even, other, own) + decay_second * middle

            @pl.when(has_chain_out & ((e >= n) | has_chain_in))
            def _():
                chain_out[e, lines] = after.astype(bf16)
                chain_copy(e, part).start()

            @pl.when(e < 2 * n)
            def _():
                back_out[e, lines] = jnp.where(even, middle, before).astype(bf16)

                @pl.when(has_chain_in)
                def _():
                    back_copy(e, part).start()

            enter[c, lines] = jnp.where(even, before, middle).astype(bf16)

        @pl.when((e == 2 * n - 1) & (hop == 0))
        def _():
            for other_e in range(2 * n):
                for part in range(SUBS):
                    back_copy(other_e, part).start()

    def last_step(f, _):
        t = f - 2 * n
        late = jnp.where(lax.rem(t, 2) == 0, n + t // 2, give + t // 2)
        c = jnp.where(f < n, keep + f, jnp.where(f < 2 * n, f - n, late))
        added = (f >= n) & ((f < 2 * n) | (lax.rem(f, 2) == 1))
        slot = jnp.where(f < 2 * n, f - n, n + t // 2)
        slot = jnp.where(added, slot, 2 * n)
        g = c // (chunks // groups)

        @pl.when(added)
        def _():
            for part in range(SUBS):
                back_copy(slot, part).wait_recv()

        entering = (enter[c].astype(f32) + back_in[slot].astype(f32)).astype(bf16)
        total = gated[c] + dot(packed[2], hot[c]) * dot(c_conv[g], entering)
        lanes = pl.ds(pl.multiple_of(c * WIDE, WIDE), WIDE)
        value = total * silu(z_ref[:, lanes].astype(f32))
        gated[c] = value
        power = value * value
        square[...] += power[:, :LANES] + power[:, LANES:]
        return 0

    def locals_before(e):
        count = jnp.where(hop == 0, e - n, chunks)
        count = jnp.where(hop == 1, e, count)
        count = jnp.where(hop == 2, e + 3 * n // 2, count)
        count = jnp.where(e >= events, chunks, count)
        return jnp.clip(jnp.where(e < 0, 0, count), 0, chunks)

    def lasts_after(e):
        count = jnp.where(e < 2 * n - 1, 0, 2 * (e + 1) - 2 * n)
        count = jnp.where(has_chain_out | (locals_before(e) < chunks), 0, count)
        return jnp.where(e >= events, chunks, count)

    def outer(e, _):
        lax.fori_loop(locals_before(e - 1), locals_before(e), local_step, 0)

        @pl.when(e < events)
        def _():
            chain_event(e)

        lax.fori_loop(lasts_after(e - 1), lasts_after(e), last_step, 0)
        return 0

    lax.fori_loop(0, events + 1, outer, 0)

    own_square = jnp.sum(square[...].T, axis=0, keepdims=True)
    square_own[...] = jnp.broadcast_to(own_square, square_own.shape)
    for d in range(1, head_size):
        square_copy(d).start()

    def drain_near(i, _):
        for part in range(SUBS):
            near_copy(i, part).wait_send()
            back_copy(i, part).wait_send()
        return 0

    def drain_chain(e, _):
        for part in range(SUBS):
            chain_copy(e, part).wait_send()
        return 0

    lax.fori_loop(0, 2 * n, drain_near, 0)

    @pl.when(has_chain_out)
    def _():
        lax.fori_loop(0, events, drain_chain, 0)

    d_copy().wait_send()

    @pl.when(has_next)
    def _():
        halo_copy().wait_send()

    for d in range(1, head_size):
        square_copy(d).wait_recv()
    total_square = square_own[...]
    for d in range(1, head_size):
        total_square = total_square + square_in[d - 1]
    inverse = lax.rsqrt(total_square / (xs_ref.shape[1] * head_size) + norm_epsilon)
    inverse = jnp.broadcast_to(inverse[0:1, :], (LANES, rows)).T
    inverse = jnp.concatenate([inverse] * (WIDE // LANES), axis=1)
    for c in range(chunks):
        lanes = slice(c * WIDE, (c + 1) * WIDE)
        out_ref[:, lanes] = (gated[c] * inverse * gain_ref[:, lanes]).astype(bf16)
    for d in range(1, head_size):
        square_copy(d).wait_send()


def solution(mesh):
    seq_size = mesh.shape["seq"]
    head_size = mesh.shape["head"]

    def per_device(
        xs, gate_z, b_in, c_in, dt, log_decay, d_skip, conv_x, conv_b, conv_c, gain, doc_lengths
    ):
        rows, width = xs.shape
        heads = dt.shape[1]
        groups = b_in.shape[1] // STATE
        chunks = width // WIDE
        blocks = rows // BLOCK
        per_chunk = WIDE // HEAD_DIM
        vmem = pltpu.VMEM
        dma = pltpu.SemaphoreType.DMA
        n = chunks // 4

        def states(count):
            return vmem((count, STATE, WIDE), bf16)

        return pl.pallas_call(
            functools.partial(kernel, seq_size, head_size),
            out_shape=pltpu.VMEM((rows, width), bf16),
            in_specs=[pl.BlockSpec(memory_space=pltpu.HBM)] * 12,
            out_specs=pl.BlockSpec(memory_space=pltpu.VMEM),
            scratch_shapes=[
                pltpu.SMEM(doc_lengths.shape, jnp.int32),
                vmem((rows, width), bf16),
                vmem((rows, width), bf16),
                vmem((rows, groups * STATE), bf16),
                vmem((rows, groups * STATE), bf16),
                vmem((heads, rows), f32),
                vmem((heads, rows), f32),
                vmem((1, heads), f32),
                vmem((4, width), f32),
                vmem((4, groups * STATE), f32),
                vmem((4, groups * STATE), f32),
                vmem((1, width), f32),
                vmem((HALO, width), bf16),
                vmem((HALO, width // 4), bf16),
                vmem((HALO, width // 4), bf16),
                vmem((HALO, width), bf16),
                vmem((HALO, groups * STATE), bf16),
                vmem((HALO, groups * STATE), bf16),
                states(chunks),
                states(chunks),
                states(chunks),
                states(2 * n + 1),
                states(3 * n),
                states(3 * n),
                states(2 * n),
                states(2 * n + 1),
                vmem((16, LANES), bf16),
                vmem((16, LANES), bf16),
                vmem((3, rows, LANES), f32),
                vmem((chunks, rows, WIDE), bf16),
                vmem((chunks, rows, WIDE), bf16),
                vmem((groups, rows, STATE), bf16),
                vmem((groups, rows, STATE), bf16),
                vmem((groups, blocks, STATE, BLOCK), bf16),
                vmem((groups, blocks, BLOCK, BLOCK), f32),
                vmem((blocks, chunks, 8, BLOCK), f32),
                vmem((6, rows, LANES), bf16),
                vmem((chunks, LANES, WIDE), bf16),
                vmem((chunks, LANES, per_chunk * BLOCK), bf16),
                vmem((chunks, rows, WIDE), f32),
                vmem((rows, LANES), f32),
                vmem((8, rows), f32),
                vmem((head_size - 1, 8, rows), f32),
                dma,
                dma,
                dma,
                dma,
                dma((2 * n, SUBS)),
                dma((2 * n, SUBS)),
                dma((3 * n, SUBS)),
                dma((3 * n, SUBS)),
                dma((2 * n, SUBS)),
                dma((2 * n, SUBS)),
                dma((head_size - 1,)),
                dma((head_size - 1,)),
                dma((13,)),
            ],
            compiler_params=pltpu.CompilerParams(
                collective_id=0, has_side_effects=True, vmem_limit_bytes=60_000_000
            ),
        )(
            doc_lengths,
            xs,
            gate_z,
            b_in,
            c_in,
            dt.T,
            log_decay.T,
            d_skip.reshape(1, -1),
            conv_x,
            conv_b,
            conv_c,
            gain.reshape(1, -1),
        )

    whole = P("seq", "head")
    across = P(None, "head")
    return jax.shard_map(
        per_device,
        mesh=mesh,
        in_specs=(
            whole,
            whole,
            whole,
            whole,
            whole,
            whole,
            P("head"),
            across,
            across,
            across,
            P("head"),
            P(),
        ),
        out_specs=whole,
        check_vma=False,
    )
```

```python
import functools

import jax
import jax.numpy as jnp
from jax import lax
from jax.experimental import pallas as pl
from jax.experimental.pallas import tpu as pltpu
from jax.sharding import PartitionSpec as P

HEAD_DIM = 64
STATE = 128
BLOCK = 128
LANES = 128
WIDE = 256
HALO = 16
SUBS = 4
NEAR = 2
CHAIN = 4
BACK = 2
norm_epsilon = 1e-05

MESH = pl.DeviceIdType.MESH
f32 = jnp.float32
bf16 = jnp.bfloat16


def silu(v):
    return v / (1.0 + jnp.exp(-v))


def split(v):
    high = v.astype(bf16)
    rest = v - high.astype(f32)
    middle = rest.astype(bf16)
    low = (rest - middle.astype(f32)).astype(bf16)
    parts = [high.astype(f32), middle.astype(f32), low.astype(f32)]
    width = LANES - 3 * v.shape[1]
    if width:
        parts.append(jnp.zeros((v.shape[0], width), f32))
    return jnp.concatenate(parts, axis=1).astype(bf16)


def dot(a, b):
    return jnp.dot(a, b, preferred_element_type=f32)


def kernel(
    seq_size,
    head_size,
    lengths_hbm,
    xs_hbm,
    z_hbm,
    b_hbm,
    c_hbm,
    dt_hbm,
    decay_hbm,
    skip_hbm,
    conv_x_hbm,
    conv_b_hbm,
    conv_c_hbm,
    gated,
    inverse_ref,
    lengths_ref,
    xs_ref,
    z_ref,
    b_ref,
    c_ref,
    dt_ref,
    decay_ref,
    skip_ref,
    conv_x_ref,
    conv_b_ref,
    conv_c_ref,
    tail_x,
    halo_out,
    halo_in,
    halo_x,
    halo_b,
    halo_c,
    own_s,
    first_s,
    enter,
    near_in,
    chain_out,
    chain_in,
    back_out,
    back_in,
    d_own,
    d_pair,
    masks,
    x_conv,
    scaled,
    c_conv,
    b_conv,
    b_turned,
    score,
    cum_turned,
    packed,
    hot,
    hot_wide,
    square,
    square_own,
    square_in,
    halo_send,
    halo_recv,
    d_send,
    d_recv,
    near_send,
    near_recv,
    chain_send,
    chain_recv,
    back_send,
    back_recv,
    square_send,
    square_recv,
    load_sem,
):
    rows = xs_ref.shape[0]
    heads = dt_ref.shape[0]
    groups = b_ref.shape[1] // STATE
    chunks = xs_ref.shape[1] // WIDE
    per_chunk = WIDE // HEAD_DIM
    blocks = rows // BLOCK
    docs = lengths_ref.shape[0]
    n = chunks // 4
    events = 3 * n
    k = lax.axis_index("seq")
    me = lax.axis_index("head")
    r = lax.rem(k, 2)
    hop = k // 2
    partner = k + 1 - 2 * r
    keep = 2 * n + r * n
    give = 3 * n - r * n
    even = r == 0
    has_prev = k > 0
    has_next = k + 1 < seq_size
    has_chain_in = k > 1
    has_chain_out = k + 2 < seq_size

    def work_chunk(p):
        c = jnp.where(p < 3 * n, p - n, keep + p - 3 * n)
        c = jnp.where(p < 2 * n, give + p - n, c)
        return jnp.where(p < n, p, c)

    def event_chunk(e):
        c = jnp.where(e < 2 * n, keep + e - n, e - n)
        return jnp.where(e < n, e, c)

    def halo_copy():
        return pltpu.make_async_remote_copy(
            src_ref=halo_out,
            dst_ref=halo_in,
            send_sem=halo_send,
            recv_sem=halo_recv,
            device_id={"seq": k + 1},
            device_id_type=MESH,
        )

    def d_copy():
        return pltpu.make_async_remote_copy(
            src_ref=d_own,
            dst_ref=d_pair,
            send_sem=d_send,
            recv_sem=d_recv,
            device_id={"seq": partner},
            device_id_type=MESH,
        )

    def lines_of(part, parts=SUBS):
        return pl.ds(part * (STATE // parts), STATE // parts)

    def near_copy(i, part):
        source = jnp.where(i < n, give + i, i)
        return pltpu.make_async_remote_copy(
            src_ref=own_s.at[source, lines_of(part, NEAR)],
            dst_ref=near_in.at[i, lines_of(part, NEAR)],
            send_sem=near_send.at[i, part],
            recv_sem=near_recv.at[i, part],
            device_id={"seq": partner},
            device_id_type=MESH,
        )

    def chain_copy(e, part):
        return pltpu.make_async_remote_copy(
            src_ref=chain_out.at[e, lines_of(part, CHAIN)],
            dst_ref=chain_in.at[e, lines_of(part, CHAIN)],
            send_sem=chain_send.at[e, part],
            recv_sem=chain_recv.at[e, part],
            device_id={"seq": k + 2},
            device_id_type=MESH,
        )

    def back_copy(e, part):
        return pltpu.make_async_remote_copy(
            src_ref=back_out.at[e, lines_of(part, BACK)],
            dst_ref=back_in.at[e, lines_of(part, BACK)],
            send_sem=back_send.at[e, part],
            recv_sem=back_recv.at[e, part],
            device_id={"seq": partner},
            device_id_type=MESH,
        )

    def square_copy(d):
        return pltpu.make_async_remote_copy(
            src_ref=square_own,
            dst_ref=square_in.at[d - 1],
            send_sem=square_send.at[d - 1],
            recv_sem=square_recv.at[d - 1],
            device_id={"head": lax.rem(me + d, head_size)},
            device_id_type=MESH,
        )

    barrier = pltpu.get_barrier_semaphore()
    for step, there in ((-1, has_prev), (1, has_next), (-2, has_chain_in), (2, has_chain_out)):

        @pl.when(there)
        def _():
            pl.semaphore_signal(
                barrier, inc=1, device_id={"seq": k + step}, device_id_type=MESH
            )

    for d in range(1, head_size):
        pl.semaphore_signal(
            barrier,
            inc=1,
            device_id={"head": lax.rem(me + d, head_size)},
            device_id_type=MESH,
        )
    expected = head_size - 1
    for there in (has_prev, has_next, has_chain_in, has_chain_out):
        expected = expected + there.astype(jnp.int32)

    moves = (
        (xs_hbm.at[pl.ds(rows - HALO, HALO)], tail_x),
        (lengths_hbm, lengths_ref),
        (b_hbm, b_ref),
        (c_hbm, c_ref),
        (decay_hbm, decay_ref),
        (dt_hbm, dt_ref),
        (xs_hbm, xs_ref),
        (conv_b_hbm, conv_b_ref),
        (conv_x_hbm, conv_x_ref),
        (conv_c_hbm, conv_c_ref),
        (skip_hbm, skip_ref),
        (z_hbm, z_ref),
    )
    loads = [
        pltpu.make_async_copy(source, target, load_sem.at[i])
        for i, (source, target) in enumerate(moves)
    ]
    for load in loads:
        load.start()
    (
        load_tail, load_lengths, load_b, load_c, load_decay, load_dt, load_x,
        load_conv_b, load_conv_x, load_conv_c, load_skip, load_z,
    ) = loads

    quarter = xs_ref.shape[1] // 4
    b_width = b_ref.shape[1]
    halo_row = lax.broadcasted_iota(jnp.int32, (HALO, quarter), 0) // 3

    load_tail.wait()
    parcel = jnp.zeros((HALO, quarter), f32)
    for q in range(4):
        piece = tail_x[:, q * quarter : (q + 1) * quarter].astype(f32)
        parcel = jnp.where(halo_row == q, pltpu.roll(piece, 3 * q + 3, 0), parcel)
    load_b.wait()
    load_c.wait()
    pieces = [b_ref[rows - HALO :, :].astype(f32), c_ref[rows - HALO :, :].astype(f32)]
    if quarter > 2 * b_width:
        pieces.append(jnp.zeros((HALO, quarter - 2 * b_width), f32))
    piece = pltpu.roll(jnp.concatenate(pieces, axis=1), 15, 0)
    halo_out[...] = jnp.where(halo_row == 4, piece, parcel).astype(bf16)

    load_lengths.wait()
    starts = []
    running = jnp.int32(0)
    for j in range(docs):
        starts.append(running)
        running = running + lengths_ref[j]

    def start_at(position):
        found = jnp.full_like(position, -1)
        for start in starts:
            found = jnp.where(start <= position, start, found)
        return found

    base = k * rows
    column = base + lax.broadcasted_iota(jnp.int32, (rows, LANES), 0)
    own_start = start_at(column)
    for d in range(1, 4):
        masks[d - 1] = jnp.where(column - own_start >= d, 1.0, 0.0).astype(f32)
    lasts = [start_at(base + (b + 1) * BLOCK - 1) for b in range(blocks)]
    load_decay.wait()
    load_dt.wait()
    load_skip.wait()

    def turn(v):
        wide = jnp.concatenate([v, jnp.zeros((LANES - heads, rows), f32)], axis=0)
        return wide.T[:, :heads]

    dt_rows = turn(dt_ref[...])
    decay_rows = turn(decay_ref[...])
    t_index = lax.broadcasted_iota(jnp.int32, (BLOCK, BLOCK), 0)
    s_index = lax.broadcasted_iota(jnp.int32, (BLOCK, BLOCK), 1)
    lower = jnp.where(s_index <= t_index, 1.0, 0.0).astype(bf16)
    ends, enters, cums = [], [], []
    for b in range(blocks):
        here = slice(b * BLOCK, (b + 1) * BLOCK)
        parts = dot(lower, split(decay_rows[here, :]))
        cum = parts[:, :heads] + parts[:, heads : 2 * heads] + parts[:, 2 * heads : 3 * heads]
        begun = own_start[here, :heads]
        ends.append(jnp.where(begun == lasts[b], jnp.exp(cum[BLOCK - 1 :, :] - cum), 0.0))
        enters.append(jnp.where(begun < base + b * BLOCK, jnp.exp(cum), 0.0))
        cums.append(cum)
    carry0 = enters[0][BLOCK - 1 :, :]
    carry1 = enters[1][BLOCK - 1 :, :]
    d_own[...] = split(jnp.broadcast_to(carry0 * carry1, (16, heads)))
    packed[0] = split(dt_rows)
    packed[1] = split(jnp.concatenate(ends, axis=0))
    few = split(
        jnp.concatenate(
            [jnp.broadcast_to(carry1, (8, heads)), jnp.broadcast_to(skip_ref[...], (8, heads))], 0
        )
    )
    packed[5, 0:16, :] = few

    def spread(c, width):
        row = lax.broadcasted_iota(jnp.int32, (LANES, per_chunk * width), 0)
        lane = lax.broadcasted_iota(jnp.int32, (LANES, per_chunk * width), 1)
        wanted = c * per_chunk + lane // width
        hit = (row == wanted) | (row == wanted + heads) | (row == wanted + 2 * heads)
        return jnp.where(hit, 1.0, 0.0).astype(bf16)

    def convolve(x, weight):
        x = x.astype(f32)
        total = weight[3:4, :] * x
        for d in range(1, 4):
            total = total + weight[3 - d : 4 - d, :] * (pltpu.roll(x, d, 0) * masks[d - 1])
        return silu(total).astype(bf16)

    def convolve_top(x, halo, weight):
        window = jnp.concatenate([halo.astype(f32), x.astype(f32)], axis=0)
        total = weight[3:4, :] * window[HALO:]
        for d in range(1, 4):
            shifted = window[HALO - d : 2 * HALO - d] * masks[d - 1, 0:HALO, :]
            total = total + weight[3 - d : 4 - d, :] * shifted
        return silu(total).astype(bf16)

    load_conv_b.wait()
    for g in range(groups):
        lanes = slice(g * STATE, (g + 1) * STATE)
        b_conv[g] = convolve(b_ref[:, lanes], conv_b_ref[:, lanes])
        b_turned[g, 1] = b_conv[g, BLOCK:, :].astype(f32).T.astype(bf16)

    load_x.wait()
    load_conv_x.wait()
    pl.semaphore_wait(barrier, expected)

    @pl.when(has_next)
    def _():
        halo_copy().start()

    d_copy().start()

    def lanes_of(c, half):
        return pl.ds(pl.multiple_of(c * WIDE + half * LANES, LANES), LANES)

    def conv_step(p, _):
        c = work_chunk(p)
        for half in range(WIDE // LANES):
            lanes = lanes_of(c, half)
            x_conv[c, :, half * LANES : (half + 1) * LANES] = convolve(
                xs_ref[:, lanes], conv_x_ref[:, lanes]
            )
        return 0

    lax.fori_loop(0, 3 * n, conv_step, 0)

    def hot_step(c, _):
        hot[c] = spread(c, HEAD_DIM)
        hot_wide[c] = spread(c, BLOCK)
        return 0

    lax.fori_loop(0, chunks, hot_step, 0)

    @pl.when(k < 2)
    def _():
        chain_in[...] = jnp.zeros_like(chain_in)

    near_in[2 * n] = jnp.zeros_like(near_in[2 * n])
    back_in[2 * n] = jnp.zeros_like(back_in[2 * n])
    for i in range(n):
        enter[give + i] = jnp.zeros_like(enter[give + i])

    @pl.when(k == 0)
    def _():
        halo_in[...] = jnp.zeros_like(halo_in)

    @pl.when(has_prev)
    def _():
        halo_copy().wait_recv()

    arrived = halo_in[...].astype(f32)
    for q in range(4):
        halo_x[:, q * quarter : (q + 1) * quarter] = pltpu.roll(
            arrived, HALO - 3 - 3 * q, 0
        ).astype(bf16)
    piece = pltpu.roll(arrived, 1, 0)
    halo_b[...] = piece[:, :b_width].astype(bf16)
    halo_c[...] = piece[:, b_width : 2 * b_width].astype(bf16)

    for g in range(groups):
        lanes = slice(g * STATE, (g + 1) * STATE)
        b_conv[g, 0:HALO, :] = convolve_top(b_ref[0:HALO, lanes], halo_b[:, lanes], conv_b_ref[:, lanes])
        b_turned[g, 0] = b_conv[g, :BLOCK, :].astype(f32).T.astype(bf16)

    def state_step(p, _):
        c = work_chunk(p)
        g = c // (chunks // groups)
        for half in range(WIDE // LANES):
            lanes = lanes_of(c, half)
            x_conv[c, 0:HALO, half * LANES : (half + 1) * LANES] = convolve_top(
                xs_ref[0:HALO, lanes], halo_x[:, lanes], conv_x_ref[:, lanes]
            )
        x = x_conv[c]
        one_hot = hot[c]
        product = (dot(packed[0], one_hot) * x.astype(f32)).astype(bf16)
        scaled[c] = product
        weighted = (dot(packed[1], one_hot) * product.astype(f32)).astype(bf16)
        state0 = dot(b_turned[g, 0], weighted[:BLOCK])
        state1 = dot(b_turned[g, 1], weighted[BLOCK:])
        few = dot(packed[5, 0:16, :], one_hot)
        first_s[c] = state0.astype(bf16)
        state = (few[0:1, :] * state0 + state1).astype(bf16)
        own_s[c] = state

        @pl.when((p >= n) & (p < 3 * n))
        def _():
            for part in range(NEAR):
                near_copy(p - n, part).start()

        @pl.when(p == 0)
        def _():
            d_copy().wait_recv()

        @pl.when((p < n) & (hop == 0) & has_chain_out)
        def _():
            decay_pair = dot(d_pair[...], one_hot)[0:1, :]
            wide = state.astype(f32)
            chain_out[p] = jnp.where(even, decay_pair * wide, wide).astype(bf16)
            for part in range(CHAIN):
                chain_copy(p, part).start()

        return 0

    lax.fori_loop(0, 3 * n, state_step, 0)
    lax.fori_loop(3 * n, chunks, conv_step, 0)
    lax.fori_loop(3 * n, chunks, state_step, 0)
    load_conv_c.wait()

    packed[2] = split(jnp.concatenate([enters[0], enters[1] * carry0], axis=0))
    packed[3] = split(jnp.concatenate([enters[0], enters[1]], axis=0))
    packed[4] = split(jnp.concatenate(cums, axis=0))
    for b in range(blocks):
        wide = jnp.concatenate([cums[b], jnp.zeros((BLOCK, LANES - heads), f32)], axis=1)
        turned = wide.T
        for c in range(chunks):
            cum_turned[b, c, 0:per_chunk, :] = turned[c * per_chunk : (c + 1) * per_chunk, :]

    for g in range(groups):
        lanes = slice(g * STATE, (g + 1) * STATE)
        c_conv[g] = convolve(c_ref[:, lanes], conv_c_ref[:, lanes])
        c_conv[g, 0:HALO, :] = convolve_top(c_ref[0:HALO, lanes], halo_c[:, lanes], conv_c_ref[:, lanes])

    for b in range(blocks):
        here = slice(b * BLOCK, (b + 1) * BLOCK)
        allowed = (base + b * BLOCK + s_index >= own_start[here, :]) & (s_index <= t_index)
        for g in range(groups):
            value = lax.dot_general(
                c_conv[g, here, :],
                b_conv[g, here, :],
                (((1,), (1,)), ((), ())),
                preferred_element_type=f32,
            )
            score[g, b] = jnp.where(allowed, value, 0.0)

    square[...] = jnp.zeros_like(square)
    load_z.wait()

    def local_step(c, _):
        g = c // (chunks // groups)
        one_hot = hot[c]
        one_hot_wide = hot_wide[c]
        lane = lax.broadcasted_iota(jnp.int32, (BLOCK, LANES), 1)
        locals_ = []
        for b in range(blocks):
            here = slice(b * BLOCK, (b + 1) * BLOCK)
            across = dot(packed[4, here, :], one_hot_wide)
            damped = score[g, b]
            pieces = []
            for j in range(per_chunk // 2):
                mixes = []
                for i in (2 * j, 2 * j + 1):
                    gap = across[:, i * BLOCK : (i + 1) * BLOCK] - cum_turned[b, c, i : i + 1, :]
                    mixes.append((damped * jnp.exp(jnp.minimum(gap, 0.0))).astype(bf16))
                values = scaled[c, here, j * LANES : (j + 1) * LANES]
                zero = jnp.zeros_like(values)
                left = jnp.where(lane < HEAD_DIM, values, zero)
                right = jnp.where(lane < HEAD_DIM, zero, values)
                pieces.append(
                    dot(jnp.concatenate(mixes, axis=1), jnp.concatenate([left, right], axis=0))
                )
            locals_.append(jnp.concatenate(pieces, axis=1))
        inner = dot(packed[3, BLOCK:, :], one_hot) * dot(c_conv[g, BLOCK:, :], first_s[c])
        few = dot(packed[5, 0:16, :], one_hot)
        total = jnp.concatenate([locals_[0], locals_[1] + inner], axis=0)
        gated[c] = total + few[8:9, :] * x_conv[c].astype(f32)
        return 0

    def chain_event(e):
        c = event_chunk(e)
        one_hot = hot[c]
        decay_own = dot(d_own[...], one_hot)[0:1, :]
        decay_pair = dot(d_pair[...], one_hot)[0:1, :]
        decay_first = jnp.where(even, decay_own, decay_pair)
        decay_second = jnp.where(even, decay_pair, decay_own)
        near = jnp.where(e < n, 2 * n, e - n)
        for part in range(SUBS):
            lines = lines_of(part)

            if part % (SUBS // NEAR) == 0:

                @pl.when(e >= n)
                def _():
                    near_copy(e - n, part * NEAR // SUBS).wait_recv()

            if part % (SUBS // CHAIN) == 0:

                @pl.when(has_chain_in)
                def _():
                    chain_copy(e, part * CHAIN // SUBS).wait_recv()

            own = own_s[c, lines].astype(f32)
            other = near_in[near, lines].astype(f32)
            before = chain_in[e, lines].astype(f32)
            middle = jnp.where(even, own, other) + decay_first * before
            after = jnp.where(even, other, own) + decay_second * middle

            @pl.when(has_chain_out & ((e >= n) | has_chain_in))
            def _():
                chain_out[e, lines] = after.astype(bf16)
                if (part + 1) % (SUBS // CHAIN) == 0:
                    chain_copy(e, part * CHAIN // SUBS).start()

            @pl.when(e < 2 * n)
            def _():
                back_out[e, lines] = jnp.where(even, middle, before).astype(bf16)

                if (part + 1) % (SUBS // BACK) == 0:

                    @pl.when(has_chain_in)
                    def _():
                        back_copy(e, part * BACK // SUBS).start()

            enter[c, lines] = jnp.where(even, before, middle).astype(bf16)

        @pl.when((e == 2 * n - 1) & (hop == 0))
        def _():
            for other_e in range(2 * n):
                for part in range(BACK):
                    back_copy(other_e, part).start()

    def last_step(f, _):
        t = f - 2 * n
        late = jnp.where(lax.rem(t, 2) == 0, n + t // 2, give + t // 2)
        c = jnp.where(f < n, keep + f, jnp.where(f < 2 * n, f - n, late))
        added = (f >= n) & ((f < 2 * n) | (lax.rem(f, 2) == 1))
        slot = jnp.where(f < 2 * n, f - n, n + t // 2)
        slot = jnp.where(added, slot, 2 * n)
        g = c // (chunks // groups)

        @pl.when(added)
        def _():
            for part in range(BACK):
                back_copy(slot, part).wait_recv()

        entering = (enter[c].astype(f32) + back_in[slot].astype(f32)).astype(bf16)
        total = gated[c] + dot(packed[2], hot[c]) * dot(c_conv[g], entering)
        lanes = pl.ds(pl.multiple_of(c * WIDE, WIDE), WIDE)
        value = total * silu(z_ref[:, lanes].astype(f32))
        gated[c] = value
        power = value * value
        square[...] += power[:, :LANES] + power[:, LANES:]
        return 0

    def locals_before(e):
        count = jnp.where(hop == 0, e - n, chunks)
        count = jnp.where(hop == 1, e, count)
        count = jnp.where(hop == 2, e + 3 * n // 2, count)
        count = jnp.where(e >= events, chunks, count)
        return jnp.clip(jnp.where(e < 0, 0, count), 0, chunks)

    def lasts_after(e):
        count = jnp.where(e < 2 * n - 1, 0, 2 * (e + 1) - 2 * n)
        count = jnp.where(has_chain_out | (locals_before(e) < chunks), 0, count)
        return jnp.where(e >= events, chunks, jnp.minimum(count, chunks))

    def outer(e, _):
        lax.fori_loop(locals_before(e - 1), locals_before(e), local_step, 0)

        @pl.when(e < events)
        def _():
            chain_event(e)

        lax.fori_loop(lasts_after(e - 1), lasts_after(e), last_step, 0)
        return 0

    lax.fori_loop(0, events + 1, outer, 0)

    own_square = jnp.sum(square[...].T, axis=0, keepdims=True)
    square_own[...] = jnp.broadcast_to(own_square, square_own.shape)
    for d in range(1, head_size):
        square_copy(d).start()

    def drain_near(i, _):
        for part in range(NEAR):
            near_copy(i, part).wait_send()
        for part in range(BACK):
            back_copy(i, part).wait_send()
        return 0

    def drain_chain(e, _):
        for part in range(CHAIN):
            chain_copy(e, part).wait_send()
        return 0

    lax.fori_loop(0, 2 * n, drain_near, 0)

    @pl.when(has_chain_out)
    def _():
        lax.fori_loop(0, events, drain_chain, 0)

    d_copy().wait_send()

    @pl.when(has_next)
    def _():
        halo_copy().wait_send()

    for d in range(1, head_size):
        square_copy(d).wait_recv()
    total_square = square_own[...]
    for d in range(1, head_size):
        total_square = total_square + square_in[d - 1]
    inverse = lax.rsqrt(total_square / (xs_ref.shape[1] * head_size) + norm_epsilon)
    inverse = jnp.broadcast_to(inverse[0:1, :], (LANES, rows)).T
    inverse_ref[...] = inverse
    for d in range(1, head_size):
        square_copy(d).wait_send()


def scale_kernel(gated, inverse_ref, gain_ref, out_hbm, out_ref, sem):
    chunks = gated.shape[0]
    inverse = jnp.concatenate([inverse_ref[...]] * (WIDE // LANES), axis=1)
    copies = []
    for c in range(chunks):
        lanes = slice(c * WIDE, (c + 1) * WIDE)
        out_ref[c] = (gated[c] * inverse * gain_ref[:, lanes]).astype(bf16)
        copies.append(pltpu.make_async_copy(out_ref.at[c], out_hbm.at[:, lanes], sem.at[c]))
        copies[-1].start()
    for copy in copies:
        copy.wait()


def solution(mesh):
    seq_size = mesh.shape["seq"]
    head_size = mesh.shape["head"]

    def per_device(
        xs, gate_z, b_in, c_in, dt, log_decay, d_skip, conv_x, conv_b, conv_c, gain, doc_lengths
    ):
        rows, width = xs.shape
        heads = dt.shape[1]
        groups = b_in.shape[1] // STATE
        chunks = width // WIDE
        blocks = rows // BLOCK
        per_chunk = WIDE // HEAD_DIM
        vmem = pltpu.VMEM
        dma = pltpu.SemaphoreType.DMA
        n = chunks // 4

        def states(count):
            return vmem((count, STATE, WIDE), bf16)

        gated, inverse = pl.pallas_call(
            functools.partial(kernel, seq_size, head_size),
            out_shape=(vmem((chunks, rows, WIDE), f32), vmem((rows, LANES), f32)),
            in_specs=[pl.BlockSpec(memory_space=pltpu.HBM)] * 11,
            out_specs=(pl.BlockSpec(memory_space=pltpu.VMEM),) * 2,
            scratch_shapes=[
                pltpu.SMEM(doc_lengths.shape, jnp.int32),
                vmem((rows, width), bf16),
                vmem((rows, width), bf16),
                vmem((rows, groups * STATE), bf16),
                vmem((rows, groups * STATE), bf16),
                vmem((heads, rows), f32),
                vmem((heads, rows), f32),
                vmem((1, heads), f32),
                vmem((4, width), f32),
                vmem((4, groups * STATE), f32),
                vmem((4, groups * STATE), f32),
                vmem((HALO, width), bf16),
                vmem((HALO, width // 4), bf16),
                vmem((HALO, width // 4), bf16),
                vmem((HALO, width), bf16),
                vmem((HALO, groups * STATE), bf16),
                vmem((HALO, groups * STATE), bf16),
                states(chunks),
                states(chunks),
                states(chunks),
                states(2 * n + 1),
                states(3 * n),
                states(3 * n),
                states(2 * n),
                states(2 * n + 1),
                vmem((16, LANES), bf16),
                vmem((16, LANES), bf16),
                vmem((3, rows, LANES), f32),
                vmem((chunks, rows, WIDE), bf16),
                vmem((chunks, rows, WIDE), bf16),
                vmem((groups, rows, STATE), bf16),
                vmem((groups, rows, STATE), bf16),
                vmem((groups, blocks, STATE, BLOCK), bf16),
                vmem((groups, blocks, BLOCK, BLOCK), f32),
                vmem((blocks, chunks, 8, BLOCK), f32),
                vmem((6, rows, LANES), bf16),
                vmem((chunks, LANES, WIDE), bf16),
                vmem((chunks, LANES, per_chunk * BLOCK), bf16),
                vmem((rows, LANES), f32),
                vmem((8, rows), f32),
                vmem((head_size - 1, 8, rows), f32),
                dma,
                dma,
                dma,
                dma,
                dma((2 * n, NEAR)),
                dma((2 * n, NEAR)),
                dma((3 * n, CHAIN)),
                dma((3 * n, CHAIN)),
                dma((2 * n, BACK)),
                dma((2 * n, BACK)),
                dma((head_size - 1,)),
                dma((head_size - 1,)),
                dma((12,)),
            ],
            compiler_params=pltpu.CompilerParams(
                collective_id=0, has_side_effects=True, vmem_limit_bytes=60_000_000
            ),
        )(
            doc_lengths,
            xs,
            gate_z,
            b_in,
            c_in,
            dt.T,
            log_decay.T,
            d_skip.reshape(1, -1),
            conv_x,
            conv_b,
            conv_c,
        )
        return pl.pallas_call(
            scale_kernel,
            out_shape=jax.ShapeDtypeStruct((rows, width), bf16),
            in_specs=[pl.BlockSpec(memory_space=pltpu.VMEM)] * 3,
            out_specs=pl.BlockSpec(memory_space=pltpu.HBM),
            scratch_shapes=[vmem((chunks, rows, WIDE), bf16), dma((chunks,))],
            compiler_params=pltpu.CompilerParams(vmem_limit_bytes=16_000_000),
        )(gated, inverse, gain.reshape(1, -1))

    whole = P("seq", "head")
    across = P(None, "head")
    return jax.shard_map(
        per_device,
        mesh=mesh,
        in_specs=(
            whole,
            whole,
            whole,
            whole,
            whole,
            whole,
            P("head"),
            across,
            across,
            across,
            P("head"),
            P(),
        ),
        out_specs=whole,
        check_vma=False,
    )
```

```python
import functools

import jax
import jax.numpy as jnp
from jax import lax
from jax.experimental import pallas as pl
from jax.experimental.pallas import tpu as pltpu
from jax.sharding import PartitionSpec as P

HEAD_DIM = 64
STATE = 128
BLOCK = 128
LANES = 128
WIDE = 256
HALO = 16
SUBS = 4
NEAR = 2
CHAIN = 4
BACK = 2
norm_epsilon = 1e-05

MESH = pl.DeviceIdType.MESH
f32 = jnp.float32
bf16 = jnp.bfloat16


def silu(v):
    return v / (1.0 + jnp.exp(-v))


def split(v):
    high = v.astype(bf16)
    rest = v - high.astype(f32)
    middle = rest.astype(bf16)
    low = (rest - middle.astype(f32)).astype(bf16)
    parts = [high.astype(f32), middle.astype(f32), low.astype(f32)]
    width = LANES - 3 * v.shape[1]
    if width:
        parts.append(jnp.zeros((v.shape[0], width), f32))
    return jnp.concatenate(parts, axis=1).astype(bf16)


def dot(a, b):
    return jnp.dot(a, b, preferred_element_type=f32)


def kernel(
    seq_size,
    head_size,
    lengths_hbm,
    xs_hbm,
    z_hbm,
    b_hbm,
    c_hbm,
    dt_hbm,
    decay_hbm,
    skip_hbm,
    conv_x_hbm,
    conv_b_hbm,
    conv_c_hbm,
    gated,
    inverse_ref,
    lengths_ref,
    xs_ref,
    z_ref,
    b_ref,
    c_ref,
    dt_ref,
    decay_ref,
    skip_ref,
    conv_x_ref,
    conv_b_ref,
    conv_c_ref,
    tail_x,
    halo_out,
    halo_in,
    halo_x,
    halo_b,
    halo_c,
    own_s,
    first_s,
    enter,
    near_in,
    chain_out,
    chain_in,
    back_out,
    back_in,
    d_own,
    d_pair,
    masks,
    x_conv,
    scaled,
    c_conv,
    b_conv,
    b_turned,
    score,
    cum_turned,
    packed,
    hot,
    cum_columns,
    carried,
    square,
    square_own,
    square_in,
    halo_send,
    halo_recv,
    d_send,
    d_recv,
    near_send,
    near_recv,
    chain_send,
    chain_recv,
    back_send,
    back_recv,
    square_send,
    square_recv,
    load_sem,
):
    rows = xs_ref.shape[0]
    heads = dt_ref.shape[0]
    groups = b_ref.shape[1] // STATE
    chunks = xs_ref.shape[1] // WIDE
    per_chunk = WIDE // HEAD_DIM
    blocks = rows // BLOCK
    docs = lengths_ref.shape[0]
    n = chunks // 4
    events = 3 * n
    k = lax.axis_index("seq")
    me = lax.axis_index("head")
    r = lax.rem(k, 2)
    hop = k // 2
    partner = k + 1 - 2 * r
    keep = 2 * n + r * n
    give = 3 * n - r * n
    even = r == 0
    has_prev = k > 0
    has_next = k + 1 < seq_size
    has_chain_in = k > 1
    has_chain_out = k + 2 < seq_size

    def work_chunk(p):
        c = jnp.where(p < 3 * n, p - n, keep + p - 3 * n)
        early = jnp.where(lax.rem(p, 2) == 0, give + p // 2, p // 2)
        return jnp.where(p < 2 * n, early, c)

    def event_chunk(e):
        c = jnp.where(e < 2 * n, keep + e - n, e - n)
        return jnp.where(e < n, e, c)

    def halo_copy():
        return pltpu.make_async_remote_copy(
            src_ref=halo_out,
            dst_ref=halo_in,
            send_sem=halo_send,
            recv_sem=halo_recv,
            device_id={"seq": k + 1},
            device_id_type=MESH,
        )

    def d_copy():
        return pltpu.make_async_remote_copy(
            src_ref=d_own,
            dst_ref=d_pair,
            send_sem=d_send,
            recv_sem=d_recv,
            device_id={"seq": partner},
            device_id_type=MESH,
        )

    def lines_of(part, parts=SUBS):
        return pl.ds(part * (STATE // parts), STATE // parts)

    def near_copy(i, part):
        source = jnp.where(i < n, give + i, i)
        return pltpu.make_async_remote_copy(
            src_ref=own_s.at[source, lines_of(part, NEAR)],
            dst_ref=near_in.at[i, lines_of(part, NEAR)],
            send_sem=near_send.at[i, part],
            recv_sem=near_recv.at[i, part],
            device_id={"seq": partner},
            device_id_type=MESH,
        )

    def chain_copy(e, part):
        return pltpu.make_async_remote_copy(
            src_ref=chain_out.at[e, lines_of(part, CHAIN)],
            dst_ref=chain_in.at[e, lines_of(part, CHAIN)],
            send_sem=chain_send.at[e, part],
            recv_sem=chain_recv.at[e, part],
            device_id={"seq": k + 2},
            device_id_type=MESH,
        )

    def back_copy(e, part):
        return pltpu.make_async_remote_copy(
            src_ref=back_out.at[e, lines_of(part, BACK)],
            dst_ref=back_in.at[e, lines_of(part, BACK)],
            send_sem=back_send.at[e, part],
            recv_sem=back_recv.at[e, part],
            device_id={"seq": partner},
            device_id_type=MESH,
        )

    def square_copy(d):
        return pltpu.make_async_remote_copy(
            src_ref=square_own,
            dst_ref=square_in.at[d - 1],
            send_sem=square_send.at[d - 1],
            recv_sem=square_recv.at[d - 1],
            device_id={"head": lax.rem(me + d, head_size)},
            device_id_type=MESH,
        )

    barrier = pltpu.get_barrier_semaphore()
    for step, there in ((-1, has_prev), (1, has_next), (-2, has_chain_in), (2, has_chain_out)):

        @pl.when(there)
        def _():
            pl.semaphore_signal(
                barrier, inc=1, device_id={"seq": k + step}, device_id_type=MESH
            )

    for d in range(1, head_size):
        pl.semaphore_signal(
            barrier,
            inc=1,
            device_id={"head": lax.rem(me + d, head_size)},
            device_id_type=MESH,
        )
    expected = head_size - 1
    for there in (has_prev, has_next, has_chain_in, has_chain_out):
        expected = expected + there.astype(jnp.int32)

    moves = (
        (xs_hbm.at[pl.ds(rows - HALO, HALO)], tail_x),
        (lengths_hbm, lengths_ref),
        (b_hbm, b_ref),
        (c_hbm, c_ref),
        (decay_hbm, decay_ref),
        (dt_hbm, dt_ref),
        (xs_hbm, xs_ref),
        (conv_b_hbm, conv_b_ref),
        (conv_x_hbm, conv_x_ref),
        (conv_c_hbm, conv_c_ref),
        (skip_hbm, skip_ref),
        (z_hbm, z_ref),
    )
    loads = [
        pltpu.make_async_copy(source, target, load_sem.at[i])
        for i, (source, target) in enumerate(moves)
    ]
    for load in loads:
        load.start()
    (
        load_tail, load_lengths, load_b, load_c, load_decay, load_dt, load_x,
        load_conv_b, load_conv_x, load_conv_c, load_skip, load_z,
    ) = loads

    quarter = xs_ref.shape[1] // 4
    b_width = b_ref.shape[1]
    halo_row = lax.broadcasted_iota(jnp.int32, (HALO, quarter), 0) // 3

    load_tail.wait()
    parcel = jnp.zeros((HALO, quarter), f32)
    for q in range(4):
        piece = tail_x[:, q * quarter : (q + 1) * quarter].astype(f32)
        parcel = jnp.where(halo_row == q, pltpu.roll(piece, 3 * q + 3, 0), parcel)
    load_b.wait()
    load_c.wait()
    pieces = [b_ref[rows - HALO :, :].astype(f32), c_ref[rows - HALO :, :].astype(f32)]
    if quarter > 2 * b_width:
        pieces.append(jnp.zeros((HALO, quarter - 2 * b_width), f32))
    piece = pltpu.roll(jnp.concatenate(pieces, axis=1), 15, 0)
    halo_out[...] = jnp.where(halo_row == 4, piece, parcel).astype(bf16)

    load_lengths.wait()
    starts = []
    running = jnp.int32(0)
    for j in range(docs):
        starts.append(running)
        running = running + lengths_ref[j]

    def start_at(position):
        found = jnp.full_like(position, -1)
        for start in starts:
            found = jnp.where(start <= position, start, found)
        return found

    base = k * rows
    column = base + lax.broadcasted_iota(jnp.int32, (rows, LANES), 0)
    own_start = start_at(column)
    for d in range(1, 4):
        masks[d - 1] = jnp.where(column - own_start >= d, 1.0, 0.0).astype(f32)
    lasts = [start_at(base + (b + 1) * BLOCK - 1) for b in range(blocks)]
    load_decay.wait()
    load_dt.wait()
    load_skip.wait()

    def turn(v):
        wide = jnp.concatenate([v, jnp.zeros((LANES - heads, rows), f32)], axis=0)
        return wide.T[:, :heads]

    dt_rows = turn(dt_ref[...])
    decay_rows = turn(decay_ref[...])
    t_index = lax.broadcasted_iota(jnp.int32, (BLOCK, BLOCK), 0)
    s_index = lax.broadcasted_iota(jnp.int32, (BLOCK, BLOCK), 1)
    lower = jnp.where(s_index <= t_index, 1.0, 0.0).astype(bf16)
    ends, enters, cums = [], [], []
    for b in range(blocks):
        here = slice(b * BLOCK, (b + 1) * BLOCK)
        parts = dot(lower, split(decay_rows[here, :]))
        cum = parts[:, :heads] + parts[:, heads : 2 * heads] + parts[:, 2 * heads : 3 * heads]
        begun = own_start[here, :heads]
        ends.append(jnp.where(begun == lasts[b], jnp.exp(cum[BLOCK - 1 :, :] - cum), 0.0))
        enters.append(jnp.where(begun < base + b * BLOCK, jnp.exp(cum), 0.0))
        cums.append(cum)
    carry0 = enters[0][BLOCK - 1 :, :]
    carry1 = enters[1][BLOCK - 1 :, :]
    d_own[...] = split(jnp.broadcast_to(carry0 * carry1, (16, heads)))
    packed[0] = split(dt_rows)
    packed[1] = split(jnp.concatenate(ends, axis=0))
    few = split(
        jnp.concatenate(
            [jnp.broadcast_to(carry1, (8, heads)), jnp.broadcast_to(skip_ref[...], (8, heads))], 0
        )
    )
    packed[5, 0:16, :] = few

    def spread(c, width):
        row = lax.broadcasted_iota(jnp.int32, (LANES, per_chunk * width), 0)
        lane = lax.broadcasted_iota(jnp.int32, (LANES, per_chunk * width), 1)
        wanted = c * per_chunk + lane // width
        hit = (row == wanted) | (row == wanted + heads) | (row == wanted + 2 * heads)
        return jnp.where(hit, 1.0, 0.0).astype(bf16)

    def convolve(x, weight):
        x = x.astype(f32)
        total = weight[3:4, :] * x
        for d in range(1, 4):
            total = total + weight[3 - d : 4 - d, :] * (pltpu.roll(x, d, 0) * masks[d - 1])
        return silu(total).astype(bf16)

    def convolve_top(x, halo, weight):
        window = jnp.concatenate([halo.astype(f32), x.astype(f32)], axis=0)
        total = weight[3:4, :] * window[HALO:]
        for d in range(1, 4):
            shifted = window[HALO - d : 2 * HALO - d] * masks[d - 1, 0:HALO, :]
            total = total + weight[3 - d : 4 - d, :] * shifted
        return silu(total).astype(bf16)

    load_conv_b.wait()
    for g in range(groups):
        lanes = slice(g * STATE, (g + 1) * STATE)
        b_conv[g] = convolve(b_ref[:, lanes], conv_b_ref[:, lanes])
        b_turned[g, 1] = b_conv[g, BLOCK:, :].astype(f32).T.astype(bf16)

    load_x.wait()
    load_conv_x.wait()
    pl.semaphore_wait(barrier, expected)

    @pl.when(has_next)
    def _():
        halo_copy().start()

    d_copy().start()

    def lanes_of(c, half):
        return pl.ds(pl.multiple_of(c * WIDE + half * LANES, LANES), LANES)

    def conv_step(p, _):
        c = work_chunk(p)
        for half in range(WIDE // LANES):
            lanes = lanes_of(c, half)
            x_conv[c, :, half * LANES : (half + 1) * LANES] = convolve(
                xs_ref[:, lanes], conv_x_ref[:, lanes]
            )
        return 0

    lax.fori_loop(0, 3 * n, conv_step, 0)

    def hot_step(c, _):
        hot[c] = spread(c, HEAD_DIM)
        return 0

    lax.fori_loop(0, chunks, hot_step, 0)

    @pl.when(k < 2)
    def _():
        chain_in[...] = jnp.zeros_like(chain_in)

    near_in[2 * n] = jnp.zeros_like(near_in[2 * n])
    back_in[2 * n] = jnp.zeros_like(back_in[2 * n])
    for i in range(n):
        enter[give + i] = jnp.zeros_like(enter[give + i])

    @pl.when(k == 0)
    def _():
        halo_in[...] = jnp.zeros_like(halo_in)

    @pl.when(has_prev)
    def _():
        halo_copy().wait_recv()

    arrived = halo_in[...].astype(f32)
    for q in range(4):
        halo_x[:, q * quarter : (q + 1) * quarter] = pltpu.roll(
            arrived, HALO - 3 - 3 * q, 0
        ).astype(bf16)
    piece = pltpu.roll(arrived, 1, 0)
    halo_b[...] = piece[:, :b_width].astype(bf16)
    halo_c[...] = piece[:, b_width : 2 * b_width].astype(bf16)

    for g in range(groups):
        lanes = slice(g * STATE, (g + 1) * STATE)
        b_conv[g, 0:HALO, :] = convolve_top(b_ref[0:HALO, lanes], halo_b[:, lanes], conv_b_ref[:, lanes])
        b_turned[g, 0] = b_conv[g, :BLOCK, :].astype(f32).T.astype(bf16)

    def state_step(p, _):
        c = work_chunk(p)
        g = c // (chunks // groups)
        for half in range(WIDE // LANES):
            lanes = lanes_of(c, half)
            x_conv[c, 0:HALO, half * LANES : (half + 1) * LANES] = convolve_top(
                xs_ref[0:HALO, lanes], halo_x[:, lanes], conv_x_ref[:, lanes]
            )
        x = x_conv[c]
        one_hot = hot[c]
        product = (dot(packed[0], one_hot) * x.astype(f32)).astype(bf16)
        scaled[c] = product
        weighted = (dot(packed[1], one_hot) * product.astype(f32)).astype(bf16)
        state0 = dot(b_turned[g, 0], weighted[:BLOCK])
        state1 = dot(b_turned[g, 1], weighted[BLOCK:])
        few = dot(packed[5, 0:16, :], one_hot)
        first_s[c] = state0.astype(bf16)
        state = (few[0:1, :] * state0 + state1).astype(bf16)
        own_s[c] = state

        @pl.when((p < 3 * n) & ((p >= 2 * n) | (lax.rem(p, 2) == 0)))
        def _():
            for part in range(NEAR):
                near_copy(jnp.where(p < 2 * n, p // 2, p - n), part).start()

        @pl.when(p == 0)
        def _():
            d_copy().wait_recv()

        @pl.when((p < 2 * n) & (lax.rem(p, 2) != 0) & (hop == 0) & has_chain_out)
        def _():
            decay_pair = dot(d_pair[...], one_hot)[0:1, :]
            wide = state.astype(f32)
            chain_out[p // 2] = jnp.where(even, decay_pair * wide, wide).astype(bf16)
            for part in range(CHAIN):
                chain_copy(p // 2, part).start()

        return 0

    lax.fori_loop(0, 3 * n, state_step, 0)
    lax.fori_loop(3 * n, chunks, conv_step, 0)
    lax.fori_loop(3 * n, chunks, state_step, 0)
    load_conv_c.wait()

    packed[2] = split(jnp.concatenate([enters[0], enters[1] * carry0], axis=0))
    packed[3] = split(jnp.concatenate([enters[0], enters[1]], axis=0))
    wide = jnp.concatenate(cums, axis=0)
    wide = jnp.concatenate([wide, jnp.zeros((rows, LANES - heads), f32)], axis=1)
    for c in range(chunks):
        shifted = pltpu.roll(wide, LANES - c * per_chunk, 1) if c else wide
        cum_columns[c] = shifted
    for b in range(blocks):
        wide = jnp.concatenate([cums[b], jnp.zeros((BLOCK, LANES - heads), f32)], axis=1)
        turned = wide.T
        for c in range(chunks):
            cum_turned[b, c, 0:per_chunk, :] = turned[c * per_chunk : (c + 1) * per_chunk, :]

    for g in range(groups):
        lanes = slice(g * STATE, (g + 1) * STATE)
        c_conv[g] = convolve(c_ref[:, lanes], conv_c_ref[:, lanes])
        c_conv[g, 0:HALO, :] = convolve_top(c_ref[0:HALO, lanes], halo_c[:, lanes], conv_c_ref[:, lanes])

    for b in range(blocks):
        here = slice(b * BLOCK, (b + 1) * BLOCK)
        allowed = (base + b * BLOCK + s_index >= own_start[here, :]) & (s_index <= t_index)
        for g in range(groups):
            value = lax.dot_general(
                c_conv[g, here, :],
                b_conv[g, here, :],
                (((1,), (1,)), ((), ())),
                preferred_element_type=f32,
            )
            score[g, b] = jnp.where(allowed, value, 0.0)

    square[...] = jnp.zeros_like(square)
    load_z.wait()

    def local_step(c, _):
        g = c // (chunks // groups)
        one_hot = hot[c]
        lane = lax.broadcasted_iota(jnp.int32, (BLOCK, LANES), 1)
        locals_ = []
        for b in range(blocks):
            here = slice(b * BLOCK, (b + 1) * BLOCK)
            columns = cum_columns[c, here, :]
            damped = score[g, b]
            pieces = []
            for j in range(per_chunk // 2):
                mixes = []
                for i in (2 * j, 2 * j + 1):
                    across = jnp.broadcast_to(columns[:, i : i + 1], (BLOCK, BLOCK))
                    gap = across - cum_turned[b, c, i : i + 1, :]
                    mixes.append((damped * jnp.exp(jnp.minimum(gap, 0.0))).astype(bf16))
                values = scaled[c, here, j * LANES : (j + 1) * LANES]
                zero = jnp.zeros_like(values)
                left = jnp.where(lane < HEAD_DIM, values, zero)
                right = jnp.where(lane < HEAD_DIM, zero, values)
                pieces.append(
                    dot(jnp.concatenate(mixes, axis=1), jnp.concatenate([left, right], axis=0))
                )
            locals_.append(jnp.concatenate(pieces, axis=1))
        inner = dot(packed[3, BLOCK:, :], one_hot) * dot(c_conv[g, BLOCK:, :], first_s[c])
        few = dot(packed[5, 0:16, :], one_hot)
        total = jnp.concatenate([locals_[0], locals_[1] + inner], axis=0)
        lanes = pl.ds(pl.multiple_of(c * WIDE, WIDE), WIDE)
        gate = silu(z_ref[:, lanes].astype(f32))
        gated[c] = (total + few[8:9, :] * x_conv[c].astype(f32)) * gate
        carried[c] = dot(packed[2], one_hot) * gate
        return 0

    def chain_event(e):
        c = event_chunk(e)
        one_hot = hot[c]
        decay_own = dot(d_own[...], one_hot)[0:1, :]
        decay_pair = dot(d_pair[...], one_hot)[0:1, :]
        decay_first = jnp.where(even, decay_own, decay_pair)
        decay_second = jnp.where(even, decay_pair, decay_own)
        near = jnp.where(e < n, 2 * n, e - n)
        for part in range(SUBS):
            lines = lines_of(part)

            if part % (SUBS // NEAR) == 0:

                @pl.when(e >= n)
                def _():
                    near_copy(e - n, part * NEAR // SUBS).wait_recv()

            if part % (SUBS // CHAIN) == 0:

                @pl.when(has_chain_in)
                def _():
                    chain_copy(e, part * CHAIN // SUBS).wait_recv()

            own = own_s[c, lines].astype(f32)
            other = near_in[near, lines].astype(f32)
            before = chain_in[e, lines].astype(f32)
            middle = jnp.where(even, own, other) + decay_first * before
            after = jnp.where(even, other, own) + decay_second * middle

            @pl.when(has_chain_out & ((e >= n) | has_chain_in))
            def _():
                chain_out[e, lines] = after.astype(bf16)
                if (part + 1) % (SUBS // CHAIN) == 0:
                    chain_copy(e, part * CHAIN // SUBS).start()

            @pl.when(e < 2 * n)
            def _():
                back_out[e, lines] = jnp.where(even, middle, before).astype(bf16)

                if (part + 1) % (SUBS // BACK) == 0:

                    @pl.when(has_chain_in)
                    def _():
                        back_copy(e, part * BACK // SUBS).start()

            enter[c, lines] = jnp.where(even, before, middle).astype(bf16)

        @pl.when((e == events - 1) & (hop == 0))
        def _():
            for other_e in range(2 * n):
                for part in range(BACK):
                    back_copy(other_e, part).start()

    def last_step(f, _):
        t = f - 2 * n
        late = jnp.where(lax.rem(t, 2) == 0, n + t // 2, give + t // 2)
        c = jnp.where(f < n, keep + f, jnp.where(f < 2 * n, f - n, late))
        added = (f >= n) & ((f < 2 * n) | (lax.rem(f, 2) == 1))
        slot = jnp.where(f < 2 * n, f - n, n + t // 2)
        slot = jnp.where(added, slot, 2 * n)
        g = c // (chunks // groups)

        @pl.when(added)
        def _():
            for part in range(BACK):
                back_copy(slot, part).wait_recv()

        entering = (enter[c].astype(f32) + back_in[slot].astype(f32)).astype(bf16)
        value = gated[c] + carried[c] * dot(c_conv[g], entering)
        gated[c] = value
        power = value * value
        square[...] += power[:, :LANES] + power[:, LANES:]
        return 0

    def locals_before(e):
        count = jnp.where(hop == 0, e - n, chunks)
        count = jnp.where(hop == 1, e, count)
        count = jnp.where(hop == 2, e + 3 * n // 2, count)
        count = jnp.where(e >= events, chunks, count)
        return jnp.clip(jnp.where(e < 0, 0, count), 0, chunks)

    def lasts_after(e):
        count = jnp.where(e < 2 * n - 1, 0, 2 * (e + 1) - 2 * n)
        count = jnp.where(has_chain_out | (locals_before(e) < chunks), 0, count)
        return jnp.where(e >= events, chunks, jnp.minimum(count, chunks))

    def outer(e, _):
        lax.fori_loop(locals_before(e - 1), locals_before(e), local_step, 0)

        @pl.when(e < events)
        def _():
            chain_event(e)

        lax.fori_loop(lasts_after(e - 1), lasts_after(e), last_step, 0)
        return 0

    lax.fori_loop(0, events + 1, outer, 0)

    own_square = jnp.sum(square[...].T, axis=0, keepdims=True)
    square_own[...] = jnp.broadcast_to(own_square, square_own.shape)
    for d in range(1, head_size):
        square_copy(d).start()

    def drain_near(i, _):
        for part in range(NEAR):
            near_copy(i, part).wait_send()
        for part in range(BACK):
            back_copy(i, part).wait_send()
        return 0

    def drain_chain(e, _):
        for part in range(CHAIN):
            chain_copy(e, part).wait_send()
        return 0

    lax.fori_loop(0, 2 * n, drain_near, 0)

    @pl.when(has_chain_out)
    def _():
        lax.fori_loop(0, events, drain_chain, 0)

    d_copy().wait_send()

    @pl.when(has_next)
    def _():
        halo_copy().wait_send()

    for d in range(1, head_size):
        square_copy(d).wait_recv()
    total_square = square_own[...]
    for d in range(1, head_size):
        total_square = total_square + square_in[d - 1]
    inverse = lax.rsqrt(total_square / (xs_ref.shape[1] * head_size) + norm_epsilon)
    inverse = jnp.broadcast_to(inverse[0:1, :], (LANES, rows)).T
    inverse_ref[...] = inverse
    for d in range(1, head_size):
        square_copy(d).wait_send()


def scale_kernel(gated, inverse_ref, gain_ref, out_hbm, out_ref, sem):
    chunks = gated.shape[0]
    inverse = jnp.concatenate([inverse_ref[...]] * (WIDE // LANES), axis=1)
    copies = []
    for c in range(chunks):
        lanes = slice(c * WIDE, (c + 1) * WIDE)
        out_ref[c] = (gated[c] * inverse * gain_ref[:, lanes]).astype(bf16)
        copies.append(pltpu.make_async_copy(out_ref.at[c], out_hbm.at[:, lanes], sem.at[c]))
        copies[-1].start()
    for copy in copies:
        copy.wait()


def solution(mesh):
    seq_size = mesh.shape["seq"]
    head_size = mesh.shape["head"]

    def per_device(
        xs, gate_z, b_in, c_in, dt, log_decay, d_skip, conv_x, conv_b, conv_c, gain, doc_lengths
    ):
        rows, width = xs.shape
        heads = dt.shape[1]
        groups = b_in.shape[1] // STATE
        chunks = width // WIDE
        blocks = rows // BLOCK
        per_chunk = WIDE // HEAD_DIM
        vmem = pltpu.VMEM
        dma = pltpu.SemaphoreType.DMA
        n = chunks // 4

        def states(count):
            return vmem((count, STATE, WIDE), bf16)

        gated, inverse = pl.pallas_call(
            functools.partial(kernel, seq_size, head_size),
            out_shape=(vmem((chunks, rows, WIDE), f32), vmem((rows, LANES), f32)),
            in_specs=[pl.BlockSpec(memory_space=pltpu.HBM)] * 11,
            out_specs=(pl.BlockSpec(memory_space=pltpu.VMEM),) * 2,
            scratch_shapes=[
                pltpu.SMEM(doc_lengths.shape, jnp.int32),
                vmem((rows, width), bf16),
                vmem((rows, width), bf16),
                vmem((rows, groups * STATE), bf16),
                vmem((rows, groups * STATE), bf16),
                vmem((heads, rows), f32),
                vmem((heads, rows), f32),
                vmem((1, heads), f32),
                vmem((4, width), f32),
                vmem((4, groups * STATE), f32),
                vmem((4, groups * STATE), f32),
                vmem((HALO, width), bf16),
                vmem((HALO, width // 4), bf16),
                vmem((HALO, width // 4), bf16),
                vmem((HALO, width), bf16),
                vmem((HALO, groups * STATE), bf16),
                vmem((HALO, groups * STATE), bf16),
                states(chunks),
                states(chunks),
                states(chunks),
                states(2 * n + 1),
                states(3 * n),
                states(3 * n),
                states(2 * n),
                states(2 * n + 1),
                vmem((16, LANES), bf16),
                vmem((16, LANES), bf16),
                vmem((3, rows, LANES), f32),
                vmem((chunks, rows, WIDE), bf16),
                vmem((chunks, rows, WIDE), bf16),
                vmem((groups, rows, STATE), bf16),
                vmem((groups, rows, STATE), bf16),
                vmem((groups, blocks, STATE, BLOCK), bf16),
                vmem((groups, blocks, BLOCK, BLOCK), f32),
                vmem((blocks, chunks, 8, BLOCK), f32),
                vmem((6, rows, LANES), bf16),
                vmem((chunks, LANES, WIDE), bf16),
                vmem((chunks, rows, LANES), f32),
                vmem((chunks, rows, WIDE), f32),
                vmem((rows, LANES), f32),
                vmem((8, rows), f32),
                vmem((head_size - 1, 8, rows), f32),
                dma,
                dma,
                dma,
                dma,
                dma((2 * n, NEAR)),
                dma((2 * n, NEAR)),
                dma((3 * n, CHAIN)),
                dma((3 * n, CHAIN)),
                dma((2 * n, BACK)),
                dma((2 * n, BACK)),
                dma((head_size - 1,)),
                dma((head_size - 1,)),
                dma((12,)),
            ],
            compiler_params=pltpu.CompilerParams(
                collective_id=0, has_side_effects=True, vmem_limit_bytes=60_000_000
            ),
        )(
            doc_lengths,
            xs,
            gate_z,
            b_in,
            c_in,
            dt.T,
            log_decay.T,
            d_skip.reshape(1, -1),
            conv_x,
            conv_b,
            conv_c,
        )
        return pl.pallas_call(
            scale_kernel,
            out_shape=jax.ShapeDtypeStruct((rows, width), bf16),
            in_specs=[pl.BlockSpec(memory_space=pltpu.VMEM)] * 3,
            out_specs=pl.BlockSpec(memory_space=pltpu.HBM),
            scratch_shapes=[vmem((chunks, rows, WIDE), bf16), dma((chunks,))],
            compiler_params=pltpu.CompilerParams(vmem_limit_bytes=16_000_000),
        )(gated, inverse, gain.reshape(1, -1))

    whole = P("seq", "head")
    across = P(None, "head")
    return jax.shard_map(
        per_device,
        mesh=mesh,
        in_specs=(
            whole,
            whole,
            whole,
            whole,
            whole,
            whole,
            P("head"),
            across,
            across,
            across,
            P("head"),
            P(),
        ),
        out_specs=whole,
        check_vma=False,
    )
```

```python
import functools

import jax
import jax.numpy as jnp
from jax import lax
from jax.experimental import pallas as pl
from jax.experimental.pallas import tpu as pltpu
from jax.sharding import PartitionSpec as P

HEAD_DIM = 64
STATE = 128
BLOCK = 128
LANES = 128
WIDE = 256
HALO = 16
SUBS = 4
NEAR = 2
CHAIN = 4
BACK = 2
norm_epsilon = 1e-05

MESH = pl.DeviceIdType.MESH
f32 = jnp.float32
bf16 = jnp.bfloat16


def silu(v):
    return v / (1.0 + jnp.exp(-v))


def split(v):
    high = v.astype(bf16)
    rest = v - high.astype(f32)
    middle = rest.astype(bf16)
    low = (rest - middle.astype(f32)).astype(bf16)
    parts = [high.astype(f32), middle.astype(f32), low.astype(f32)]
    width = LANES - 3 * v.shape[1]
    if width:
        parts.append(jnp.zeros((v.shape[0], width), f32))
    return jnp.concatenate(parts, axis=1).astype(bf16)


def dot(a, b):
    return jnp.dot(a, b, preferred_element_type=f32)


def kernel(
    seq_size,
    head_size,
    lengths_hbm,
    xs_hbm,
    z_hbm,
    b_hbm,
    c_hbm,
    dt_hbm,
    decay_hbm,
    skip_hbm,
    conv_x_hbm,
    conv_b_hbm,
    conv_c_hbm,
    gated,
    inverse_ref,
    lengths_ref,
    xs_ref,
    z_ref,
    b_ref,
    c_ref,
    dt_ref,
    decay_ref,
    skip_ref,
    conv_x_ref,
    conv_b_ref,
    conv_c_ref,
    tail_x,
    halo_out,
    halo_in,
    halo_x,
    halo_b,
    halo_c,
    own_s,
    first_s,
    enter,
    near_in,
    chain_out,
    chain_in,
    back_out,
    back_in,
    d_own,
    d_pair,
    masks,
    x_conv,
    scaled,
    c_conv,
    b_conv,
    b_turned,
    score,
    cum_turned,
    packed,
    hot,
    cum_columns,
    carried,
    square,
    square_own,
    square_in,
    halo_send,
    halo_recv,
    d_send,
    d_recv,
    near_send,
    near_recv,
    chain_send,
    chain_recv,
    back_send,
    back_recv,
    square_send,
    square_recv,
    load_sem,
):
    rows = xs_ref.shape[0]
    heads = dt_ref.shape[0]
    groups = b_ref.shape[1] // STATE
    chunks = xs_ref.shape[1] // WIDE
    per_chunk = WIDE // HEAD_DIM
    blocks = rows // BLOCK
    docs = lengths_ref.shape[0]
    n = chunks // 4
    events = 3 * n
    k = lax.axis_index("seq")
    me = lax.axis_index("head")
    r = lax.rem(k, 2)
    hop = k // 2
    partner = k + 1 - 2 * r
    keep = 2 * n + r * n
    give = 3 * n - r * n
    even = r == 0
    has_prev = k > 0
    has_next = k + 1 < seq_size
    has_chain_in = k > 1
    has_chain_out = k + 2 < seq_size

    def work_chunk(p):
        c = jnp.where(p < 3 * n, p - n, keep + p - 3 * n)
        early = jnp.where(lax.rem(p, 2) == 0, give + p // 2, p // 2)
        return jnp.where(p < 2 * n, early, c)

    def event_chunk(e):
        c = jnp.where(e < 2 * n, keep + e - n, e - n)
        return jnp.where(e < n, e, c)

    def halo_copy():
        return pltpu.make_async_remote_copy(
            src_ref=halo_out,
            dst_ref=halo_in,
            send_sem=halo_send,
            recv_sem=halo_recv,
            device_id={"seq": k + 1},
            device_id_type=MESH,
        )

    def d_copy():
        return pltpu.make_async_remote_copy(
            src_ref=d_own,
            dst_ref=d_pair,
            send_sem=d_send,
            recv_sem=d_recv,
            device_id={"seq": partner},
            device_id_type=MESH,
        )

    def lines_of(part, parts=SUBS):
        return pl.ds(part * (STATE // parts), STATE // parts)

    def near_copy(i, part):
        source = jnp.where(i < n, give + i, i)
        return pltpu.make_async_remote_copy(
            src_ref=own_s.at[source, lines_of(part, NEAR)],
            dst_ref=near_in.at[i, lines_of(part, NEAR)],
            send_sem=near_send.at[i, part],
            recv_sem=near_recv.at[i, part],
            device_id={"seq": partner},
            device_id_type=MESH,
        )

    def chain_copy(e, part):
        return pltpu.make_async_remote_copy(
            src_ref=chain_out.at[e, lines_of(part, CHAIN)],
            dst_ref=chain_in.at[e, lines_of(part, CHAIN)],
            send_sem=chain_send.at[e, part],
            recv_sem=chain_recv.at[e, part],
            device_id={"seq": k + 2},
            device_id_type=MESH,
        )

    def back_copy(e, part):
        return pltpu.make_async_remote_copy(
            src_ref=back_out.at[e, lines_of(part, BACK)],
            dst_ref=back_in.at[e, lines_of(part, BACK)],
            send_sem=back_send.at[e, part],
            recv_sem=back_recv.at[e, part],
            device_id={"seq": partner},
            device_id_type=MESH,
        )

    def square_copy(d):
        return pltpu.make_async_remote_copy(
            src_ref=square_own,
            dst_ref=square_in.at[d - 1],
            send_sem=square_send.at[d - 1],
            recv_sem=square_recv.at[d - 1],
            device_id={"head": lax.rem(me + d, head_size)},
            device_id_type=MESH,
        )

    barrier = pltpu.get_barrier_semaphore()
    for step, there in ((-1, has_prev), (1, has_next), (-2, has_chain_in), (2, has_chain_out)):

        @pl.when(there)
        def _():
            pl.semaphore_signal(
                barrier, inc=1, device_id={"seq": k + step}, device_id_type=MESH
            )

    for d in range(1, head_size):
        pl.semaphore_signal(
            barrier,
            inc=1,
            device_id={"head": lax.rem(me + d, head_size)},
            device_id_type=MESH,
        )
    expected = head_size - 1
    for there in (has_prev, has_next, has_chain_in, has_chain_out):
        expected = expected + there.astype(jnp.int32)

    moves = (
        (xs_hbm.at[pl.ds(rows - HALO, HALO)], tail_x),
        (lengths_hbm, lengths_ref),
        (b_hbm, b_ref),
        (c_hbm, c_ref),
        (decay_hbm, decay_ref),
        (dt_hbm, dt_ref),
        (xs_hbm, xs_ref),
        (conv_b_hbm, conv_b_ref),
        (conv_x_hbm, conv_x_ref),
        (conv_c_hbm, conv_c_ref),
        (skip_hbm, skip_ref),
        (z_hbm, z_ref),
    )
    loads = [
        pltpu.make_async_copy(source, target, load_sem.at[i])
        for i, (source, target) in enumerate(moves)
    ]
    for load in loads:
        load.start()
    (
        load_tail, load_lengths, load_b, load_c, load_decay, load_dt, load_x,
        load_conv_b, load_conv_x, load_conv_c, load_skip, load_z,
    ) = loads

    quarter = xs_ref.shape[1] // 4
    b_width = b_ref.shape[1]
    halo_row = lax.broadcasted_iota(jnp.int32, (HALO, quarter), 0) // 3

    load_tail.wait()
    parcel = jnp.zeros((HALO, quarter), f32)
    for q in range(4):
        piece = tail_x[:, q * quarter : (q + 1) * quarter].astype(f32)
        parcel = jnp.where(halo_row == q, pltpu.roll(piece, 3 * q + 3, 0), parcel)
    load_b.wait()
    load_c.wait()
    pieces = [b_ref[rows - HALO :, :].astype(f32), c_ref[rows - HALO :, :].astype(f32)]
    if quarter > 2 * b_width:
        pieces.append(jnp.zeros((HALO, quarter - 2 * b_width), f32))
    piece = pltpu.roll(jnp.concatenate(pieces, axis=1), 15, 0)
    halo_out[...] = jnp.where(halo_row == 4, piece, parcel).astype(bf16)

    load_lengths.wait()
    starts = []
    running = jnp.int32(0)
    for j in range(docs):
        starts.append(running)
        running = running + lengths_ref[j]

    def start_at(position):
        found = jnp.full_like(position, -1)
        for start in starts:
            found = jnp.where(start <= position, start, found)
        return found

    base = k * rows
    column = base + lax.broadcasted_iota(jnp.int32, (rows, LANES), 0)
    own_start = start_at(column)
    for d in range(1, 4):
        masks[d - 1] = jnp.where(column - own_start >= d, 1.0, 0.0).astype(f32)
    lasts = [start_at(base + (b + 1) * BLOCK - 1) for b in range(blocks)]
    load_decay.wait()
    load_dt.wait()
    load_skip.wait()

    def turn(v):
        wide = jnp.concatenate([v, jnp.zeros((LANES - heads, rows), f32)], axis=0)
        return wide.T[:, :heads]

    dt_rows = turn(dt_ref[...])
    decay_rows = turn(decay_ref[...])
    t_index = lax.broadcasted_iota(jnp.int32, (BLOCK, BLOCK), 0)
    s_index = lax.broadcasted_iota(jnp.int32, (BLOCK, BLOCK), 1)
    lower = jnp.where(s_index <= t_index, 1.0, 0.0).astype(bf16)
    ends, enters, cums = [], [], []
    for b in range(blocks):
        here = slice(b * BLOCK, (b + 1) * BLOCK)
        parts = dot(lower, split(decay_rows[here, :]))
        cum = parts[:, :heads] + parts[:, heads : 2 * heads] + parts[:, 2 * heads : 3 * heads]
        begun = own_start[here, :heads]
        ends.append(jnp.where(begun == lasts[b], jnp.exp(cum[BLOCK - 1 :, :] - cum), 0.0))
        enters.append(jnp.where(begun < base + b * BLOCK, jnp.exp(cum), 0.0))
        cums.append(cum)
    carry0 = enters[0][BLOCK - 1 :, :]
    carry1 = enters[1][BLOCK - 1 :, :]
    d_own[...] = split(jnp.broadcast_to(carry0 * carry1, (16, heads)))
    packed[0] = split(dt_rows)
    packed[1] = split(jnp.concatenate(ends, axis=0))
    few = split(
        jnp.concatenate(
            [jnp.broadcast_to(carry1, (8, heads)), jnp.broadcast_to(skip_ref[...], (8, heads))], 0
        )
    )
    packed[5, 0:16, :] = few

    def spread(c, width):
        row = lax.broadcasted_iota(jnp.int32, (LANES, per_chunk * width), 0)
        lane = lax.broadcasted_iota(jnp.int32, (LANES, per_chunk * width), 1)
        wanted = c * per_chunk + lane // width
        hit = (row == wanted) | (row == wanted + heads) | (row == wanted + 2 * heads)
        return jnp.where(hit, 1.0, 0.0).astype(bf16)

    def convolve(x, weight):
        x = x.astype(f32)
        total = weight[3:4, :] * x
        for d in range(1, 4):
            total = total + weight[3 - d : 4 - d, :] * (pltpu.roll(x, d, 0) * masks[d - 1])
        return silu(total).astype(bf16)

    def convolve_top(x, halo, weight):
        window = jnp.concatenate([halo.astype(f32), x.astype(f32)], axis=0)
        total = weight[3:4, :] * window[HALO:]
        for d in range(1, 4):
            shifted = window[HALO - d : 2 * HALO - d] * masks[d - 1, 0:HALO, :]
            total = total + weight[3 - d : 4 - d, :] * shifted
        return silu(total).astype(bf16)

    load_conv_b.wait()
    for g in range(groups):
        lanes = slice(g * STATE, (g + 1) * STATE)
        b_conv[g] = convolve(b_ref[:, lanes], conv_b_ref[:, lanes])
        b_turned[g, 1] = b_conv[g, BLOCK:, :].astype(f32).T.astype(bf16)

    load_x.wait()
    load_conv_x.wait()
    pl.semaphore_wait(barrier, expected)

    @pl.when(has_next)
    def _():
        halo_copy().start()

    d_copy().start()

    def lanes_of(c, half):
        return pl.ds(pl.multiple_of(c * WIDE + half * LANES, LANES), LANES)

    def conv_step(p, _):
        c = work_chunk(p)
        for half in range(WIDE // LANES):
            lanes = lanes_of(c, half)
            x_conv[c, :, half * LANES : (half + 1) * LANES] = convolve(
                xs_ref[:, lanes], conv_x_ref[:, lanes]
            )
        return 0

    lax.fori_loop(0, chunks, conv_step, 0)

    def hot_step(c, _):
        hot[c] = spread(c, HEAD_DIM)
        return 0

    lax.fori_loop(0, chunks, hot_step, 0)

    @pl.when(k < 2)
    def _():
        chain_in[...] = jnp.zeros_like(chain_in)

    near_in[2 * n] = jnp.zeros_like(near_in[2 * n])
    back_in[2 * n] = jnp.zeros_like(back_in[2 * n])
    for i in range(n):
        enter[give + i] = jnp.zeros_like(enter[give + i])

    @pl.when(k == 0)
    def _():
        halo_in[...] = jnp.zeros_like(halo_in)

    @pl.when(has_prev)
    def _():
        halo_copy().wait_recv()

    arrived = halo_in[...].astype(f32)
    for q in range(4):
        halo_x[:, q * quarter : (q + 1) * quarter] = pltpu.roll(
            arrived, HALO - 3 - 3 * q, 0
        ).astype(bf16)
    piece = pltpu.roll(arrived, 1, 0)
    halo_b[...] = piece[:, :b_width].astype(bf16)
    halo_c[...] = piece[:, b_width : 2 * b_width].astype(bf16)

    for g in range(groups):
        lanes = slice(g * STATE, (g + 1) * STATE)
        b_conv[g, 0:HALO, :] = convolve_top(b_ref[0:HALO, lanes], halo_b[:, lanes], conv_b_ref[:, lanes])
        b_turned[g, 0] = b_conv[g, :BLOCK, :].astype(f32).T.astype(bf16)

    def state_step(p, _):
        c = work_chunk(p)
        g = c // (chunks // groups)
        for half in range(WIDE // LANES):
            lanes = lanes_of(c, half)
            x_conv[c, 0:HALO, half * LANES : (half + 1) * LANES] = convolve_top(
                xs_ref[0:HALO, lanes], halo_x[:, lanes], conv_x_ref[:, lanes]
            )
        x = x_conv[c]
        one_hot = hot[c]
        product = (dot(packed[0], one_hot) * x.astype(f32)).astype(bf16)
        scaled[c] = product
        weighted = (dot(packed[1], one_hot) * product.astype(f32)).astype(bf16)
        state0 = dot(b_turned[g, 0], weighted[:BLOCK])
        state1 = dot(b_turned[g, 1], weighted[BLOCK:])
        few = dot(packed[5, 0:16, :], one_hot)
        first_s[c] = state0.astype(bf16)
        state = (few[0:1, :] * state0 + state1).astype(bf16)
        own_s[c] = state

        @pl.when((p < 3 * n) & ((p >= 2 * n) | (lax.rem(p, 2) == 0)))
        def _():
            for part in range(NEAR):
                near_copy(jnp.where(p < 2 * n, p // 2, p - n), part).start()

        @pl.when(p == 0)
        def _():
            d_copy().wait_recv()

        @pl.when((p < 2 * n) & (lax.rem(p, 2) != 0) & (hop == 0) & has_chain_out)
        def _():
            decay_pair = dot(d_pair[...], one_hot)[0:1, :]
            wide = state.astype(f32)
            chain_out[p // 2] = jnp.where(even, decay_pair * wide, wide).astype(bf16)
            for part in range(CHAIN):
                chain_copy(p // 2, part).start()

        return 0

    lax.fori_loop(0, 3 * n, state_step, 0)
    lax.fori_loop(3 * n, chunks, state_step, 0)
    load_conv_c.wait()

    def prepare():
        packed[2] = split(jnp.concatenate([enters[0], enters[1] * carry0], axis=0))
        packed[3] = split(jnp.concatenate([enters[0], enters[1]], axis=0))
        wide = jnp.concatenate(cums, axis=0)
        wide = jnp.concatenate([wide, jnp.zeros((rows, LANES - heads), f32)], axis=1)
        for c in range(chunks):
            shifted = pltpu.roll(wide, LANES - c * per_chunk, 1) if c else wide
            cum_columns[c] = shifted
        for b in range(blocks):
            wide = jnp.concatenate([cums[b], jnp.zeros((BLOCK, LANES - heads), f32)], axis=1)
            turned = wide.T
            for c in range(chunks):
                cum_turned[b, c, 0:per_chunk, :] = turned[c * per_chunk : (c + 1) * per_chunk, :]

        for g in range(groups):
            lanes = slice(g * STATE, (g + 1) * STATE)
            c_conv[g] = convolve(c_ref[:, lanes], conv_c_ref[:, lanes])
            c_conv[g, 0:HALO, :] = convolve_top(c_ref[0:HALO, lanes], halo_c[:, lanes], conv_c_ref[:, lanes])

        for b in range(blocks):
            here = slice(b * BLOCK, (b + 1) * BLOCK)
            allowed = (base + b * BLOCK + s_index >= own_start[here, :]) & (s_index <= t_index)
            for g in range(groups):
                value = lax.dot_general(
                    c_conv[g, here, :],
                    b_conv[g, here, :],
                    (((1,), (1,)), ((), ())),
                    preferred_element_type=f32,
                )
                score[g, b] = jnp.where(allowed, value, 0.0)

    square[...] = jnp.zeros_like(square)
    load_z.wait()

    def local_step(c, _):
        g = c // (chunks // groups)
        one_hot = hot[c]
        lane = lax.broadcasted_iota(jnp.int32, (BLOCK, LANES), 1)
        locals_ = []
        for b in range(blocks):
            here = slice(b * BLOCK, (b + 1) * BLOCK)
            columns = cum_columns[c, here, :]
            damped = score[g, b]
            pieces = []
            for j in range(per_chunk // 2):
                mixes = []
                for i in (2 * j, 2 * j + 1):
                    across = jnp.broadcast_to(columns[:, i : i + 1], (BLOCK, BLOCK))
                    gap = across - cum_turned[b, c, i : i + 1, :]
                    mixes.append((damped * jnp.exp(jnp.minimum(gap, 0.0))).astype(bf16))
                values = scaled[c, here, j * LANES : (j + 1) * LANES]
                zero = jnp.zeros_like(values)
                left = jnp.where(lane < HEAD_DIM, values, zero)
                right = jnp.where(lane < HEAD_DIM, zero, values)
                pieces.append(
                    dot(jnp.concatenate(mixes, axis=1), jnp.concatenate([left, right], axis=0))
                )
            locals_.append(jnp.concatenate(pieces, axis=1))
        inner = dot(packed[3, BLOCK:, :], one_hot) * dot(c_conv[g, BLOCK:, :], first_s[c])
        few = dot(packed[5, 0:16, :], one_hot)
        total = jnp.concatenate([locals_[0], locals_[1] + inner], axis=0)
        lanes = pl.ds(pl.multiple_of(c * WIDE, WIDE), WIDE)
        gate = silu(z_ref[:, lanes].astype(f32))
        gated[c] = (total + few[8:9, :] * x_conv[c].astype(f32)) * gate
        carried[c] = dot(packed[2], one_hot) * gate
        return 0

    def chain_event(e):
        c = event_chunk(e)
        one_hot = hot[c]
        decay_own = dot(d_own[...], one_hot)[0:1, :]
        decay_pair = dot(d_pair[...], one_hot)[0:1, :]
        decay_first = jnp.where(even, decay_own, decay_pair)
        decay_second = jnp.where(even, decay_pair, decay_own)
        near = jnp.where(e < n, 2 * n, e - n)
        for part in range(SUBS):
            lines = lines_of(part)

            if part % (SUBS // NEAR) == 0:

                @pl.when(e >= n)
                def _():
                    near_copy(e - n, part * NEAR // SUBS).wait_recv()

            if part % (SUBS // CHAIN) == 0:

                @pl.when(has_chain_in)
                def _():
                    chain_copy(e, part * CHAIN // SUBS).wait_recv()

            own = own_s[c, lines].astype(f32)
            other = near_in[near, lines].astype(f32)
            before = chain_in[e, lines].astype(f32)
            middle = jnp.where(even, own, other) + decay_first * before
            after = jnp.where(even, other, own) + decay_second * middle

            @pl.when(has_chain_out & ((e >= n) | has_chain_in))
            def _():
                chain_out[e, lines] = after.astype(bf16)
                if (part + 1) % (SUBS // CHAIN) == 0:
                    chain_copy(e, part * CHAIN // SUBS).start()

            @pl.when(e < 2 * n)
            def _():
                back_out[e, lines] = jnp.where(even, middle, before).astype(bf16)

                if (part + 1) % (SUBS // BACK) == 0:

                    @pl.when(has_chain_in)
                    def _():
                        back_copy(e, part * BACK // SUBS).start()

            enter[c, lines] = jnp.where(even, before, middle).astype(bf16)

        @pl.when((e == events - 1) & (hop == 0))
        def _():
            for other_e in range(2 * n):
                for part in range(BACK):
                    back_copy(other_e, part).start()

    def last_step(f, _):
        t = f - 2 * n
        late = jnp.where(lax.rem(t, 2) == 0, n + t // 2, give + t // 2)
        c = jnp.where(f < n, keep + f, jnp.where(f < 2 * n, f - n, late))
        added = (f >= n) & ((f < 2 * n) | (lax.rem(f, 2) == 1))
        slot = jnp.where(f < 2 * n, f - n, n + t // 2)
        slot = jnp.where(added, slot, 2 * n)
        g = c // (chunks // groups)

        @pl.when(added)
        def _():
            for part in range(BACK):
                back_copy(slot, part).wait_recv()

        entering = (enter[c].astype(f32) + back_in[slot].astype(f32)).astype(bf16)
        value = gated[c] + carried[c] * dot(c_conv[g], entering)
        gated[c] = value
        power = value * value
        square[...] += power[:, :LANES] + power[:, LANES:]
        return 0

    def locals_before(e):
        count = jnp.where(hop == 0, jnp.where(e < 2 * n, 0, e - n), chunks)
        count = jnp.where(hop == 1, jnp.where(e < n, 0, e), count)
        count = jnp.where(hop == 2, e + 3 * n // 2, count)
        count = jnp.where(e >= events, chunks, count)
        return jnp.clip(jnp.where(e < 0, 0, count), 0, chunks)

    def lasts_after(e):
        count = jnp.where(e < 2 * n - 1, 0, 2 * (e + 1) - 2 * n)
        count = jnp.where(has_chain_out | (locals_before(e) < chunks), 0, count)
        return jnp.where(e >= events, chunks, jnp.minimum(count, chunks))

    def outer(e, _):
        @pl.when(e == jnp.where(hop == 0, 2 * n, jnp.where(hop == 1, n, 0)))
        def _():
            prepare()

        lax.fori_loop(locals_before(e - 1), locals_before(e), local_step, 0)

        @pl.when(e < events)
        def _():
            chain_event(e)

        lax.fori_loop(lasts_after(e - 1), lasts_after(e), last_step, 0)
        return 0

    lax.fori_loop(0, events + 1, outer, 0)

    own_square = jnp.sum(square[...].T, axis=0, keepdims=True)
    square_own[...] = jnp.broadcast_to(own_square, square_own.shape)
    for d in range(1, head_size):
        square_copy(d).start()

    def drain_near(i, _):
        for part in range(NEAR):
            near_copy(i, part).wait_send()
        for part in range(BACK):
            back_copy(i, part).wait_send()
        return 0

    def drain_chain(e, _):
        for part in range(CHAIN):
            chain_copy(e, part).wait_send()
        return 0

    lax.fori_loop(0, 2 * n, drain_near, 0)

    @pl.when(has_chain_out)
    def _():
        lax.fori_loop(0, events, drain_chain, 0)

    d_copy().wait_send()

    @pl.when(has_next)
    def _():
        halo_copy().wait_send()

    for d in range(1, head_size):
        square_copy(d).wait_recv()
    total_square = square_own[...]
    for d in range(1, head_size):
        total_square = total_square + square_in[d - 1]
    inverse = lax.rsqrt(total_square / (xs_ref.shape[1] * head_size) + norm_epsilon)
    inverse = jnp.broadcast_to(inverse[0:1, :], (LANES, rows)).T
    inverse_ref[...] = inverse
    for d in range(1, head_size):
        square_copy(d).wait_send()


def scale_kernel(gated, inverse_ref, gain_ref, out_hbm, out_ref, sem):
    chunks = gated.shape[0]
    inverse = jnp.concatenate([inverse_ref[...]] * (WIDE // LANES), axis=1)
    copies = []
    for c in range(chunks):
        lanes = slice(c * WIDE, (c + 1) * WIDE)
        out_ref[c] = (gated[c] * inverse * gain_ref[:, lanes]).astype(bf16)
        copies.append(pltpu.make_async_copy(out_ref.at[c], out_hbm.at[:, lanes], sem.at[c]))
        copies[-1].start()
    for copy in copies:
        copy.wait()


def solution(mesh):
    seq_size = mesh.shape["seq"]
    head_size = mesh.shape["head"]

    def per_device(
        xs, gate_z, b_in, c_in, dt, log_decay, d_skip, conv_x, conv_b, conv_c, gain, doc_lengths
    ):
        rows, width = xs.shape
        heads = dt.shape[1]
        groups = b_in.shape[1] // STATE
        chunks = width // WIDE
        blocks = rows // BLOCK
        per_chunk = WIDE // HEAD_DIM
        vmem = pltpu.VMEM
        dma = pltpu.SemaphoreType.DMA
        n = chunks // 4

        def states(count):
            return vmem((count, STATE, WIDE), bf16)

        gated, inverse = pl.pallas_call(
            functools.partial(kernel, seq_size, head_size),
            out_shape=(vmem((chunks, rows, WIDE), f32), vmem((rows, LANES), f32)),
            in_specs=[pl.BlockSpec(memory_space=pltpu.HBM)] * 11,
            out_specs=(pl.BlockSpec(memory_space=pltpu.VMEM),) * 2,
            scratch_shapes=[
                pltpu.SMEM(doc_lengths.shape, jnp.int32),
                vmem((rows, width), bf16),
                vmem((rows, width), bf16),
                vmem((rows, groups * STATE), bf16),
                vmem((rows, groups * STATE), bf16),
                vmem((heads, rows), f32),
                vmem((heads, rows), f32),
                vmem((1, heads), f32),
                vmem((4, width), f32),
                vmem((4, groups * STATE), f32),
                vmem((4, groups * STATE), f32),
                vmem((HALO, width), bf16),
                vmem((HALO, width // 4), bf16),
                vmem((HALO, width // 4), bf16),
                vmem((HALO, width), bf16),
                vmem((HALO, groups * STATE), bf16),
                vmem((HALO, groups * STATE), bf16),
                states(chunks),
                states(chunks),
                states(chunks),
                states(2 * n + 1),
                states(3 * n),
                states(3 * n),
                states(2 * n),
                states(2 * n + 1),
                vmem((16, LANES), bf16),
                vmem((16, LANES), bf16),
                vmem((3, rows, LANES), f32),
                vmem((chunks, rows, WIDE), bf16),
                vmem((chunks, rows, WIDE), bf16),
                vmem((groups, rows, STATE), bf16),
                vmem((groups, rows, STATE), bf16),
                vmem((groups, blocks, STATE, BLOCK), bf16),
                vmem((groups, blocks, BLOCK, BLOCK), f32),
                vmem((blocks, chunks, 8, BLOCK), f32),
                vmem((6, rows, LANES), bf16),
                vmem((chunks, LANES, WIDE), bf16),
                vmem((chunks, rows, LANES), f32),
                vmem((chunks, rows, WIDE), f32),
                vmem((rows, LANES), f32),
                vmem((8, rows), f32),
                vmem((head_size - 1, 8, rows), f32),
                dma,
                dma,
                dma,
                dma,
                dma((2 * n, NEAR)),
                dma((2 * n, NEAR)),
                dma((3 * n, CHAIN)),
                dma((3 * n, CHAIN)),
                dma((2 * n, BACK)),
                dma((2 * n, BACK)),
                dma((head_size - 1,)),
                dma((head_size - 1,)),
                dma((12,)),
            ],
            compiler_params=pltpu.CompilerParams(
                collective_id=0, has_side_effects=True, vmem_limit_bytes=60_000_000
            ),
        )(
            doc_lengths,
            xs,
            gate_z,
            b_in,
            c_in,
            dt.T,
            log_decay.T,
            d_skip.reshape(1, -1),
            conv_x,
            conv_b,
            conv_c,
        )
        return pl.pallas_call(
            scale_kernel,
            out_shape=jax.ShapeDtypeStruct((rows, width), bf16),
            in_specs=[pl.BlockSpec(memory_space=pltpu.VMEM)] * 3,
            out_specs=pl.BlockSpec(memory_space=pltpu.HBM),
            scratch_shapes=[vmem((chunks, rows, WIDE), bf16), dma((chunks,))],
            compiler_params=pltpu.CompilerParams(vmem_limit_bytes=16_000_000),
        )(gated, inverse, gain.reshape(1, -1))

    whole = P("seq", "head")
    across = P(None, "head")
    return jax.shard_map(
        per_device,
        mesh=mesh,
        in_specs=(
            whole,
            whole,
            whole,
            whole,
            whole,
            whole,
            P("head"),
            across,
            across,
            across,
            P("head"),
            P(),
        ),
        out_specs=whole,
        check_vma=False,
    )
```

```python
import functools

import jax
import jax.numpy as jnp
from jax import lax
from jax.experimental import pallas as pl
from jax.experimental.pallas import tpu as pltpu
from jax.sharding import PartitionSpec as P

HEAD_DIM = 64
STATE = 128
BLOCK = 128
LANES = 128
WIDE = 256
HALO = 16
SUBS = 2
NEAR = 2
CHAIN = 2
BACK = 2
norm_epsilon = 1e-05

MESH = pl.DeviceIdType.MESH
f32 = jnp.float32
bf16 = jnp.bfloat16


def silu(v):
    return v / (1.0 + jnp.exp(-v))


def split(v):
    high = v.astype(bf16)
    rest = v - high.astype(f32)
    middle = rest.astype(bf16)
    low = (rest - middle.astype(f32)).astype(bf16)
    parts = [high.astype(f32), middle.astype(f32), low.astype(f32)]
    width = LANES - 3 * v.shape[1]
    if width:
        parts.append(jnp.zeros((v.shape[0], width), f32))
    return jnp.concatenate(parts, axis=1).astype(bf16)


def dot(a, b):
    return jnp.dot(a, b, preferred_element_type=f32)


def kernel(
    seq_size,
    head_size,
    lengths_hbm,
    xs_hbm,
    z_hbm,
    b_hbm,
    c_hbm,
    dt_hbm,
    decay_hbm,
    skip_hbm,
    conv_x_hbm,
    conv_b_hbm,
    conv_c_hbm,
    gated,
    inverse_ref,
    lengths_ref,
    xs_ref,
    z_ref,
    b_ref,
    c_ref,
    dt_ref,
    decay_ref,
    skip_ref,
    conv_x_ref,
    conv_b_ref,
    conv_c_ref,
    tail_x,
    halo_out,
    halo_in,
    halo_x,
    halo_b,
    halo_c,
    own_s,
    first_s,
    enter,
    near_in,
    chain_out,
    chain_in,
    back_out,
    back_in,
    d_own,
    d_pair,
    masks,
    x_conv,
    scaled,
    c_conv,
    b_conv,
    b_turned,
    score,
    cum_turned,
    packed,
    hot,
    cum_columns,
    carried,
    square,
    square_own,
    square_in,
    halo_send,
    halo_recv,
    d_send,
    d_recv,
    near_send,
    near_recv,
    chain_send,
    chain_recv,
    back_send,
    back_recv,
    square_send,
    square_recv,
    load_sem,
):
    rows = xs_ref.shape[0]
    heads = dt_ref.shape[0]
    groups = b_ref.shape[1] // STATE
    chunks = xs_ref.shape[1] // WIDE
    per_chunk = WIDE // HEAD_DIM
    blocks = rows // BLOCK
    docs = lengths_ref.shape[0]
    n = chunks // 4
    events = 3 * n
    k = lax.axis_index("seq")
    me = lax.axis_index("head")
    r = lax.rem(k, 2)
    hop = k // 2
    partner = k + 1 - 2 * r
    keep = 2 * n + r * n
    give = 3 * n - r * n
    even = r == 0
    has_prev = k > 0
    has_next = k + 1 < seq_size
    has_chain_in = k > 1
    has_chain_out = k + 2 < seq_size

    def work_chunk(p):
        c = jnp.where(p < 3 * n, p - n, keep + p - 3 * n)
        early = jnp.where(lax.rem(p, 2) == 0, give + p // 2, p // 2)
        return jnp.where(p < 2 * n, early, c)

    def event_chunk(e):
        c = jnp.where(e < 2 * n, keep + e - n, e - n)
        return jnp.where(e < n, e, c)

    def halo_copy():
        return pltpu.make_async_remote_copy(
            src_ref=halo_out,
            dst_ref=halo_in,
            send_sem=halo_send,
            recv_sem=halo_recv,
            device_id={"seq": k + 1},
            device_id_type=MESH,
        )

    def d_copy():
        return pltpu.make_async_remote_copy(
            src_ref=d_own,
            dst_ref=d_pair,
            send_sem=d_send,
            recv_sem=d_recv,
            device_id={"seq": partner},
            device_id_type=MESH,
        )

    def lines_of(part, parts=SUBS):
        return pl.ds(part * (STATE // parts), STATE // parts)

    def near_copy(i, part):
        source = jnp.where(i < n, give + i, i)
        return pltpu.make_async_remote_copy(
            src_ref=own_s.at[source, lines_of(part, NEAR)],
            dst_ref=near_in.at[i, lines_of(part, NEAR)],
            send_sem=near_send.at[i, part],
            recv_sem=near_recv.at[i, part],
            device_id={"seq": partner},
            device_id_type=MESH,
        )

    def chain_copy(e, part):
        return pltpu.make_async_remote_copy(
            src_ref=chain_out.at[e, lines_of(part, CHAIN)],
            dst_ref=chain_in.at[e, lines_of(part, CHAIN)],
            send_sem=chain_send.at[e, part],
            recv_sem=chain_recv.at[e, part],
            device_id={"seq": k + 2},
            device_id_type=MESH,
        )

    def back_copy(e, part):
        return pltpu.make_async_remote_copy(
            src_ref=back_out.at[e, lines_of(part, BACK)],
            dst_ref=back_in.at[e, lines_of(part, BACK)],
            send_sem=back_send.at[e, part],
            recv_sem=back_recv.at[e, part],
            device_id={"seq": partner},
            device_id_type=MESH,
        )

    def square_copy(d):
        return pltpu.make_async_remote_copy(
            src_ref=square_own,
            dst_ref=square_in.at[d - 1],
            send_sem=square_send.at[d - 1],
            recv_sem=square_recv.at[d - 1],
            device_id={"head": lax.rem(me + d, head_size)},
            device_id_type=MESH,
        )

    barrier = pltpu.get_barrier_semaphore()
    for step, there in ((-1, has_prev), (1, has_next), (-2, has_chain_in), (2, has_chain_out)):

        @pl.when(there)
        def _():
            pl.semaphore_signal(
                barrier, inc=1, device_id={"seq": k + step}, device_id_type=MESH
            )

    for d in range(1, head_size):
        pl.semaphore_signal(
            barrier,
            inc=1,
            device_id={"head": lax.rem(me + d, head_size)},
            device_id_type=MESH,
        )
    expected = head_size - 1
    for there in (has_prev, has_next, has_chain_in, has_chain_out):
        expected = expected + there.astype(jnp.int32)

    moves = (
        (xs_hbm.at[pl.ds(rows - HALO, HALO)], tail_x),
        (lengths_hbm, lengths_ref),
        (b_hbm, b_ref),
        (c_hbm, c_ref),
        (decay_hbm, decay_ref),
        (dt_hbm, dt_ref),
        (xs_hbm, xs_ref),
        (conv_b_hbm, conv_b_ref),
        (conv_x_hbm, conv_x_ref),
        (conv_c_hbm, conv_c_ref),
        (skip_hbm, skip_ref),
        (z_hbm, z_ref),
    )
    loads = [
        pltpu.make_async_copy(source, target, load_sem.at[i])
        for i, (source, target) in enumerate(moves)
    ]
    for load in loads:
        load.start()
    (
        load_tail, load_lengths, load_b, load_c, load_decay, load_dt, load_x,
        load_conv_b, load_conv_x, load_conv_c, load_skip, load_z,
    ) = loads

    quarter = xs_ref.shape[1] // 4
    b_width = b_ref.shape[1]
    halo_row = lax.broadcasted_iota(jnp.int32, (HALO, quarter), 0) // 3

    load_tail.wait()
    parcel = jnp.zeros((HALO, quarter), f32)
    for q in range(4):
        piece = tail_x[:, q * quarter : (q + 1) * quarter].astype(f32)
        parcel = jnp.where(halo_row == q, pltpu.roll(piece, 3 * q + 3, 0), parcel)
    load_b.wait()
    load_c.wait()
    pieces = [b_ref[rows - HALO :, :].astype(f32), c_ref[rows - HALO :, :].astype(f32)]
    if quarter > 2 * b_width:
        pieces.append(jnp.zeros((HALO, quarter - 2 * b_width), f32))
    piece = pltpu.roll(jnp.concatenate(pieces, axis=1), 15, 0)
    halo_out[...] = jnp.where(halo_row == 4, piece, parcel).astype(bf16)

    load_lengths.wait()
    starts = []
    running = jnp.int32(0)
    for j in range(docs):
        starts.append(running)
        running = running + lengths_ref[j]

    def start_at(position):
        found = jnp.full_like(position, -1)
        for start in starts:
            found = jnp.where(start <= position, start, found)
        return found

    base = k * rows
    column = base + lax.broadcasted_iota(jnp.int32, (rows, LANES), 0)
    own_start = start_at(column)
    for d in range(1, 4):
        masks[d - 1] = jnp.where(column - own_start >= d, 1.0, 0.0).astype(f32)
    lasts = [start_at(base + (b + 1) * BLOCK - 1) for b in range(blocks)]
    load_decay.wait()
    load_dt.wait()
    load_skip.wait()

    def turn(v):
        wide = jnp.concatenate([v, jnp.zeros((LANES - heads, rows), f32)], axis=0)
        return wide.T[:, :heads]

    dt_rows = turn(dt_ref[...])
    decay_rows = turn(decay_ref[...])
    t_index = lax.broadcasted_iota(jnp.int32, (BLOCK, BLOCK), 0)
    s_index = lax.broadcasted_iota(jnp.int32, (BLOCK, BLOCK), 1)
    lower = jnp.where(s_index <= t_index, 1.0, 0.0).astype(bf16)
    ends, enters, cums = [], [], []
    for b in range(blocks):
        here = slice(b * BLOCK, (b + 1) * BLOCK)
        parts = dot(lower, split(decay_rows[here, :]))
        cum = parts[:, :heads] + parts[:, heads : 2 * heads] + parts[:, 2 * heads : 3 * heads]
        begun = own_start[here, :heads]
        ends.append(jnp.where(begun == lasts[b], jnp.exp(cum[BLOCK - 1 :, :] - cum), 0.0))
        enters.append(jnp.where(begun < base + b * BLOCK, jnp.exp(cum), 0.0))
        cums.append(cum)
    carry0 = enters[0][BLOCK - 1 :, :]
    carry1 = enters[1][BLOCK - 1 :, :]
    d_own[...] = split(jnp.broadcast_to(carry0 * carry1, (16, heads)))
    packed[0] = split(dt_rows)
    packed[1] = split(jnp.concatenate(ends, axis=0))
    few = split(
        jnp.concatenate(
            [jnp.broadcast_to(carry1, (8, heads)), jnp.broadcast_to(skip_ref[...], (8, heads))], 0
        )
    )
    packed[5, 0:16, :] = few

    def spread(c, width):
        row = lax.broadcasted_iota(jnp.int32, (LANES, per_chunk * width), 0)
        lane = lax.broadcasted_iota(jnp.int32, (LANES, per_chunk * width), 1)
        wanted = c * per_chunk + lane // width
        hit = (row == wanted) | (row == wanted + heads) | (row == wanted + 2 * heads)
        return jnp.where(hit, 1.0, 0.0).astype(bf16)

    def convolve(x, weight):
        x = x.astype(f32)
        total = weight[3:4, :] * x
        for d in range(1, 4):
            total = total + weight[3 - d : 4 - d, :] * (pltpu.roll(x, d, 0) * masks[d - 1])
        return silu(total).astype(bf16)

    def convolve_top(x, halo, weight):
        window = jnp.concatenate([halo.astype(f32), x.astype(f32)], axis=0)
        total = weight[3:4, :] * window[HALO:]
        for d in range(1, 4):
            shifted = window[HALO - d : 2 * HALO - d] * masks[d - 1, 0:HALO, :]
            total = total + weight[3 - d : 4 - d, :] * shifted
        return silu(total).astype(bf16)

    load_conv_b.wait()
    for g in range(groups):
        lanes = slice(g * STATE, (g + 1) * STATE)
        b_conv[g] = convolve(b_ref[:, lanes], conv_b_ref[:, lanes])
        b_turned[g, 1] = b_conv[g, BLOCK:, :].astype(f32).T.astype(bf16)

    load_x.wait()
    load_conv_x.wait()
    pl.semaphore_wait(barrier, expected)

    @pl.when(has_next)
    def _():
        halo_copy().start()

    d_copy().start()

    def lanes_of(c, half):
        return pl.ds(pl.multiple_of(c * WIDE + half * LANES, LANES), LANES)

    def conv_step(p, _):
        c = work_chunk(p)
        for half in range(WIDE // LANES):
            lanes = lanes_of(c, half)
            x_conv[c, :, half * LANES : (half + 1) * LANES] = convolve(
                xs_ref[:, lanes], conv_x_ref[:, lanes]
            )
        return 0

    lax.fori_loop(0, chunks, conv_step, 0)

    def hot_step(c, _):
        hot[c] = spread(c, HEAD_DIM)
        return 0

    lax.fori_loop(0, chunks, hot_step, 0)

    @pl.when(k < 2)
    def _():
        chain_in[...] = jnp.zeros_like(chain_in)

    near_in[2 * n] = jnp.zeros_like(near_in[2 * n])
    back_in[2 * n] = jnp.zeros_like(back_in[2 * n])
    for i in range(n):
        enter[give + i] = jnp.zeros_like(enter[give + i])

    @pl.when(k == 0)
    def _():
        halo_in[...] = jnp.zeros_like(halo_in)

    @pl.when(has_prev)
    def _():
        halo_copy().wait_recv()

    arrived = halo_in[...].astype(f32)
    for q in range(4):
        halo_x[:, q * quarter : (q + 1) * quarter] = pltpu.roll(
            arrived, HALO - 3 - 3 * q, 0
        ).astype(bf16)
    piece = pltpu.roll(arrived, 1, 0)
    halo_b[...] = piece[:, :b_width].astype(bf16)
    halo_c[...] = piece[:, b_width : 2 * b_width].astype(bf16)

    for g in range(groups):
        lanes = slice(g * STATE, (g + 1) * STATE)
        b_conv[g, 0:HALO, :] = convolve_top(b_ref[0:HALO, lanes], halo_b[:, lanes], conv_b_ref[:, lanes])
        b_turned[g, 0] = b_conv[g, :BLOCK, :].astype(f32).T.astype(bf16)

    def state_step(p, _):
        c = work_chunk(p)
        g = c // (chunks // groups)
        for half in range(WIDE // LANES):
            lanes = lanes_of(c, half)
            x_conv[c, 0:HALO, half * LANES : (half + 1) * LANES] = convolve_top(
                xs_ref[0:HALO, lanes], halo_x[:, lanes], conv_x_ref[:, lanes]
            )
        x = x_conv[c]
        one_hot = hot[c]
        product = (dot(packed[0], one_hot) * x.astype(f32)).astype(bf16)
        scaled[c] = product
        weighted = (dot(packed[1], one_hot) * product.astype(f32)).astype(bf16)
        state0 = dot(b_turned[g, 0], weighted[:BLOCK])
        state1 = dot(b_turned[g, 1], weighted[BLOCK:])
        few = dot(packed[5, 0:16, :], one_hot)
        first_s[c] = state0.astype(bf16)
        state = (few[0:1, :] * state0 + state1).astype(bf16)
        own_s[c] = state

        @pl.when((p < 3 * n) & ((p >= 2 * n) | (lax.rem(p, 2) == 0)))
        def _():
            for part in range(NEAR):
                near_copy(jnp.where(p < 2 * n, p // 2, p - n), part).start()

        @pl.when(p == 0)
        def _():
            d_copy().wait_recv()

        @pl.when((p < 2 * n) & (lax.rem(p, 2) != 0) & (hop == 0) & has_chain_out)
        def _():
            decay_pair = dot(d_pair[...], one_hot)[0:1, :]
            wide = state.astype(f32)
            chain_out[p // 2] = jnp.where(even, decay_pair * wide, wide).astype(bf16)
            for part in range(CHAIN):
                chain_copy(p // 2, part).start()

        return 0

    lax.fori_loop(0, 2 * n, state_step, 0)
    lax.fori_loop(3 * n, chunks, state_step, 0)
    lax.fori_loop(2 * n, 3 * n, state_step, 0)
    load_conv_c.wait()

    def prepare():
        packed[2] = split(jnp.concatenate([enters[0], enters[1] * carry0], axis=0))
        packed[3] = split(jnp.concatenate([enters[0], enters[1]], axis=0))
        wide = jnp.concatenate(cums, axis=0)
        wide = jnp.concatenate([wide, jnp.zeros((rows, LANES - heads), f32)], axis=1)
        for c in range(chunks):
            shifted = pltpu.roll(wide, LANES - c * per_chunk, 1) if c else wide
            cum_columns[c] = shifted
        for b in range(blocks):
            wide = jnp.concatenate([cums[b], jnp.zeros((BLOCK, LANES - heads), f32)], axis=1)
            turned = wide.T
            for c in range(chunks):
                cum_turned[b, c, 0:per_chunk, :] = turned[c * per_chunk : (c + 1) * per_chunk, :]

        for g in range(groups):
            lanes = slice(g * STATE, (g + 1) * STATE)
            c_conv[g] = convolve(c_ref[:, lanes], conv_c_ref[:, lanes])
            c_conv[g, 0:HALO, :] = convolve_top(c_ref[0:HALO, lanes], halo_c[:, lanes], conv_c_ref[:, lanes])

        for b in range(blocks):
            here = slice(b * BLOCK, (b + 1) * BLOCK)
            allowed = (base + b * BLOCK + s_index >= own_start[here, :]) & (s_index <= t_index)
            for g in range(groups):
                value = lax.dot_general(
                    c_conv[g, here, :],
                    b_conv[g, here, :],
                    (((1,), (1,)), ((), ())),
                    preferred_element_type=f32,
                )
                score[g, b] = jnp.where(allowed, value, 0.0)

    square[...] = jnp.zeros_like(square)
    load_z.wait()

    def local_step(c, _):
        g = c // (chunks // groups)
        one_hot = hot[c]
        lane = lax.broadcasted_iota(jnp.int32, (BLOCK, LANES), 1)
        locals_ = []
        for b in range(blocks):
            here = slice(b * BLOCK, (b + 1) * BLOCK)
            columns = cum_columns[c, here, :]
            damped = score[g, b]
            pieces = []
            for j in range(per_chunk // 2):
                mixes = []
                for i in (2 * j, 2 * j + 1):
                    across = jnp.broadcast_to(columns[:, i : i + 1], (BLOCK, BLOCK))
                    gap = across - cum_turned[b, c, i : i + 1, :]
                    mixes.append((damped * jnp.exp(jnp.minimum(gap, 0.0))).astype(bf16))
                values = scaled[c, here, j * LANES : (j + 1) * LANES]
                zero = jnp.zeros_like(values)
                left = jnp.where(lane < HEAD_DIM, values, zero)
                right = jnp.where(lane < HEAD_DIM, zero, values)
                pieces.append(
                    dot(jnp.concatenate(mixes, axis=1), jnp.concatenate([left, right], axis=0))
                )
            locals_.append(jnp.concatenate(pieces, axis=1))
        inner = dot(packed[3, BLOCK:, :], one_hot) * dot(c_conv[g, BLOCK:, :], first_s[c])
        few = dot(packed[5, 0:16, :], one_hot)
        total = jnp.concatenate([locals_[0], locals_[1] + inner], axis=0)
        lanes = pl.ds(pl.multiple_of(c * WIDE, WIDE), WIDE)
        gate = silu(z_ref[:, lanes].astype(f32))
        gated[c] = (total + few[8:9, :] * x_conv[c].astype(f32)) * gate
        carried[c] = dot(packed[2], one_hot) * gate
        return 0

    def chain_event(e):
        c = event_chunk(e)
        one_hot = hot[c]
        decay_own = dot(d_own[...], one_hot)[0:1, :]
        decay_pair = dot(d_pair[...], one_hot)[0:1, :]
        decay_first = jnp.where(even, decay_own, decay_pair)
        decay_second = jnp.where(even, decay_pair, decay_own)
        near = jnp.where(e < n, 2 * n, e - n)
        for part in range(SUBS):
            lines = lines_of(part)

            if part % (SUBS // NEAR) == 0:

                @pl.when(e >= n)
                def _():
                    near_copy(e - n, part * NEAR // SUBS).wait_recv()

            if part % (SUBS // CHAIN) == 0:

                @pl.when(has_chain_in)
                def _():
                    chain_copy(e, part * CHAIN // SUBS).wait_recv()

            own = own_s[c, lines].astype(f32)
            other = near_in[near, lines].astype(f32)
            before = chain_in[e, lines].astype(f32)
            middle = jnp.where(even, own, other) + decay_first * before
            after = jnp.where(even, other, own) + decay_second * middle

            @pl.when(has_chain_out & ((e >= n) | has_chain_in))
            def _():
                chain_out[e, lines] = after.astype(bf16)
                if (part + 1) % (SUBS // CHAIN) == 0:
                    chain_copy(e, part * CHAIN // SUBS).start()

            @pl.when(e < 2 * n)
            def _():
                back_out[e, lines] = jnp.where(even, middle, before).astype(bf16)

                if (part + 1) % (SUBS // BACK) == 0:

                    @pl.when(has_chain_in)
                    def _():
                        back_copy(e, part * BACK // SUBS).start()

            enter[c, lines] = jnp.where(even, before, middle).astype(bf16)

        @pl.when((e == events - 1) & (hop == 0))
        def _():
            for other_e in range(2 * n):
                for part in range(BACK):
                    back_copy(other_e, part).start()

    def last_step(f, _):
        t = f - 2 * n
        late = jnp.where(lax.rem(t, 2) == 0, n + t // 2, give + t // 2)
        c = jnp.where(f < n, keep + f, jnp.where(f < 2 * n, f - n, late))
        added = (f >= n) & ((f < 2 * n) | (lax.rem(f, 2) == 1))
        slot = jnp.where(f < 2 * n, f - n, n + t // 2)
        slot = jnp.where(added, slot, 2 * n)
        g = c // (chunks // groups)

        @pl.when(added)
        def _():
            for part in range(BACK):
                back_copy(slot, part).wait_recv()

        entering = (enter[c].astype(f32) + back_in[slot].astype(f32)).astype(bf16)
        value = gated[c] + carried[c] * dot(c_conv[g], entering)
        gated[c] = value
        power = value * value
        square[...] += power[:, :LANES] + power[:, LANES:]
        return 0

    def locals_before(e):
        count = jnp.where(hop == 0, jnp.where(e < 2 * n, 0, e - n), chunks)
        count = jnp.where(hop == 1, jnp.where(e < n, 0, e), count)
        count = jnp.where(hop == 2, e + 3 * n // 2, count)
        count = jnp.where(e >= events, chunks, count)
        return jnp.clip(jnp.where(e < 0, 0, count), 0, chunks)

    def lasts_after(e):
        count = jnp.where(e < 2 * n - 1, 0, 2 * (e + 1) - 2 * n)
        count = jnp.where(has_chain_out | (locals_before(e) < chunks), 0, count)
        return jnp.where(e >= events, chunks, jnp.minimum(count, chunks))

    def outer(e, _):
        @pl.when(e == jnp.where(hop == 0, 2 * n, jnp.where(hop == 1, n, 0)))
        def _():
            prepare()

        lax.fori_loop(locals_before(e - 1), locals_before(e), local_step, 0)

        @pl.when(e < events)
        def _():
            chain_event(e)

        lax.fori_loop(lasts_after(e - 1), lasts_after(e), last_step, 0)
        return 0

    lax.fori_loop(0, events + 1, outer, 0)

    own_square = jnp.sum(square[...].T, axis=0, keepdims=True)
    square_own[...] = jnp.broadcast_to(own_square, square_own.shape)
    for d in range(1, head_size):
        square_copy(d).start()

    def drain_near(i, _):
        for part in range(NEAR):
            near_copy(i, part).wait_send()
        for part in range(BACK):
            back_copy(i, part).wait_send()
        return 0

    def drain_chain(e, _):
        for part in range(CHAIN):
            chain_copy(e, part).wait_send()
        return 0

    lax.fori_loop(0, 2 * n, drain_near, 0)

    @pl.when(has_chain_out)
    def _():
        lax.fori_loop(0, events, drain_chain, 0)

    d_copy().wait_send()

    @pl.when(has_next)
    def _():
        halo_copy().wait_send()

    for d in range(1, head_size):
        square_copy(d).wait_recv()
    total_square = square_own[...]
    for d in range(1, head_size):
        total_square = total_square + square_in[d - 1]
    inverse = lax.rsqrt(total_square / (xs_ref.shape[1] * head_size) + norm_epsilon)
    inverse = jnp.broadcast_to(inverse[0:1, :], (LANES, rows)).T
    inverse_ref[...] = inverse
    for d in range(1, head_size):
        square_copy(d).wait_send()


def scale_kernel(gated, inverse_ref, gain_ref, out_hbm, out_ref, sem):
    chunks = gated.shape[0]
    inverse = jnp.concatenate([inverse_ref[...]] * (WIDE // LANES), axis=1)
    copies = []
    for c in range(chunks):
        lanes = slice(c * WIDE, (c + 1) * WIDE)
        out_ref[c] = (gated[c] * inverse * gain_ref[:, lanes]).astype(bf16)
        copies.append(pltpu.make_async_copy(out_ref.at[c], out_hbm.at[:, lanes], sem.at[c]))
        copies[-1].start()
    for copy in copies:
        copy.wait()


def solution(mesh):
    seq_size = mesh.shape["seq"]
    head_size = mesh.shape["head"]

    def per_device(
        xs, gate_z, b_in, c_in, dt, log_decay, d_skip, conv_x, conv_b, conv_c, gain, doc_lengths
    ):
        rows, width = xs.shape
        heads = dt.shape[1]
        groups = b_in.shape[1] // STATE
        chunks = width // WIDE
        blocks = rows // BLOCK
        per_chunk = WIDE // HEAD_DIM
        vmem = pltpu.VMEM
        dma = pltpu.SemaphoreType.DMA
        n = chunks // 4

        def states(count):
            return vmem((count, STATE, WIDE), bf16)

        gated, inverse = pl.pallas_call(
            functools.partial(kernel, seq_size, head_size),
            out_shape=(vmem((chunks, rows, WIDE), f32), vmem((rows, LANES), f32)),
            in_specs=[pl.BlockSpec(memory_space=pltpu.HBM)] * 11,
            out_specs=(pl.BlockSpec(memory_space=pltpu.VMEM),) * 2,
            scratch_shapes=[
                pltpu.SMEM(doc_lengths.shape, jnp.int32),
                vmem((rows, width), bf16),
                vmem((rows, width), bf16),
                vmem((rows, groups * STATE), bf16),
                vmem((rows, groups * STATE), bf16),
                vmem((heads, rows), f32),
                vmem((heads, rows), f32),
                vmem((1, heads), f32),
                vmem((4, width), f32),
                vmem((4, groups * STATE), f32),
                vmem((4, groups * STATE), f32),
                vmem((HALO, width), bf16),
                vmem((HALO, width // 4), bf16),
                vmem((HALO, width // 4), bf16),
                vmem((HALO, width), bf16),
                vmem((HALO, groups * STATE), bf16),
                vmem((HALO, groups * STATE), bf16),
                states(chunks),
                states(chunks),
                states(chunks),
                states(2 * n + 1),
                states(3 * n),
                states(3 * n),
                states(2 * n),
                states(2 * n + 1),
                vmem((16, LANES), bf16),
                vmem((16, LANES), bf16),
                vmem((3, rows, LANES), f32),
                vmem((chunks, rows, WIDE), bf16),
                vmem((chunks, rows, WIDE), bf16),
                vmem((groups, rows, STATE), bf16),
                vmem((groups, rows, STATE), bf16),
                vmem((groups, blocks, STATE, BLOCK), bf16),
                vmem((groups, blocks, BLOCK, BLOCK), f32),
                vmem((blocks, chunks, 8, BLOCK), f32),
                vmem((6, rows, LANES), bf16),
                vmem((chunks, LANES, WIDE), bf16),
                vmem((chunks, rows, LANES), f32),
                vmem((chunks, rows, WIDE), f32),
                vmem((rows, LANES), f32),
                vmem((8, rows), f32),
                vmem((head_size - 1, 8, rows), f32),
                dma,
                dma,
                dma,
                dma,
                dma((2 * n, NEAR)),
                dma((2 * n, NEAR)),
                dma((3 * n, CHAIN)),
                dma((3 * n, CHAIN)),
                dma((2 * n, BACK)),
                dma((2 * n, BACK)),
                dma((head_size - 1,)),
                dma((head_size - 1,)),
                dma((12,)),
            ],
            compiler_params=pltpu.CompilerParams(
                collective_id=0, has_side_effects=True, vmem_limit_bytes=60_000_000
            ),
        )(
            doc_lengths,
            xs,
            gate_z,
            b_in,
            c_in,
            dt.T,
            log_decay.T,
            d_skip.reshape(1, -1),
            conv_x,
            conv_b,
            conv_c,
        )
        return pl.pallas_call(
            scale_kernel,
            out_shape=jax.ShapeDtypeStruct((rows, width), bf16),
            in_specs=[pl.BlockSpec(memory_space=pltpu.VMEM)] * 3,
            out_specs=pl.BlockSpec(memory_space=pltpu.HBM),
            scratch_shapes=[vmem((chunks, rows, WIDE), bf16), dma((chunks,))],
            compiler_params=pltpu.CompilerParams(vmem_limit_bytes=16_000_000),
        )(gated, inverse, gain.reshape(1, -1))

    whole = P("seq", "head")
    across = P(None, "head")
    return jax.shard_map(
        per_device,
        mesh=mesh,
        in_specs=(
            whole,
            whole,
            whole,
            whole,
            whole,
            whole,
            P("head"),
            across,
            across,
            across,
            P("head"),
            P(),
        ),
        out_specs=whole,
        check_vma=False,
    )
```
